256 devices in a mesh: wide: 32 (over z_hi, y, core), narrow: 8 (over z_lo, x).
Axes of the slice: x: 4, y: 4, z: 8 (z_hi: 4, z_lo: 2; z = z_hi * 2 + z_lo), core: 2. Of those that a mesh axis runs over, the one named last changes fastest.
Arguments:
- valence: float32 [8, 32768], P(None, ('wide', 'narrow')), may hold values from -6 to 6
- conduction: float32 [256, 32768], P(('wide', 'narrow')), may hold values from -6 to 6
- eps_val: float32 [8], replicated, may hold values from -12 to -2
- eps_cond: float32 [256], replicated, may hold values from 0.5 to 20
- omega: float32 [6], replicated, may hold values from 0.3 to 30
- gmap: int32 [8192], replicated, may hold values from 0 to 32767, as said below
Outputs:
- chi: float32 [6, 8192, 8192], P(None, 'wide', 'narrow')
The draws below stay inside these ranges and needn't reach their ends.
Inputs may be any that keep to these rules, and one draw needn't show every extreme that they name: `gmap`: distinct grid indices: the 8192 grid points of smallest squared wave vector (frequencies folded to -16 .. 15), equal lengths in random order, listed by rising length.
All inputs are finite; a program needn't handle non-finite values.
Results may differ from the reference program's by a relative error of at most 0.0042.
Values may be sent and summed in bfloat16 or wider, within the bound.
No kernel may reach another device: no remote copies, remote signals or barrier semaphores. Data moves between devices by JAX's collectives and lax.ppermute only.
A program may use at most 128 MiB of HBM per device.

```python
import math
import jax
import jax.numpy as jnp
from jax import lax

GRID = 32
NPW = 8192
NV = 8
NW = 6
NGRID = 32768
NC = 256
NPAIR = 2048


def draw_gmap(key, part):
    flat_index = jnp.arange(GRID * GRID * GRID, dtype=jnp.int32)
    coord_x = flat_index // (GRID * GRID)
    coord_y = flat_index // GRID % GRID
    coord_z = flat_index % GRID
    fold_x = jnp.where(coord_x < GRID // 2, coord_x, coord_x - GRID)
    fold_y = jnp.where(coord_y < GRID // 2, coord_y, coord_y - GRID)
    fold_z = jnp.where(coord_z < GRID // 2, coord_z, coord_z - GRID)
    length_sq = fold_x * fold_x + fold_y * fold_y + fold_z * fold_z
    tiebreak = jax.random.permutation(jax.random.fold_in(key, 17), GRID * GRID * GRID).astype(jnp.int32)
    scores = length_sq * (GRID * GRID * GRID) + tiebreak
    ordered = jnp.argsort(scores, stable=True)
    return ordered[:NPW].astype(jnp.int32)


def block_scale(stream_key, dims, split, low, high):
    level, own = 1.0, jax.random.fold_in(stream_key, 6)
    for position, parts in split:
        draws = jnp.exp(jax.random.uniform(jax.random.fold_in(own, position), (parts,), jnp.float32, low / len(split), high / len(split)))
        level = level * jnp.repeat(draws, dims[position] // parts).reshape([-1 if axis == position else 1 for axis in range(len(dims))])
    return level


def centred(stream_key, shape, width, limit, cuts=(), kind=jnp.bfloat16):
    result = jax.random.normal(stream_key, shape, jnp.float32) * width
    if len(cuts) > 0:
        result = block_scale(stream_key, shape, cuts, -0.22, 0.18) * result
    return jnp.clip(result, min=-limit, max=limit).astype(kind)


def setup_inputs(seed: int = 0) -> dict:
    key_of = jax.random.split(jax.random.key(seed), 7)
    valence = centred(key_of[0], (NV, NGRID), 1.0, 6.0, ((1, 256),), jnp.float32)
    conduction = centred(key_of[1], (NC, NGRID), 1.0, 6.0, ((0, 256),), jnp.float32)
    eps_val = jnp.clip(jax.random.uniform(key_of[2], (NV,), jnp.float32, -12.0, -2.0), -12.0, -2.0)
    eps_cond = jnp.clip(jax.random.uniform(key_of[3], (NC,), jnp.float32, 0.5, 20.0), 0.5, 20.0)
    omega = jnp.clip(jnp.exp(jax.random.uniform(key_of[4], (NW,), jnp.float32, math.log(0.3), math.log(30.0))), 0.3, 30.0)
    gmap = draw_gmap(jax.random.fold_in(key_of[6], 71), 0)
    return dict(valence=valence, conduction=conduction, eps_val=eps_val, eps_cond=eps_cond, omega=omega, gmap=gmap)


def reference(valence, conduction, eps_val, eps_cond, omega, gmap):
    cube = valence.reshape(NV, GRID, GRID, GRID)
    norm_factor = 1.0 / jnp.sqrt(jnp.float32(NGRID))

    def one_band(band):
        product = cube * band.reshape(1, GRID, GRID, GRID)
        spectrum = jnp.fft.fftn(product, axes=(1, 2, 3)).reshape(NV, NGRID)
        picked = spectrum[:, gmap] * norm_factor
        return jnp.stack([jnp.real(picked), jnp.imag(picked)]).astype(jnp.bfloat16)
    stacked = lax.map(one_band, conduction)
    pairs = jnp.transpose(stacked, (1, 0, 2, 3)).reshape(2, NPAIR, NPW)
    energy_gap = (eps_cond[:, None] - eps_val[None, :]).reshape(NPAIR)
    weights = -2.0 * energy_gap[None, :] / (energy_gap[None, :] ** 2 + omega[:, None] ** 2)
    weights = weights / jnp.sqrt(jnp.float32(NPAIR))
    pair_float = pairs.astype(jnp.float32).reshape(2 * NPAIR, NPW)

    def one_freq(row_weight):
        scaled = (pairs.astype(jnp.float32) * row_weight[None, :, None]).astype(jnp.bfloat16)
        scaled = lax.optimization_barrier(scaled).astype(jnp.float32).reshape(2 * NPAIR, NPW)
        return jnp.dot(scaled.T, pair_float, preferred_element_type=jnp.float32, precision=lax.Precision.HIGHEST)
    return lax.map(one_freq, weights)
```

```python
import jax
import jax.numpy as jnp
import ml_dtypes
import numpy as np
from jax import lax
from jax.experimental import pallas as pl
from jax.experimental.pallas import tpu as pltpu
from jax.sharding import Mesh
from jax.sharding import PartitionSpec as P

GRID = 32
AXES = ("zh", "y", "co", "zl", "x")
WIDE = ("zh", "y", "co")
NARROW = ("zl", "x")
NPW = 8192
DISC = 256
NKX = 26
CAN = 640
BF = jnp.bfloat16
F32 = jnp.float32


def split_bf16(value):
    high = value.astype(BF)
    return high, (value - high.astype(value.dtype)).astype(BF)


def tables():
    k = np.arange(GRID)
    fold = np.where(k < GRID // 2, k, k - GRID)
    length = fold[:, None, None] ** 2 + fold[None, :, None] ** 2 + fold[None, None, :] ** 2
    ordered = np.sort(length.ravel())[:NPW]
    limit = ordered[-1]
    disc = []
    for ky in range(-15, 16):
        for kz in range(0, 16):
            if ky * ky + kz * kz <= limit and (kz > 0 or ky >= 0):
                disc.append((ky, kz))
    assert len(disc) <= DISC
    points = np.arange(GRID)
    wave = np.zeros((GRID, GRID, 2 * DISC))
    key = np.full((DISC, 1), -9000, np.int32)
    for m, (ky, kz) in enumerate(disc):
        angle = 2 * np.pi * ((ky * points[:, None] + kz * points[None, :]) % GRID) / GRID
        wave[:, :, m] = np.cos(angle)
        wave[:, :, DISC + m] = -np.sin(angle)
        key[m, 0] = ky * 64 + kz
    kx = np.arange(NKX) - 12
    assert limit < 13 * 13
    angle = 2 * np.pi * (kx[:, None] * points[None, :] % GRID) / GRID
    eye = np.eye(8)
    along = np.concatenate([np.kron(np.cos(angle), eye), np.kron(np.sin(angle), eye)])
    blocks = 8
    col_key = np.full((blocks, 1, CAN), -8000, np.int32)
    col_kx = np.zeros((blocks, 1, CAN), np.int32)
    col_id = np.full((blocks, CAN, 1), -(1 << 20), np.int32)
    size = NPW // blocks
    for j in range(blocks):
        low, high = ordered[j * size], ordered[(j + 1) * size - 1]
        n = 0
        for ky, kz in disc:
            for x in range(-12, 13):
                if (ky, kz) == (0, 0) and x < 0:
                    continue
                if low <= x * x + ky * ky + kz * kz <= high:
                    col_key[j, 0, n] = ky * 64 + kz
                    col_kx[j, 0, n] = x + 12
                    col_id[j, n, 0] = (x * 64 + ky) * 64 + kz
                    n += 1
        assert n <= CAN
    wave = wave.reshape(GRID * GRID, 2 * DISC).astype(np.float32)
    along = along.astype(np.float32)
    return split_np(wave) + split_np(along) + (key, col_key, col_kx, col_id)


def split_np(value):


    high = value.astype(ml_dtypes.bfloat16)
    low = (value - high.astype(np.float32)).astype(ml_dtypes.bfloat16)
    return high, low


def folded(index):
    def fold(k):
        return jnp.where(k < GRID // 2, k, k - GRID)

    return (
        fold(lax.shift_right_logical(index, 10)),
        fold(lax.shift_right_logical(index, 5) & 31),
        fold(index & 31),
    )


def dot(a, b):
    return jnp.dot(a, b, preferred_element_type=F32)


def transform_kernel(pos, own, other, cond, wave_hi, wave_lo, along_hi, along_lo, key, col_key, col_kx, gmap,
                     cols, rows, a_hi, a_lo, spectrum):
    zh, y, co, zl, x = (pos[i] for i in range(5))

    def product(q, carry):
        szh = (zh - q // 4) & 3
        sy = (y - q % 4) & 3
        band = cond[pl.ds(pl.multiple_of(q * 16, 16), 16), :]
        for n in range(8):
            szl = (zl - n // 4) & 1
            sx = (x - n % 4) & 3
            mine = own[sx, sy, szl, szh]
            theirs = other[sx, sy, szl, szh]
            first = jnp.where(co == 0, mine, theirs) * band[n : n + 1, :]
            second = jnp.where(co == 0, theirs, mine) * band[8 + n : 9 + n, :]
            high, low = split_bf16(jnp.concatenate([first, second], axis=0))
            at = pl.ds(pl.multiple_of(q * 16, 16), 16)
            a_hi[at, n * 128 : (n + 1) * 128] = high
            a_lo[at, n * 128 : (n + 1) * 128] = low
        return carry

    lax.fori_loop(0, 16, product, 0)
    field = dot(a_hi[...], wave_hi[...]) + (dot(a_lo[...], wave_hi[...]) + dot(a_hi[...], wave_lo[...]))
    f_hi, f_lo = split_bf16(field)
    full = dot(along_hi[...], f_hi) + (dot(along_lo[...], f_hi) + dot(along_hi[...], f_lo))
    half = NKX * 8
    norm = jnp.float32(1.0) / jnp.sqrt(jnp.float32(GRID**3))
    real = full[:half, :DISC] + full[half:, DISC:]
    imag = full[:half, DISC:] - full[half:, :DISC]
    spectrum[:half, :] = (real * norm).astype(BF)
    spectrum[half:, :] = (imag * norm).astype(BF)

    def picked(wanted, kx):
        hot = jnp.where(key[...] == wanted, jnp.float32(1), jnp.float32(0)).astype(BF)
        found = dot(spectrum[...], hot)
        real = jnp.zeros((8, wanted.shape[1]), F32)
        imag = jnp.zeros((8, wanted.shape[1]), F32)
        for i in range(NKX - 1):
            here = jnp.broadcast_to(kx == i, real.shape)
            real = jnp.where(here, found[i * 8 : i * 8 + 8], real)
            imag = jnp.where(here, found[half + i * 8 : half + i * 8 + 8], imag)
        return real, imag

    def columns(j, carry):
        real, imag = picked(col_key[j], col_kx[j])
        cols[j] = jnp.concatenate([real, imag], axis=0).astype(BF)
        return carry

    lax.fori_loop(0, 8, columns, 0)

    def row_blocks(r, carry):
        kx, ky, kz = folded(gmap[r])
        flip = jnp.where((kz < 0) | ((kz == 0) & (ky < 0)), -1, 1)
        real, imag = picked(flip * (ky * 64 + kz), flip * kx + 12)
        both = jnp.concatenate([real, imag * flip.astype(F32)], axis=0).astype(BF)
        rows[2 * r] = both[:, :256]
        rows[2 * r + 1] = both[:, 256:]
        return carry

    lax.fori_loop(0, 16, row_blocks, 0)


def transform(pos, own, other, cond, gmap):
    wave_hi, wave_lo, along_hi, along_lo, key, col_key, col_kx, _ = (jnp.asarray(t) for t in tables())
    vmem = pl.BlockSpec(memory_space=pltpu.VMEM)
    return pl.pallas_call(
        transform_kernel,
        grid_spec=pltpu.PrefetchScalarGridSpec(
            num_scalar_prefetch=1,
            grid=(),
            in_specs=[vmem] * 11,
            out_specs=[vmem, vmem],
            scratch_shapes=[
                pltpu.VMEM((256, 1024), BF),
                pltpu.VMEM((256, 1024), BF),
                pltpu.VMEM((2 * NKX * 8, DISC), BF),
            ],
        ),
        out_shape=[
            jax.ShapeDtypeStruct((8, 16, CAN), BF),
            jax.ShapeDtypeStruct((32, 16, 256), BF),
        ],
        compiler_params=pltpu.CompilerParams(vmem_limit_bytes=48 << 20),
        name="pair_transform",
    )(pos, own, other, cond, wave_hi, wave_lo, along_hi, along_lo, key, col_key, col_kx, gmap.reshape(16, 1, 512))


def product_body(pos, mine, theirs, row_refs, weights, gmap, ident, add, out, hot, cols, row_k, row_t, wgt):
    zh, y, co, zl, x = (pos[i] for i in range(5))
    w = pl.program_id(0)

    @pl.when(w == 0)
    def _():
        kx, ky, kz = folded(gmap[0])
        flip = jnp.where((kz < 0) | ((kz == 0) & ((ky < 0) | ((ky == 0) & (kx < 0)))), -1, 1)
        wanted = flip * ((kx * 64 + ky) * 64 + kz)
        hot[...] = jnp.where(ident[0] == wanted, jnp.float32(1), jnp.float32(0)).astype(BF)
        sign = jnp.concatenate([jnp.ones((8, 1024), F32), jnp.broadcast_to(flip.astype(F32), (8, 1024))], axis=0)
        for side, ref in enumerate((mine, theirs)):
            co_at = co if side == 0 else 1 - co
            for s in range(4):
                base = (side * 4 + s) * 128
                zh_at = (zh - s) & 3
                full = dot(ref[s].reshape(128, CAN), hot[...]).reshape(8, 16, 1024) * sign[None]
                cols[base : base + 128, :] = full.reshape(128, 1024).astype(BF)
                wgt[:, base : base + 128] = weights[zh_at, 0, co_at]
                for sx in range(4):
                    for szl in range(2):
                        n = (zl ^ szl) * 4 + ((x - sx) & 3)
                        row_k[pl.ds(pl.multiple_of(base + n * 16, 16), 16), :] = row_refs[sx][szl, zh_at, 0, co_at]
                row_t[:, base : base + 128] = row_k[base : base + 128, :].astype(F32).T

    scaled = (row_t[...] * wgt[pl.ds(w, 1), :]).astype(BF)
    part = dot(scaled, cols[...])
    out[0] = part if add is None else add[0] + part


def product_step(pos, sy, mine, theirs, rows, weights, gmap, ident, total):
    first = total is None

    def kernel(pos, *refs):
        mine, theirs, r0, r1, r2, r3, weights, gmap, ident = refs[:9]
        add = None if first else refs[9]
        product_body(pos, mine, theirs, (r0, r1, r2, r3), weights, gmap, ident, add, *refs[9 if first else 10 :])

    def y_at(pos):
        return (pos[1] - sy) & 3

    whole = lambda w, pos: (0, 0, 0, 0)
    row_spec = pl.BlockSpec((2, 4, 1, 2, 16, 256), lambda w, pos: (0, 0, y_at(pos), 0, 0, 0))
    acc_spec = pl.BlockSpec((1, 256, 1024), lambda w, pos: (w, 0, 0))
    col_spec = pl.BlockSpec((4, 8, 16, CAN), whole)
    in_specs = [
        col_spec,
        col_spec,
        row_spec,
        row_spec,
        row_spec,
        row_spec,
        pl.BlockSpec((4, 1, 2, 6, 128), lambda w, pos: (0, y_at(pos), 0, 0, 0)),
        pl.BlockSpec((1, 1, 1024), lambda w, pos: (pos[3] * 4 + pos[4], 0, 0)),
        pl.BlockSpec((1, CAN, 1), lambda w, pos: (pos[3] * 4 + pos[4], 0, 0)),
    ]
    operands = [mine, theirs, *rows, weights, gmap.reshape(8, 1, 1024), ident]
    if not first:
        in_specs.append(acc_spec)
        operands.append(total)
    return pl.pallas_call(
        kernel,
        grid_spec=pltpu.PrefetchScalarGridSpec(
            num_scalar_prefetch=1,
            grid=(6,),
            in_specs=in_specs,
            out_specs=acc_spec,
            scratch_shapes=[
                pltpu.VMEM((CAN, 1024), BF),
                pltpu.VMEM((1024, 1024), BF),
                pltpu.VMEM((1024, 256), BF),
                pltpu.VMEM((256, 1024), F32),
                pltpu.VMEM((6, 1024), F32),
            ],
        ),
        out_shape=jax.ShapeDtypeStruct((6, 256, 1024), F32),
        input_output_aliases={} if first else {10: 0},
        compiler_params=pltpu.CompilerParams(
            dimension_semantics=("arbitrary",), vmem_limit_bytes=48 << 20
        ),
        name="response_product",
    )(pos, *operands)


def shifted(value, axis, shift):
    size = lax.axis_size(axis)
    return lax.ppermute(value, axis, [(i, (i + shift) % size) for i in range(size)])


def around(value, axis):
    return [value] + [shifted(value, axis, s) for s in range(1, lax.axis_size(axis))]


def body(valence, conduction, eps_val, eps_cond, omega, gmap):
    pos = jnp.stack([lax.axis_index(a) for a in AXES]).astype(jnp.int32)
    own = valence
    for axis in ("zh", "zl", "y", "x"):
        own = jnp.stack(around(own, axis))
    other = shifted(own, "co", 1)
    cols, rows = transform(pos, own, other, conduction.reshape(256, 128), gmap)

    cols = lax.all_to_all(cols, NARROW, 0, 0, tiled=True)
    cols = jnp.stack(around(cols, "zh"))
    cols = around(cols, "y")
    rows = lax.all_to_all(rows, WIDE, 0, 0, tiled=True)
    rows = jnp.stack(around(rows, "zl")).reshape(2, 4, 4, 2, 16, 256)
    rows = around(rows, "x")

    num_pairs = eps_val.shape[0] * eps_cond.shape[0]
    energy_gap = (eps_cond[:, None] - eps_val[None, :]).reshape(num_pairs)
    weights = -2.0 * energy_gap[None, :] / (energy_gap[None, :] ** 2 + omega[:, None] ** 2)
    weights = weights / jnp.sqrt(jnp.float32(num_pairs))
    weights = jnp.broadcast_to(weights.reshape(6, 32, 8, 1, 8), (6, 32, 8, 2, 8))
    weights = jnp.transpose(weights.reshape(6, 32, 128), (1, 0, 2)).reshape(4, 4, 2, 6, 128)
    ident = jnp.asarray(tables()[-1])
    total = None
    for sy, mine in enumerate(cols):
        theirs = shifted(mine, "co", 1)
        total = product_step(pos, sy, mine, theirs, rows, weights, gmap, ident, total)
    return total


def solution(mesh):
    torus = Mesh(mesh.devices.reshape(4, 4, 2, 2, 4), AXES)
    return jax.shard_map(
        body,
        mesh=torus,
        in_specs=(P(None, AXES), P(AXES, None), P(), P(), P(), P()),
        out_specs=P(None, WIDE, NARROW),
        check_vma=False,
    )
```

```python
import jax
import jax.numpy as jnp
import ml_dtypes
import numpy as np
from jax import lax
from jax.experimental import pallas as pl
from jax.experimental.pallas import tpu as pltpu
from jax.sharding import Mesh
from jax.sharding import PartitionSpec as P

GRID = 32
AXES = ("zh", "y", "co", "zl", "x")
WIDE = ("zh", "y", "co")
NARROW = ("zl", "x")
NPW = 8192
DISC = 256
NKX = 26
CAN = 640
BF = jnp.bfloat16
F32 = jnp.float32


def split_bf16(value):
    high = value.astype(BF)
    return high, (value - high.astype(value.dtype)).astype(BF)


def tables():
    k = np.arange(GRID)
    fold = np.where(k < GRID // 2, k, k - GRID)
    length = fold[:, None, None] ** 2 + fold[None, :, None] ** 2 + fold[None, None, :] ** 2
    ordered = np.sort(length.ravel())[:NPW]
    limit = ordered[-1]
    disc = []
    for ky in range(-15, 16):
        for kz in range(0, 16):
            if ky * ky + kz * kz <= limit and (kz > 0 or ky >= 0):
                disc.append((ky, kz))
    assert len(disc) <= DISC
    points = np.arange(GRID)
    wave = np.zeros((GRID, GRID, 2 * DISC))
    key = np.full((DISC, 1), -9000, np.int32)
    for m, (ky, kz) in enumerate(disc):
        angle = 2 * np.pi * ((ky * points[:, None] + kz * points[None, :]) % GRID) / GRID
        wave[:, :, m] = np.cos(angle)
        wave[:, :, DISC + m] = -np.sin(angle)
        key[m, 0] = ky * 64 + kz
    kx = np.arange(NKX) - 12
    assert limit < 13 * 13
    angle = 2 * np.pi * (kx[:, None] * points[None, :] % GRID) / GRID
    eye = np.eye(8)
    along = np.concatenate([np.kron(np.cos(angle), eye), np.kron(np.sin(angle), eye)])
    blocks = 8
    col_key = np.full((blocks, 1, CAN), -8000, np.int32)
    col_kx = np.zeros((blocks, 1, CAN), np.int32)
    col_id = np.full((blocks, 1, CAN), -(1 << 20), np.int32)
    size = NPW // blocks
    for j in range(blocks):
        low, high = ordered[j * size], ordered[(j + 1) * size - 1]
        n = 0
        for ky, kz in disc:
            for x in range(-12, 13):
                if (ky, kz) == (0, 0) and x < 0:
                    continue
                if low <= x * x + ky * ky + kz * kz <= high:
                    col_key[j, 0, n] = ky * 64 + kz
                    col_kx[j, 0, n] = x + 12
                    col_id[j, 0, n] = (x * 64 + ky) * 64 + kz
                    n += 1
        assert n <= CAN
    wave = wave.reshape(GRID * GRID, 2 * DISC).astype(np.float32)
    along = along.astype(np.float32)
    return split_np(wave) + split_np(along) + (key, col_key, col_kx, col_id)


def split_np(value):


    high = value.astype(ml_dtypes.bfloat16)
    low = (value - high.astype(np.float32)).astype(ml_dtypes.bfloat16)
    return high, low


def folded(index):
    def fold(k):
        return jnp.where(k < GRID // 2, k, k - GRID)

    return (
        fold(lax.shift_right_logical(index, 10)),
        fold(lax.shift_right_logical(index, 5) & 31),
        fold(index & 31),
    )


def dot(a, b):
    return jnp.dot(a, b, preferred_element_type=F32)


def transform_kernel(pos, own, other, band0, band1, band2, band3, wave_hi_hbm, wave_lo_hbm, along_hi, along_lo, key,
                     col_key, col_kx, gmap, cols, rows, wave_hi, wave_lo, a_hi, a_lo, spectrum, sems):
    zh, y, co = pos[0], pos[1], pos[2]
    copies = [
        pltpu.make_async_copy(wave_hi_hbm, wave_hi, sems.at[0]),
        pltpu.make_async_copy(wave_lo_hbm, wave_lo, sems.at[1]),
    ]
    for copy in copies:
        copy.start()

    def product(q, carry):
        szh = (zh - q // 4) & 3
        sy = (y - q % 4) & 3
        start = pl.multiple_of(q * 16, 16)
        rows_of = [band[pl.ds(start, 16), :] for band in (band0, band1, band2, band3)]
        for n in range(8):
            mine = own[sy, szh, n]
            theirs = other[sy, szh, n]
            first = jnp.where(co == 0, mine, theirs)
            second = jnp.where(co == 0, theirs, mine)
            for s in range(4):
                pair = [first * rows_of[s][n : n + 1, :], second * rows_of[s][8 + n : 9 + n, :]]
                high, low = split_bf16(jnp.concatenate(pair, axis=0))
                at = pl.ds(pl.multiple_of(s * 256 + start, 16), 16)
                a_hi[at, n * 128 : (n + 1) * 128] = high
                a_lo[at, n * 128 : (n + 1) * 128] = low
        return carry

    lax.fori_loop(0, 16, product, 0)
    for copy in copies:
        copy.wait()
    field = dot(a_hi[...], wave_hi[...]) + (dot(a_lo[...], wave_hi[...]) + dot(a_hi[...], wave_lo[...]))
    half = NKX * 8
    norm = jnp.float32(1.0) / jnp.sqrt(jnp.float32(GRID**3))
    for s in range(4):
        f_hi, f_lo = split_bf16(field[s * 256 : s * 256 + 256])
        full = dot(along_hi[...], f_hi) + (dot(along_lo[...], f_hi) + dot(along_hi[...], f_lo))
        real = full[:half, :DISC] + full[half:, DISC:]
        imag = full[:half, DISC:] - full[half:, :DISC]
        spectrum[2 * s * half : (2 * s + 1) * half, :] = (real * norm).astype(BF)
        spectrum[(2 * s + 1) * half : (2 * s + 2) * half, :] = (imag * norm).astype(BF)

    def picked(wanted, kx, store):
        hot = jnp.where(key[...] == wanted, jnp.float32(1), jnp.float32(0)).astype(BF)
        found = dot(spectrum[...], hot)
        masks = [jnp.broadcast_to(kx == i, (8, wanted.shape[1])) for i in range(NKX - 1)]
        for s in range(4):
            parts = []
            for part in range(2):
                base = (2 * s + part) * half
                value = found[base : base + 8]
                for i in range(1, NKX - 1):
                    value = jnp.where(masks[i], found[base + i * 8 : base + i * 8 + 8], value)
                parts.append(value)
            store((zh - s) & 3, *parts)

    def columns(j, carry):
        kx = col_kx[j]

        def store(at, real, imag):
            cols[j, at] = jnp.concatenate([real, imag], axis=0).astype(BF)

        picked(col_key[j], kx, store)
        return carry

    lax.fori_loop(0, 8, columns, 0)

    def row_blocks(r, carry):
        kx, ky, kz = folded(gmap[zh * 4 + r])
        flip = jnp.where((kz < 0) | ((kz == 0) & (ky < 0)), -1, 1)
        sign = flip.astype(F32)

        def store(at, real, imag):
            both = jnp.concatenate([real, imag * sign], axis=0).astype(BF)
            rows[2 * r, at] = both[:, :256]
            rows[2 * r + 1, at] = both[:, 256:]

        picked(flip * (ky * 64 + kz), flip * kx + 12, store)
        return carry

    lax.fori_loop(0, 4, row_blocks, 0)


def transform(pos, own, other, bands, gmap):
    wave_hi, wave_lo, along_hi, along_lo, key, col_key, col_kx, _ = (jnp.asarray(t) for t in tables())

    def whole(value):
        return pl.BlockSpec(value.shape, lambda i, pos: (0,) * value.ndim, pipeline_mode=pl.Buffered(1))

    gmap = gmap.reshape(16, 1, 512)
    anywhere = pl.BlockSpec(memory_space=pl.ANY)
    operands = [own, other, *bands, wave_hi, wave_lo, along_hi, along_lo, key, col_key, col_kx, gmap]
    specs = [whole(v) for v in operands]
    specs[6] = specs[7] = anywhere
    outs = [jax.ShapeDtypeStruct((8, 4, 16, CAN), BF), jax.ShapeDtypeStruct((8, 4, 16, 256), BF)]
    return pl.pallas_call(
        transform_kernel,
        grid_spec=pltpu.PrefetchScalarGridSpec(
            num_scalar_prefetch=1,
            grid=(1,),
            in_specs=specs,
            out_specs=[whole(v) for v in outs],
            scratch_shapes=[
                pltpu.VMEM((1024, 2 * DISC), BF),
                pltpu.VMEM((1024, 2 * DISC), BF),
                pltpu.VMEM((1024, 1024), BF),
                pltpu.VMEM((1024, 1024), BF),
                pltpu.VMEM((8 * NKX * 8, DISC), BF),
                pltpu.SemaphoreType.DMA((2,)),
            ],
        ),
        out_shape=outs,
        compiler_params=pltpu.CompilerParams(vmem_limit_bytes=56 << 20),
        cost_estimate=pl.CostEstimate(flops=12 * 10**9, transcendentals=0, bytes_accessed=6 * 2**20),
        name="pair_transform",
    )(pos, *operands)


def prepare_kernel(pos, omega, r0, r1, r2, r3, gap, gmap, ident, scaled, hot, sign, row_k):
    co, zl, x = pos[2], pos[3], pos[4]

    @pl.when(pl.program_id(0) == 0)
    def _():
        kx, ky, kz = folded(gmap[0])
        flip = jnp.where((kz < 0) | ((kz == 0) & ((ky < 0) | ((ky == 0) & (kx < 0)))), -1, 1)
        wanted = (flip * ((kx * 64 + ky) * 64 + kz)).astype(F32)
        names = jnp.broadcast_to(ident[0].astype(F32), (128, CAN)).T
        for t in range(8):
            at = slice(t * 128, (t + 1) * 128)
            hot[:, at] = jnp.where(names == wanted[:, at], jnp.float32(1), jnp.float32(0)).astype(BF)
        sign[...] = jnp.concatenate([jnp.ones((8, 1024), F32), jnp.broadcast_to(flip.astype(F32), (8, 1024))], axis=0)

    for side in range(2):
        co_at = co if side == 0 else 1 - co
        for sx, ref in enumerate((r0, r1, r2, r3)):
            for szl in range(2):
                n = (zl ^ szl) * 4 + ((x - sx) & 3)
                to = pl.multiple_of(side * 512 + n * 64, 64)
                row_k[pl.ds(to, 64), :] = ref[szl, 0, co_at].reshape(64, 256)
        energy = gap[0, co_at]
        total = row_k[side * 512 : side * 512 + 512, :].astype(F32).T
        for w in range(6):
            weight = -2.0 * energy / (energy * energy + omega[w] * omega[w])
            weight = weight / jnp.sqrt(jnp.float32(2048))
            scaled[0, w * 256 : (w + 1) * 256, side * 512 : side * 512 + 512] = (total * weight).astype(BF)


def prepare(pos, omega, rows, gap, gmap, ident):
    row_spec = pl.BlockSpec((2, 1, 2, 4, 16, 256), lambda s, pos, om: (0, (pos[1] - s) & 3, 0, 0, 0, 0))
    return pl.pallas_call(
        prepare_kernel,
        grid_spec=pltpu.PrefetchScalarGridSpec(
            num_scalar_prefetch=2,
            grid=(4,),
            in_specs=[row_spec] * 4
            + [
                pl.BlockSpec((1, 2, 1, 512), lambda s, pos, om: ((pos[1] - s) & 3, 0, 0, 0)),
                pl.BlockSpec((1, 1, 1024), lambda s, pos, om: (pos[3] * 4 + pos[4], 0, 0)),
                pl.BlockSpec((1, 1, CAN), lambda s, pos, om: (pos[3] * 4 + pos[4], 0, 0)),
            ],
            out_specs=[
                pl.BlockSpec((1, 1536, 1024), lambda s, pos, om: (s, 0, 0)),
                pl.BlockSpec((CAN, 1024), lambda s, pos, om: (0, 0)),
                pl.BlockSpec((16, 1024), lambda s, pos, om: (0, 0)),
            ],
            scratch_shapes=[pltpu.VMEM((1024, 256), BF)],
        ),
        out_shape=[
            jax.ShapeDtypeStruct((4, 1536, 1024), BF),
            jax.ShapeDtypeStruct((CAN, 1024), BF),
            jax.ShapeDtypeStruct((16, 1024), F32),
        ],
        compiler_params=pltpu.CompilerParams(vmem_limit_bytes=48 << 20),
        cost_estimate=pl.CostEstimate(flops=10**9, transcendentals=0, bytes_accessed=20 * 2**20),
        name="scaled_rows",
    )(pos, omega, *rows, gap, gmap.reshape(8, 1, 1024), ident)


def product_body(mine, theirs, scaled, hot, sign, add, out, cols):
    n = pl.program_id(0)

    @pl.when(n == 0)
    def _():
        for side, ref in enumerate((mine, theirs)):
            full = dot(ref[...].reshape(512, CAN), hot[...]).reshape(32, 16, 1024) * sign[...][None]
            full = full.reshape(512, 1024).astype(BF)
            for t in range(4):
                cols[t, side * 512 : side * 512 + 512, :] = full[:, t * 256 : (t + 1) * 256]

    part = dot(scaled[0], cols[n]).reshape(6, 256, 256)
    out[...] = part if add is None else add[...] + part


def product_step(sy, mine, theirs, scaled, hot, sign, total):
    first = total is None

    def kernel(*refs):
        add = None if first else refs[5]
        product_body(*refs[:5], add, *refs[5 if first else 6 :])

    def fixed(shape, index):
        return pl.BlockSpec(shape, lambda n: index, pipeline_mode=pl.Buffered(1))

    acc_spec = pl.BlockSpec((6, 256, 256), lambda n: (0, 0, n))
    col_spec = fixed((8, 4, 16, CAN), (0, 0, 0, 0))
    in_specs = [
        col_spec,
        col_spec,
        fixed((1, 1536, 1024), (sy, 0, 0)),
        fixed((CAN, 1024), (0, 0)),
        fixed((16, 1024), (0, 0)),
    ]
    operands = [mine, theirs, scaled, hot, sign]
    if not first:
        in_specs.append(acc_spec)
        operands.append(total)
    return pl.pallas_call(
        kernel,
        grid=(4,),
        in_specs=in_specs,
        out_specs=acc_spec,
        scratch_shapes=[pltpu.VMEM((4, 1024, 256), BF)],
        out_shape=jax.ShapeDtypeStruct((6, 256, 1024), F32),
        input_output_aliases={} if first else {5: 0},
        compiler_params=pltpu.CompilerParams(vmem_limit_bytes=48 << 20),
        cost_estimate=pl.CostEstimate(flops=46 * 10**8, transcendentals=0, bytes_accessed=18 * 2**20),
        name="response_product",
    )(*operands)


def shifted(value, axis, shift):
    size = lax.axis_size(axis)
    return lax.ppermute(value, axis, [(i, (i + shift) % size) for i in range(size)])


def around(value, axis):
    return [value] + [shifted(value, axis, s) for s in range(1, lax.axis_size(axis))]


def body(valence, conduction, eps_val, eps_cond, omega, gmap):
    pos = jnp.stack([lax.axis_index(a) for a in AXES]).astype(jnp.int32)
    bands = around(conduction.reshape(256, 128), "zh")
    own = lax.all_to_all(jnp.broadcast_to(valence, (8, *valence.shape)), NARROW, 0, 0, tiled=True)
    own, bands = lax.optimization_barrier((own, bands))
    for axis in ("zh", "y"):
        own = jnp.stack(around(own, axis))
    other = shifted(own, "co", 1)
    cols, rows = transform(pos, own, other, bands, gmap)

    rows = lax.all_to_all(rows, ("y", "co"), 0, 0, tiled=True)
    cols = lax.all_to_all(cols, NARROW, 0, 0, tiled=True)
    cols = around(cols, "y")
    rows = jnp.stack(around(rows, "zl")).reshape(2, 4, 2, 4, 16, 256)
    rows = around(rows, "x")

    ec = jnp.transpose(eps_cond.reshape(4, 4, 2, 8), (1, 2, 3, 0)).reshape(4, 2, 32, 1, 1)
    gap = jnp.broadcast_to(ec - eps_val, (4, 2, 32, 2, 8)).reshape(4, 2, 1, 512)
    ident = jnp.asarray(tables()[-1])
    scaled, hot, sign = prepare(pos, omega, rows, gap, gmap, ident)
    total = None
    for sy in (0, 1, 3, 2):
        mine = cols[sy]
        if sy == 2:
            mine, total = lax.optimization_barrier((mine, total))
        theirs = shifted(mine, "co", 1)
        total = product_step(sy, mine, theirs, scaled, hot, sign, total)
    return total


def solution(mesh):
    torus = Mesh(mesh.devices.reshape(4, 4, 2, 2, 4), AXES)
    return jax.shard_map(
        body,
        mesh=torus,
        in_specs=(P(None, AXES), P(AXES, None), P(), P(), P(), P()),
        out_specs=P(None, WIDE, NARROW),
        check_vma=False,
    )
```

```python
import jax
import jax.numpy as jnp
import ml_dtypes
import numpy as np
from jax import lax
from jax.experimental import pallas as pl
from jax.experimental.pallas import tpu as pltpu
from jax.sharding import Mesh
from jax.sharding import PartitionSpec as P

GRID = 32
AXES = ("zh", "y", "co", "zl", "x")
WIDE = ("zh", "y", "co")
NARROW = ("zl", "x")
NPW = 8192
DISC = 256
NKX = 26
CAN = 640
BF = jnp.bfloat16
F32 = jnp.float32


def split_bf16(value):
    high = value.astype(BF)
    return high, (value - high.astype(value.dtype)).astype(BF)


def tables():
    k = np.arange(GRID)
    fold = np.where(k < GRID // 2, k, k - GRID)
    length = fold[:, None, None] ** 2 + fold[None, :, None] ** 2 + fold[None, None, :] ** 2
    ordered = np.sort(length.ravel())[:NPW]
    limit = ordered[-1]
    disc = []
    for ky in range(-15, 16):
        for kz in range(0, 16):
            if ky * ky + kz * kz <= limit and (kz > 0 or ky >= 0):
                disc.append((ky, kz))
    assert len(disc) <= DISC
    points = np.arange(GRID)
    wave = np.zeros((GRID, GRID, 2 * DISC))
    key = np.full((DISC, 1), -9000, np.int32)
    for m, (ky, kz) in enumerate(disc):
        angle = 2 * np.pi * ((ky * points[:, None] + kz * points[None, :]) % GRID) / GRID
        wave[:, :, m] = np.cos(angle)
        wave[:, :, DISC + m] = -np.sin(angle)
        key[m, 0] = ky * 64 + kz
    kx = np.arange(NKX) - 12
    assert limit < 13 * 13
    angle = 2 * np.pi * (kx[:, None] * points[None, :] % GRID) / GRID
    eye = np.eye(8)
    along = np.concatenate([np.kron(np.cos(angle), eye), np.kron(np.sin(angle), eye)])
    blocks = 8
    col_key = np.full((blocks, 1, CAN), -8000, np.int32)
    col_kx = np.zeros((blocks, 1, CAN), np.int32)
    col_id = np.full((blocks, 1, CAN), -(1 << 20), np.int32)
    size = NPW // blocks
    for j in range(blocks):
        low, high = ordered[j * size], ordered[(j + 1) * size - 1]
        n = 0
        for ky, kz in disc:
            for x in range(-12, 13):
                if (ky, kz) == (0, 0) and x < 0:
                    continue
                if low <= x * x + ky * ky + kz * kz <= high:
                    col_key[j, 0, n] = ky * 64 + kz
                    col_kx[j, 0, n] = x + 12
                    col_id[j, 0, n] = (x * 64 + ky) * 64 + kz
                    n += 1
        assert n <= CAN
    wave = wave.reshape(GRID * GRID, 2 * DISC).astype(np.float32)
    along = along.astype(np.float32)
    return split_np(wave) + split_np(along) + (key, col_key, col_kx, col_id)


def split_np(value):


    high = value.astype(ml_dtypes.bfloat16)
    low = (value - high.astype(np.float32)).astype(ml_dtypes.bfloat16)
    return high, low


def folded(index):
    def fold(k):
        return jnp.where(k < GRID // 2, k, k - GRID)

    return (
        fold(lax.shift_right_logical(index, 10)),
        fold(lax.shift_right_logical(index, 5) & 31),
        fold(index & 31),
    )


def dot(a, b):
    return jnp.dot(a, b, preferred_element_type=F32)


def picked(spectrum, key, wanted, kx, zh, store):
    half = NKX * 8
    hot = jnp.where(key[...] == wanted, jnp.float32(1), jnp.float32(0)).astype(BF)
    found = dot(spectrum[...], hot)
    masks = [jnp.broadcast_to(kx == i, (8, wanted.shape[1])) for i in range(NKX - 1)]
    for s in range(4):
        parts = []
        for part in range(2):
            base = (2 * s + part) * half
            value = found[base : base + 8]
            for i in range(1, NKX - 1):
                value = jnp.where(masks[i], found[base + i * 8 : base + i * 8 + 8], value)
            parts.append(value)
        store((zh - s) & 3, *parts)


def fetch(sources, targets, sems):
    copies = [pltpu.make_async_copy(s, t, sems.at[i]) for i, (s, t) in enumerate(zip(sources, targets))]
    for copy in copies:
        copy.start()
    return copies


def column_kernel(pos, *refs):
    cols = refs[4]
    spectrum, key, col_key, col_kx = refs[5:9]
    for copy in fetch(refs[:4], refs[5:9], refs[9]):
        copy.wait()

    def columns(j, carry):
        def store(at, real, imag):
            cols[j, at] = jnp.concatenate([real, imag], axis=0).astype(BF)

        picked(spectrum, key, col_key[j], col_kx[j], pos[0], store)
        return carry

    lax.fori_loop(0, 8, columns, 0)


def transform_kernel(pos, *refs):
    sources, rows, spectrum, targets = refs[:12], refs[12], refs[13], refs[14:26]
    a_hi, a_lo, sems = refs[26:]
    own, other, band0, band1, band2, band3, wave_hi, wave_lo, along_hi, along_lo, key, gmap = targets
    zh, y, co = pos[0], pos[1], pos[2]
    copies = fetch(sources, targets, sems)
    for copy in copies[:6]:
        copy.wait()

    def product(q, carry):
        szh = (zh - q // 4) & 3
        sy = (y - q % 4) & 3
        start = pl.multiple_of(q * 16, 16)
        rows_of = [band[pl.ds(start, 16), :] for band in (band0, band1, band2, band3)]
        for n in range(8):
            mine = own[sy, szh, n]
            theirs = other[sy, szh, n]
            first = jnp.where(co == 0, mine, theirs)
            second = jnp.where(co == 0, theirs, mine)
            for s in range(4):
                pair = [first * rows_of[s][n : n + 1, :], second * rows_of[s][8 + n : 9 + n, :]]
                high, low = split_bf16(jnp.concatenate(pair, axis=0))
                at = pl.ds(pl.multiple_of(s * 256 + start, 16), 16)
                a_hi[at, n * 128 : (n + 1) * 128] = high
                a_lo[at, n * 128 : (n + 1) * 128] = low
        return carry

    lax.fori_loop(0, 16, product, 0)
    for copy in copies[6:]:
        copy.wait()
    field = dot(a_hi[...], wave_hi[...]) + (dot(a_lo[...], wave_hi[...]) + dot(a_hi[...], wave_lo[...]))
    half = NKX * 8
    norm = jnp.float32(1.0) / jnp.sqrt(jnp.float32(GRID**3))
    for s in range(4):
        f_hi, f_lo = split_bf16(field[s * 256 : s * 256 + 256])
        full = dot(along_hi[...], f_hi) + (dot(along_lo[...], f_hi) + dot(along_hi[...], f_lo))
        real = full[:half, :DISC] + full[half:, DISC:]
        imag = full[:half, DISC:] - full[half:, :DISC]
        spectrum[2 * s * half : (2 * s + 1) * half, :] = (real * norm).astype(BF)
        spectrum[(2 * s + 1) * half : (2 * s + 2) * half, :] = (imag * norm).astype(BF)

    def row_blocks(r, carry):
        kx, ky, kz = folded(gmap[zh * 4 + r])
        flip = jnp.where((kz < 0) | ((kz == 0) & (ky < 0)), -1, 1)
        sign = flip.astype(F32)

        def store(at, real, imag):
            both = jnp.concatenate([real, imag * sign], axis=0).astype(BF)
            rows[2 * r, at] = both[:, :256]
            rows[2 * r + 1, at] = both[:, 256:]

        picked(spectrum, key, flip * (ky * 64 + kz), flip * kx + 12, zh, store)
        return carry

    lax.fori_loop(0, 4, row_blocks, 0)


def whole(value):
    zeros = (0,) * len(value.shape)
    return pl.BlockSpec(value.shape, lambda *_: zeros, pipeline_mode=pl.Buffered(1))


def resident():
    return pl.BlockSpec(memory_space=pltpu.VMEM)


def transform(pos, own, other, bands, gmap):
    wave_hi, wave_lo, along_hi, along_lo, key, col_key, col_kx, _ = (jnp.asarray(t) for t in tables())
    gmap = gmap.reshape(16, 1, 512)
    operands = [own, other, *bands, wave_hi, wave_lo, along_hi, along_lo, key, gmap]
    anywhere = pl.BlockSpec(memory_space=pl.ANY)
    in_hbm = pl.BlockSpec(memory_space=pltpu.HBM)
    lines = 8 * NKX * 8
    rows, spectrum = pl.pallas_call(
        transform_kernel,
        grid_spec=pltpu.PrefetchScalarGridSpec(
            num_scalar_prefetch=1,
            grid=(1,),
            in_specs=[anywhere] * 2 + [in_hbm] + [anywhere] * 3 + [in_hbm] * 6,
            out_specs=[whole(np.zeros((8, 4, 16, 256))), whole(np.zeros((lines, DISC)))],
            scratch_shapes=[pltpu.VMEM(v.shape, v.dtype) for v in operands]
            + [pltpu.VMEM((1024, 1024), BF), pltpu.VMEM((1024, 1024), BF), pltpu.SemaphoreType.DMA((len(operands),))],
        ),
        out_shape=[jax.ShapeDtypeStruct((8, 4, 16, 256), BF), jax.ShapeDtypeStruct((lines, DISC), BF)],
        compiler_params=pltpu.CompilerParams(vmem_limit_bytes=60 << 20),
        cost_estimate=pl.CostEstimate(flops=8 * 10**9, transcendentals=0, bytes_accessed=6 * 2**20),
        name="pair_transform",
    )(pos, *operands)
    cols = pl.pallas_call(
        column_kernel,
        grid_spec=pltpu.PrefetchScalarGridSpec(
            num_scalar_prefetch=1,
            grid=(1,),
            in_specs=[in_hbm] * 4,
            out_specs=whole(np.zeros((8, 4, 16, CAN))),
            scratch_shapes=[pltpu.VMEM(v.shape, v.dtype) for v in (spectrum, key, col_key, col_kx)]
            + [pltpu.SemaphoreType.DMA((4,))],
        ),
        out_shape=jax.ShapeDtypeStruct((8, 4, 16, CAN), BF),
        compiler_params=pltpu.CompilerParams(vmem_limit_bytes=60 << 20),
        cost_estimate=pl.CostEstimate(flops=8 * 10**9, transcendentals=0, bytes_accessed=2 * 2**20),
        name="column_pairs",
    )(pos, spectrum, key, col_key, col_kx)
    return cols, rows


def prepare_kernel(pos, omega, r0, r1, r2, r3, gap, gmap, ident, scaled, hot, sign, row_k):
    co, zl, x = pos[2], pos[3], pos[4]

    @pl.when(pl.program_id(0) == 0)
    def _():
        kx, ky, kz = folded(gmap[0])
        flip = jnp.where((kz < 0) | ((kz == 0) & ((ky < 0) | ((ky == 0) & (kx < 0)))), -1, 1)
        wanted = (flip * ((kx * 64 + ky) * 64 + kz)).astype(F32)
        names = jnp.broadcast_to(ident[0].astype(F32), (128, CAN)).T
        for t in range(8):
            at = slice(t * 128, (t + 1) * 128)
            hot[:, at] = jnp.where(names == wanted[:, at], jnp.float32(1), jnp.float32(0)).astype(BF)
        sign[...] = jnp.concatenate([jnp.ones((8, 1024), F32), jnp.broadcast_to(flip.astype(F32), (8, 1024))], axis=0)

    for side in range(2):
        co_at = co if side == 0 else 1 - co
        for sx, ref in enumerate((r0, r1, r2, r3)):
            for szl in range(2):
                n = (zl ^ szl) * 4 + ((x - sx) & 3)
                to = pl.multiple_of(side * 512 + n * 64, 64)
                row_k[pl.ds(to, 64), :] = ref[szl, 0, co_at].reshape(64, 256)
        energy = gap[0, co_at]
        total = row_k[side * 512 : side * 512 + 512, :].astype(F32).T
        for w in range(6):
            weight = -2.0 * energy / (energy * energy + omega[w] * omega[w])
            weight = weight / jnp.sqrt(jnp.float32(2048))
            scaled[pl.program_id(0), w * 256 : (w + 1) * 256, side * 512 : side * 512 + 512] = (total * weight).astype(BF)


def prepare(pos, omega, rows, gap, gmap, ident):
    row_spec = pl.BlockSpec((2, 1, 2, 4, 16, 256), lambda s, pos, om: (0, (pos[1] - s) & 3, 0, 0, 0, 0))
    rows = [pltpu.with_memory_space_constraint(r, pltpu.HBM) for r in rows]
    gmap, ident = (pltpu.with_memory_space_constraint(v, pltpu.HBM) for v in (gmap.reshape(8, 1, 1024), ident))
    return pl.pallas_call(
        prepare_kernel,
        grid_spec=pltpu.PrefetchScalarGridSpec(
            num_scalar_prefetch=2,
            grid=(4,),
            in_specs=[row_spec] * 4
            + [
                pl.BlockSpec((1, 2, 1, 512), lambda s, pos, om: ((pos[1] - s) & 3, 0, 0, 0)),
                pl.BlockSpec((1, 1, 1024), lambda s, pos, om: (pos[3] * 4 + pos[4], 0, 0)),
                pl.BlockSpec((1, 1, CAN), lambda s, pos, om: (pos[3] * 4 + pos[4], 0, 0)),
            ],
            out_specs=[resident(), resident(), resident()],
            scratch_shapes=[pltpu.VMEM((1024, 256), BF)],
        ),
        out_shape=[pltpu.VMEM((4, 1536, 1024), BF), pltpu.VMEM((CAN, 1024), BF), pltpu.VMEM((16, 1024), F32)],
        compiler_params=pltpu.CompilerParams(vmem_limit_bytes=20 << 20),
        cost_estimate=pl.CostEstimate(flops=10**9, transcendentals=0, bytes_accessed=20 * 2**20),
        name="scaled_rows",
    )(pos, omega, *rows, gap, gmap, ident)


def expand(mine, theirs, hot, sign, cols):
    for side, ref in enumerate((mine, theirs)):
        full = dot(ref[...].reshape(512, CAN), hot[...]).reshape(32, 16, 1024) * sign[...][None]
        full = full.reshape(512, 1024).astype(BF)
        for t in range(4):
            cols[t, side * 512 : side * 512 + 512, :] = full[:, t * 256 : (t + 1) * 256]


def product_step(sy, mine, theirs, scaled, hot, sign, total, last):
    def kernel(mine, theirs, scaled, hot, sign, *refs):
        out, cols = refs[-2:]
        add = None if total is None else refs[0]
        if last:
            n = pl.program_id(0)
            pl.when(n == 0)(lambda: expand(mine, theirs, hot, sign, cols))
            at = pl.ds(pl.multiple_of(n * 256, 256), 256)
            out[...] = add[:, :, at] + dot(scaled[sy], cols[n]).reshape(6, 256, 256)
        else:
            expand(mine, theirs, hot, sign, cols)
            for n in range(4):
                at = slice(n * 256, n * 256 + 256)
                part = dot(scaled[sy], cols[n]).reshape(6, 256, 256)
                out[:, :, at] = part if add is None else add[:, :, at] + part

    operands = [mine, theirs, scaled, hot, sign] + ([] if total is None else [total])
    aliases = {} if total is None or last else {5: 0}
    return pl.pallas_call(
        kernel,
        grid=(4 if last else 1,),
        in_specs=[resident()] * len(operands),
        out_specs=pl.BlockSpec((6, 256, 256), lambda n: (0, 0, n)) if last else resident(),
        scratch_shapes=[pltpu.VMEM((4, 1024, 256), BF)],
        out_shape=(jax.ShapeDtypeStruct if last else pltpu.VMEM)((6, 256, 1024), F32),
        input_output_aliases=aliases,
        compiler_params=pltpu.CompilerParams(vmem_limit_bytes=20 << 20),
        cost_estimate=pl.CostEstimate(flops=46 * 10**8, transcendentals=0, bytes_accessed=10 * 2**20),
        name="response_product",
    )(*operands)


def shifted(value, axis, shift):
    size = lax.axis_size(axis)
    return lax.ppermute(value, axis, [(i, (i + shift) % size) for i in range(size)])


def around(value, axis):
    return [value] + [shifted(value, axis, s) for s in range(1, lax.axis_size(axis))]


def ring(value, axis):
    behind = shifted(value, axis, 1)
    ahead = shifted(value, axis, 3)
    half = value.shape[0] // 2
    opposite = [shifted(ahead[:half], axis, 3), shifted(behind[half:], axis, 1)]
    return [value, behind, opposite, ahead]


def body(valence, conduction, eps_val, eps_cond, omega, gmap):
    pos = jnp.stack([lax.axis_index(a) for a in AXES]).astype(jnp.int32)
    bands = around(conduction.reshape(256, 128), "zh")
    own = lax.all_to_all(jnp.broadcast_to(valence, (8, *valence.shape)), NARROW, 0, 0, tiled=True)
    own, bands = lax.optimization_barrier((own, bands))
    for axis in ("zh", "y"):
        own = jnp.stack(around(own, axis))
    other = shifted(own, "co", 1)
    cols, rows = transform(pos, own, other, bands, gmap)

    rows = lax.all_to_all(rows, ("y", "co"), 0, 0, tiled=True)
    cols = lax.all_to_all(cols, NARROW, 0, 0, tiled=True)
    cols = ring(cols, "y")
    far_cols = cols.pop(2)
    rows = jnp.stack(around(rows, "zl")).reshape(2, 4, 2, 4, 16, 256)
    rows = ring(rows, "x")
    rows[2] = jnp.concatenate(rows[2])

    rows, cols = lax.optimization_barrier((rows, cols))
    ec = jnp.transpose(eps_cond.reshape(4, 4, 2, 8), (1, 2, 3, 0)).reshape(4, 2, 32, 1, 1)
    gap = jnp.broadcast_to(ec - eps_val, (4, 2, 32, 2, 8)).reshape(4, 2, 1, 512)
    ident = jnp.asarray(tables()[-1])
    scaled, hot, sign = prepare(pos, omega, rows, gap, gmap, ident)
    total = None
    for sy, mine in zip((0, 1, 3), cols):
        theirs = shifted(mine, "co", 1)
        total = product_step(sy, mine, theirs, scaled, hot, sign, total, False)
    mine = jnp.concatenate(far_cols)
    theirs = shifted(mine, "co", 1)
    return product_step(2, mine, theirs, scaled, hot, sign, total, True)


def solution(mesh):
    torus = Mesh(mesh.devices.reshape(4, 4, 2, 2, 4), AXES)
    return jax.shard_map(
        body,
        mesh=torus,
        in_specs=(P(None, AXES), P(AXES, None), P(), P(), P(), P()),
        out_specs=P(None, WIDE, NARROW),
        check_vma=False,
    )
```

```python
import functools

import jax
import jax.numpy as jnp
import ml_dtypes
import numpy as np
from jax import lax
from jax.experimental import pallas as pl
from jax.experimental.pallas import tpu as pltpu
from jax.sharding import Mesh
from jax.sharding import PartitionSpec as P

GRID = 32
AXES = ("zh", "y", "co", "zl", "x")
WIDE = ("zh", "y", "co")
NARROW = ("zl", "x")
NPW = 8192
DISC = 256
NKX = 26
CAN = 640
BF = jnp.bfloat16
F32 = jnp.float32


def split_bf16(value):
    high = value.astype(BF)
    return high, (value - high.astype(value.dtype)).astype(BF)


def tables():
    k = np.arange(GRID)
    fold = np.where(k < GRID // 2, k, k - GRID)
    length = fold[:, None, None] ** 2 + fold[None, :, None] ** 2 + fold[None, None, :] ** 2
    ordered = np.sort(length.ravel())[:NPW]
    limit = ordered[-1]
    disc = []
    for ky in range(-15, 16):
        for kz in range(0, 16):
            if ky * ky + kz * kz <= limit and (kz > 0 or ky >= 0):
                disc.append((ky, kz))
    assert len(disc) <= DISC
    points = np.arange(GRID)
    wave = np.zeros((GRID, GRID, 2 * DISC))
    key = np.full((DISC, 1), -9000, np.int32)
    for m, (ky, kz) in enumerate(disc):
        angle = 2 * np.pi * ((ky * points[:, None] + kz * points[None, :]) % GRID) / GRID
        wave[:, :, m] = np.cos(angle)
        wave[:, :, DISC + m] = -np.sin(angle)
        key[m, 0] = ky * 64 + kz
    kx = np.arange(NKX) - 12
    assert limit < 13 * 13
    angle = 2 * np.pi * (kx[:, None] * points[None, :] % GRID) / GRID
    eye = np.eye(8)
    along = np.concatenate([np.kron(np.cos(angle), eye), np.kron(np.sin(angle), eye)])
    blocks = 8
    col_key = np.full((blocks, 1, CAN), -8000, np.int32)
    col_kx = np.zeros((blocks, 1, CAN), np.int32)
    col_id = np.full((blocks, 1, CAN), -(1 << 20), np.int32)
    size = NPW // blocks
    for j in range(blocks):
        low, high = ordered[j * size], ordered[(j + 1) * size - 1]
        n = 0
        for ky, kz in disc:
            for x in range(-12, 13):
                if (ky, kz) == (0, 0) and x < 0:
                    continue
                if low <= x * x + ky * ky + kz * kz <= high:
                    col_key[j, 0, n] = ky * 64 + kz
                    col_kx[j, 0, n] = x + 12
                    col_id[j, 0, n] = (x * 64 + ky) * 64 + kz
                    n += 1
        assert n <= CAN
    wave = wave.reshape(GRID * GRID, 2 * DISC).astype(np.float32)
    along = along.astype(np.float32)
    return split_np(wave) + split_np(along) + (key, col_key, col_kx, col_id)


def split_np(value):


    high = value.astype(ml_dtypes.bfloat16)
    low = (value - high.astype(np.float32)).astype(ml_dtypes.bfloat16)
    return high, low


def folded(index):
    def fold(k):
        return jnp.where(k < GRID // 2, k, k - GRID)

    return (
        fold(lax.shift_right_logical(index, 10)),
        fold(lax.shift_right_logical(index, 5) & 31),
        fold(index & 31),
    )


def dot(a, b):
    return jnp.dot(a, b, preferred_element_type=F32)


def picked(spectrum, key, wanted, kx, zh, store):
    half = NKX * 8
    hot = jnp.where(key[...] == wanted, jnp.float32(1), jnp.float32(0)).astype(BF)
    found = dot(spectrum[...], hot)
    masks = [jnp.broadcast_to(kx == i, (8, wanted.shape[1])) for i in range(NKX - 1)]
    for s in range(4):
        parts = []
        for part in range(2):
            base = (2 * s + part) * half
            value = found[base : base + 8]
            for i in range(1, NKX - 1):
                value = jnp.where(masks[i], found[base + i * 8 : base + i * 8 + 8], value)
            parts.append(value)
        store((zh - s) & 3, *parts)


def fetch(sources, targets, sems):
    copies = [pltpu.make_async_copy(s, t, sems.at[i]) for i, (s, t) in enumerate(zip(sources, targets))]
    for copy in copies:
        copy.start()
    return copies


def column_kernel(first, count, pos, *refs):
    cols = refs[-6]
    spectrum, key, col_key, col_kx = refs[-5:-1]
    for copy in fetch(refs[:4], refs[-5:-1], refs[-1]):
        copy.wait()

    def columns(j, carry):
        def store(at, real, imag):
            cols[j, at] = jnp.concatenate([real, imag], axis=0).astype(BF)

        picked(spectrum, key, col_key[first + j], col_kx[first + j], pos[0], store)
        return carry

    lax.fori_loop(0, count, columns, 0)


def transform_kernel(pos, *refs):
    sources, rows, spectrum, targets = refs[:12], refs[12], refs[13], refs[14:26]
    a_hi, a_lo, sems = refs[26:]
    own, other, band0, band1, band2, band3, wave_hi, wave_lo, along_hi, along_lo, key, gmap = targets
    zh, y, co = pos[0], pos[1], pos[2]
    copies = fetch(sources, targets, sems)
    for copy in copies[:6]:
        copy.wait()

    def product(q, carry):
        szh = (zh - q // 4) & 3
        sy = (y - q % 4) & 3
        start = pl.multiple_of(q * 16, 16)
        rows_of = [band[pl.ds(start, 16), :] for band in (band0, band1, band2, band3)]
        for n in range(8):
            mine = own[sy, szh, n]
            theirs = other[sy, szh, n]
            first = jnp.where(co == 0, mine, theirs)
            second = jnp.where(co == 0, theirs, mine)
            for s in range(4):
                pair = [first * rows_of[s][n : n + 1, :], second * rows_of[s][8 + n : 9 + n, :]]
                high, low = split_bf16(jnp.concatenate(pair, axis=0))
                at = pl.ds(pl.multiple_of(s * 256 + start, 16), 16)
                a_hi[at, n * 128 : (n + 1) * 128] = high
                a_lo[at, n * 128 : (n + 1) * 128] = low
        return carry

    lax.fori_loop(0, 16, product, 0)
    for copy in copies[6:]:
        copy.wait()
    field = dot(a_hi[...], wave_hi[...]) + (dot(a_lo[...], wave_hi[...]) + dot(a_hi[...], wave_lo[...]))
    half = NKX * 8
    norm = jnp.float32(1.0) / jnp.sqrt(jnp.float32(GRID**3))
    for s in range(4):
        f_hi, f_lo = split_bf16(field[s * 256 : s * 256 + 256])
        full = dot(along_hi[...], f_hi) + (dot(along_lo[...], f_hi) + dot(along_hi[...], f_lo))
        real = full[:half, :DISC] + full[half:, DISC:]
        imag = full[:half, DISC:] - full[half:, :DISC]
        spectrum[2 * s * half : (2 * s + 1) * half, :] = (real * norm).astype(BF)
        spectrum[(2 * s + 1) * half : (2 * s + 2) * half, :] = (imag * norm).astype(BF)

    def row_blocks(r, carry):
        kx, ky, kz = folded(gmap[zh * 4 + r])
        flip = jnp.where((kz < 0) | ((kz == 0) & (ky < 0)), -1, 1)
        sign = flip.astype(F32)

        def store(at, real, imag):
            both = jnp.concatenate([real, imag * sign], axis=0).astype(BF)
            rows[2 * r, at] = both[:, :256]
            rows[2 * r + 1, at] = both[:, 256:]

        picked(spectrum, key, flip * (ky * 64 + kz), flip * kx + 12, zh, store)
        return carry

    lax.fori_loop(0, 4, row_blocks, 0)


def whole(value):
    zeros = (0,) * len(value.shape)
    return pl.BlockSpec(value.shape, lambda *_: zeros, pipeline_mode=pl.Buffered(1))


def resident():
    return pl.BlockSpec(memory_space=pltpu.VMEM)


def transform(pos, own, other, bands, gmap):
    wave_hi, wave_lo, along_hi, along_lo, key = (jnp.asarray(t) for t in tables()[:5])
    gmap = gmap.reshape(16, 1, 512)
    operands = [own, other, *bands, wave_hi, wave_lo, along_hi, along_lo, key, gmap]
    anywhere = pl.BlockSpec(memory_space=pl.ANY)
    in_hbm = pl.BlockSpec(memory_space=pltpu.HBM)
    lines = 8 * NKX * 8
    rows, spectrum = pl.pallas_call(
        transform_kernel,
        grid_spec=pltpu.PrefetchScalarGridSpec(
            num_scalar_prefetch=1,
            grid=(1,),
            in_specs=[anywhere] * 2 + [in_hbm] + [anywhere] * 3 + [in_hbm] * 6,
            out_specs=[whole(np.zeros((8, 4, 16, 256))), whole(np.zeros((lines, DISC)))],
            scratch_shapes=[pltpu.VMEM(v.shape, v.dtype) for v in operands]
            + [pltpu.VMEM((1024, 1024), BF), pltpu.VMEM((1024, 1024), BF), pltpu.SemaphoreType.DMA((len(operands),))],
        ),
        out_shape=[jax.ShapeDtypeStruct((8, 4, 16, 256), BF), jax.ShapeDtypeStruct((lines, DISC), BF)],
        compiler_params=pltpu.CompilerParams(vmem_limit_bytes=60 << 20),
        cost_estimate=pl.CostEstimate(flops=8 * 10**9, transcendentals=0, bytes_accessed=6 * 2**20),
        name="pair_transform",
    )(pos, *operands)
    return rows, spectrum


def column_pairs(pos, spectrum, first, count, earlier):
    key, col_key, col_kx = (jnp.asarray(t) for t in tables()[4:7])
    in_hbm = pl.BlockSpec(memory_space=pltpu.HBM)
    operands = [spectrum, key, col_key, col_kx] + ([] if earlier is None else [earlier])
    return pl.pallas_call(
        functools.partial(column_kernel, first, count),
        grid_spec=pltpu.PrefetchScalarGridSpec(
            num_scalar_prefetch=1,
            grid=(1,),
            in_specs=[in_hbm] * len(operands),
            out_specs=pl.BlockSpec((count, 4, 16, CAN), lambda i, pos: (first // count, 0, 0, 0)),
            scratch_shapes=[pltpu.VMEM(v.shape, v.dtype) for v in operands[:4]] + [pltpu.SemaphoreType.DMA((4,))],
        ),
        out_shape=jax.ShapeDtypeStruct((8, 4, 16, CAN), BF),
        input_output_aliases={} if earlier is None else {5: 0},
        compiler_params=pltpu.CompilerParams(vmem_limit_bytes=60 << 20),
        cost_estimate=pl.CostEstimate(flops=count * 10**9, transcendentals=0, bytes_accessed=2 * 2**20),
        name="column_pairs",
    )(pos, *operands)


def prepare_kernel(pos, omega, r0, r1, r2, r3, gap, gmap, ident, scaled, hot, sign, row_k):
    co, zl, x = pos[2], pos[3], pos[4]

    @pl.when(pl.program_id(0) == 0)
    def _():
        kx, ky, kz = folded(gmap[0])
        flip = jnp.where((kz < 0) | ((kz == 0) & ((ky < 0) | ((ky == 0) & (kx < 0)))), -1, 1)
        wanted = (flip * ((kx * 64 + ky) * 64 + kz)).astype(F32)
        names = jnp.broadcast_to(ident[0].astype(F32), (128, CAN)).T
        for t in range(8):
            at = slice(t * 128, (t + 1) * 128)
            hot[:, at] = jnp.where(names == wanted[:, at], jnp.float32(1), jnp.float32(0)).astype(BF)
        sign[...] = jnp.concatenate([jnp.ones((8, 1024), F32), jnp.broadcast_to(flip.astype(F32), (8, 1024))], axis=0)

    for side in range(2):
        co_at = co if side == 0 else 1 - co
        for sx, ref in enumerate((r0, r1, r2, r3)):
            for szl in range(2):
                n = (zl ^ szl) * 4 + ((x - sx) & 3)
                to = pl.multiple_of(side * 512 + n * 64, 64)
                row_k[pl.ds(to, 64), :] = ref[szl, 0, co_at].reshape(64, 256)
        energy = gap[0, co_at]
        total = row_k[side * 512 : side * 512 + 512, :].astype(F32).T
        for w in range(6):
            weight = -2.0 * energy / (energy * energy + omega[w] * omega[w])
            weight = weight / jnp.sqrt(jnp.float32(2048))
            scaled[pl.program_id(0), w * 256 : (w + 1) * 256, side * 512 : side * 512 + 512] = (total * weight).astype(BF)


def prepare(pos, omega, rows, gap, gmap, ident):
    row_spec = pl.BlockSpec((2, 1, 2, 4, 16, 256), lambda s, pos, om: (0, (pos[1] - s) & 3, 0, 0, 0, 0))
    rows = [pltpu.with_memory_space_constraint(r, pltpu.HBM) for r in rows]
    gmap, ident = (pltpu.with_memory_space_constraint(v, pltpu.HBM) for v in (gmap.reshape(8, 1, 1024), ident))
    return pl.pallas_call(
        prepare_kernel,
        grid_spec=pltpu.PrefetchScalarGridSpec(
            num_scalar_prefetch=2,
            grid=(4,),
            in_specs=[row_spec] * 4
            + [
                pl.BlockSpec((1, 2, 1, 512), lambda s, pos, om: ((pos[1] - s) & 3, 0, 0, 0)),
                pl.BlockSpec((1, 1, 1024), lambda s, pos, om: (pos[3] * 4 + pos[4], 0, 0)),
                pl.BlockSpec((1, 1, CAN), lambda s, pos, om: (pos[3] * 4 + pos[4], 0, 0)),
            ],
            out_specs=[resident(), resident(), resident()],
            scratch_shapes=[pltpu.VMEM((1024, 256), BF)],
        ),
        out_shape=[pltpu.VMEM((4, 1536, 1024), BF), pltpu.VMEM((CAN, 1024), BF), pltpu.VMEM((16, 1024), F32)],
        compiler_params=pltpu.CompilerParams(vmem_limit_bytes=20 << 20),
        cost_estimate=pl.CostEstimate(flops=10**9, transcendentals=0, bytes_accessed=20 * 2**20),
        name="scaled_rows",
    )(pos, omega, *rows, gap, gmap, ident)


def expand(mine, theirs, hot, sign, cols):
    for side, ref in enumerate((mine, theirs)):
        full = dot(ref[...].reshape(512, CAN), hot[...]).reshape(32, 16, 1024) * sign[...][None]
        full = full.reshape(512, 1024).astype(BF)
        for t in range(4):
            cols[t, side * 512 : side * 512 + 512, :] = full[:, t * 256 : (t + 1) * 256]


def product_step(sy, mine, theirs, scaled, hot, sign, total, last):
    def kernel(mine, theirs, scaled, hot, sign, *refs):
        out, cols = refs[-2:]
        add = None if total is None else refs[0]
        if last:
            n = pl.program_id(0)
            pl.when(n == 0)(lambda: expand(mine, theirs, hot, sign, cols))
            at = pl.ds(pl.multiple_of(n * 256, 256), 256)
            out[...] = add[:, :, at] + dot(scaled[sy], cols[n]).reshape(6, 256, 256)
        else:
            expand(mine, theirs, hot, sign, cols)
            for n in range(4):
                at = slice(n * 256, n * 256 + 256)
                part = dot(scaled[sy], cols[n]).reshape(6, 256, 256)
                out[:, :, at] = part if add is None else add[:, :, at] + part

    operands = [mine, theirs, scaled, hot, sign] + ([] if total is None else [total])
    aliases = {} if total is None or last else {5: 0}
    return pl.pallas_call(
        kernel,
        grid=(4 if last else 1,),
        in_specs=[resident()] * len(operands),
        out_specs=pl.BlockSpec((6, 256, 256), lambda n: (0, 0, n)) if last else resident(),
        scratch_shapes=[pltpu.VMEM((4, 1024, 256), BF)],
        out_shape=(jax.ShapeDtypeStruct if last else pltpu.VMEM)((6, 256, 1024), F32),
        input_output_aliases=aliases,
        compiler_params=pltpu.CompilerParams(vmem_limit_bytes=20 << 20),
        cost_estimate=pl.CostEstimate(flops=46 * 10**8, transcendentals=0, bytes_accessed=10 * 2**20),
        name="response_product",
    )(*operands)


def shifted(value, axis, shift):
    size = lax.axis_size(axis)
    return lax.ppermute(value, axis, [(i, (i + shift) % size) for i in range(size)])


def around(value, axis):
    return [value] + [shifted(value, axis, s) for s in range(1, lax.axis_size(axis))]


def ring(value, axis):
    behind = shifted(value, axis, 1)
    ahead = shifted(value, axis, 3)
    half = value.shape[0] // 2
    opposite = [shifted(ahead[:half], axis, 3), shifted(behind[half:], axis, 1)]
    return [value, behind, opposite, ahead]


def body(valence, conduction, eps_val, eps_cond, omega, gmap):
    pos = jnp.stack([lax.axis_index(a) for a in AXES]).astype(jnp.int32)
    bands = around(conduction.reshape(256, 128), "zh")
    own = lax.all_to_all(jnp.broadcast_to(valence, (8, *valence.shape)), NARROW, 0, 0, tiled=True)
    own, bands = lax.optimization_barrier((own, bands))
    own = jnp.stack(around(own, "zh"))
    ec = jnp.transpose(eps_cond.reshape(4, 4, 2, 8), (1, 2, 3, 0)).reshape(4, 2, 32, 1, 1)
    gap = jnp.broadcast_to(ec - eps_val, (4, 2, 32, 2, 8)).reshape(4, 2, 1, 512)
    own, gap = lax.optimization_barrier((own, gap))
    own = jnp.stack(around(own, "y"))
    other = shifted(own, "co", 1)
    rows, spectrum = transform(pos, own, other, bands, gmap)

    rows = lax.all_to_all(rows, ("y", "co"), 0, 0, tiled=True)
    cols = column_pairs(pos, spectrum, 0, 8, None)
    rows = jnp.stack(around(rows, "zl")).reshape(2, 4, 2, 4, 16, 256)
    cols, rows = lax.optimization_barrier((cols, rows))
    cols = lax.all_to_all(cols, NARROW, 0, 0, tiled=True)
    rows = ring(rows, "x")
    rows[2] = jnp.concatenate(rows[2])
    ident = jnp.asarray(tables()[-1])
    behind, ahead = shifted(cols, "y", 1), shifted(cols, "y", 3)
    scaled, hot, sign = prepare(pos, omega, rows, gap, gmap, ident)
    total = product_step(0, cols, shifted(cols, "co", 1), scaled, hot, sign, None, False)
    total, behind, ahead = lax.optimization_barrier((total, behind, ahead))
    far = jnp.concatenate([shifted(ahead[:4], "y", 3), shifted(behind[4:], "y", 1)])
    for sy, mine in ((1, behind), (3, ahead), (2, far)):
        theirs = shifted(mine, "co", 1)
        total = product_step(sy, mine, theirs, scaled, hot, sign, total, sy == 2)
    return total


def solution(mesh):
    torus = Mesh(mesh.devices.reshape(4, 4, 2, 2, 4), AXES)
    return jax.shard_map(
        body,
        mesh=torus,
        in_specs=(P(None, AXES), P(AXES, None), P(), P(), P(), P()),
        out_specs=P(None, WIDE, NARROW),
        check_vma=False,
    )
```

```python
import functools

import jax
import jax.numpy as jnp
import ml_dtypes
import numpy as np
from jax import lax
from jax.experimental import pallas as pl
from jax.experimental.pallas import tpu as pltpu
from jax.sharding import Mesh
from jax.sharding import PartitionSpec as P

GRID = 32
AXES = ("zh", "y", "co", "zl", "x")
WIDE = ("zh", "y", "co")
NARROW = ("zl", "x")
NPW = 8192
DISC = 256
NKX = 26
CAN = 640
BF = jnp.bfloat16
F32 = jnp.float32


def split_bf16(value):
    high = value.astype(BF)
    return high, (value - high.astype(value.dtype)).astype(BF)


def tables():
    k = np.arange(GRID)
    fold = np.where(k < GRID // 2, k, k - GRID)
    length = fold[:, None, None] ** 2 + fold[None, :, None] ** 2 + fold[None, None, :] ** 2
    ordered = np.sort(length.ravel())[:NPW]
    limit = ordered[-1]
    disc = []
    for ky in range(-15, 16):
        for kz in range(0, 16):
            if ky * ky + kz * kz <= limit and (kz > 0 or ky >= 0):
                disc.append((ky, kz))
    assert len(disc) <= DISC
    points = np.arange(GRID)
    wave = np.zeros((GRID, GRID, 2 * DISC))
    key = np.full((DISC, 1), -9000, np.int32)
    for m, (ky, kz) in enumerate(disc):
        angle = 2 * np.pi * ((ky * points[:, None] + kz * points[None, :]) % GRID) / GRID
        wave[:, :, m] = np.cos(angle)
        wave[:, :, DISC + m] = -np.sin(angle)
        key[m, 0] = ky * 64 + kz
    kx = np.arange(NKX) - 12
    assert limit < 13 * 13
    angle = 2 * np.pi * (kx[:, None] * points[None, :] % GRID) / GRID
    eye = np.eye(8)
    along = np.concatenate([np.kron(np.cos(angle), eye), np.kron(np.sin(angle), eye)])
    blocks = 8
    col_key = np.full((blocks, 1, CAN), -8000, np.int32)
    col_kx = np.zeros((blocks, 1, CAN), np.int32)
    col_id = np.full((blocks, 1, CAN), -(1 << 20), np.int32)
    size = NPW // blocks
    for j in range(blocks):
        low, high = ordered[j * size], ordered[(j + 1) * size - 1]
        n = 0
        for ky, kz in disc:
            for x in range(-12, 13):
                if (ky, kz) == (0, 0) and x < 0:
                    continue
                if low <= x * x + ky * ky + kz * kz <= high:
                    col_key[j, 0, n] = ky * 64 + kz
                    col_kx[j, 0, n] = x + 12
                    col_id[j, 0, n] = (x * 64 + ky) * 64 + kz
                    n += 1
        assert n <= CAN
    wave = wave.reshape(GRID * GRID, 2 * DISC).astype(np.float32)
    along = along.astype(np.float32)
    return split_np(wave) + split_np(along) + (key, col_key, col_kx, col_id)


def split_np(value):


    high = value.astype(ml_dtypes.bfloat16)
    low = (value - high.astype(np.float32)).astype(ml_dtypes.bfloat16)
    return high, low


def folded(index):
    def fold(k):
        return jnp.where(k < GRID // 2, k, k - GRID)

    return (
        fold(lax.shift_right_logical(index, 10)),
        fold(lax.shift_right_logical(index, 5) & 31),
        fold(index & 31),
    )


def dot(a, b):
    return jnp.dot(a, b, preferred_element_type=F32)


def fetch(sources, targets, sems):
    copies = [pltpu.make_async_copy(s, t, sems.at[i]) for i, (s, t) in enumerate(zip(sources, targets))]
    for copy in copies:
        copy.start()
    return copies


def picked(spectrum, count, key, wanted, kx, store):
    half = NKX * 8
    hot = jnp.where(key[...] == wanted, jnp.float32(1), jnp.float32(0)).astype(BF)
    found = dot(spectrum[: 2 * count * half, :], hot)
    masks = [jnp.broadcast_to(kx == i, (8, wanted.shape[1])) for i in range(NKX - 1)]
    for s in range(count):
        parts = []
        for part in range(2):
            base = (2 * s + part) * half
            value = found[base : base + 8]
            for i in range(1, NKX - 1):
                value = jnp.where(masks[i], found[base + i * 8 : base + i * 8 + 8], value)
            parts.append(value)
        store(s, *parts)


def waves(pos, own, other, bands, wave_hi, wave_lo, along_hi, along_lo, ready, a_hi, a_lo, spectrum, first):
    zh, y, co = pos[0], pos[1], pos[2]
    count = len(bands)

    def product(q, carry):
        szh = (zh - q // 4) & 3
        sy = (y - q % 4) & 3
        start = pl.multiple_of(q * 16, 16)
        rows_of = [band[pl.ds(start, 16), :] for band in bands]
        for n in range(8):
            mine = own[sy, szh, n]
            theirs = other[sy, szh, n]
            lower = jnp.where(co == 0, mine, theirs)
            upper = jnp.where(co == 0, theirs, mine)
            for s in range(count):
                pair = [lower * rows_of[s][n : n + 1, :], upper * rows_of[s][8 + n : 9 + n, :]]
                high, low = split_bf16(jnp.concatenate(pair, axis=0))
                at = pl.ds(pl.multiple_of(s * 256 + start, 16), 16)
                a_hi[at, n * 128 : (n + 1) * 128] = high
                a_lo[at, n * 128 : (n + 1) * 128] = low
        return carry

    lax.fori_loop(0, 16, product, 0)
    ready()
    field = dot(a_hi[...], wave_hi[...]) + (dot(a_lo[...], wave_hi[...]) + dot(a_hi[...], wave_lo[...]))
    half = NKX * 8
    norm = jnp.float32(1.0) / jnp.sqrt(jnp.float32(GRID**3))
    for s in range(count):
        f_hi, f_lo = split_bf16(field[s * 256 : s * 256 + 256])
        full = dot(along_hi[...], f_hi) + (dot(along_lo[...], f_hi) + dot(along_hi[...], f_lo))
        real = full[:half, :DISC] + full[half:, DISC:]
        imag = full[:half, DISC:] - full[half:, :DISC]
        at = 2 * (first + s) * half
        spectrum[at : at + half, :] = (real * norm).astype(BF)
        spectrum[at + half : at + 2 * half, :] = (imag * norm).astype(BF)


def row_kernel(pos, *refs):
    sources, rows, spectrum, targets = refs[:9], refs[9], refs[10], refs[11:20]
    a_hi, a_lo, sems = refs[20:]
    own, other, band, wave_hi, wave_lo, along_hi, along_lo, key, gmap = targets
    copies = fetch(sources, targets, sems)
    for copy in copies[:3]:
        copy.wait()

    def ready():
        for copy in copies[3:]:
            copy.wait()

    waves(pos, own, other, [band], wave_hi, wave_lo, along_hi, along_lo, ready, a_hi, a_lo, spectrum, 0)

    def row_blocks(r, carry):
        kx, ky, kz = folded(gmap[r])
        flip = jnp.where((kz < 0) | ((kz == 0) & (ky < 0)), -1, 1)
        sign = flip.astype(F32)

        def store(s, real, imag):
            both = jnp.concatenate([real, imag * sign], axis=0).astype(BF)
            for t in range(4):
                rows[4 * r + t] = both[:, t * 256 : (t + 1) * 256]

        picked(spectrum, 1, key, flip * (ky * 64 + kz), flip * kx + 12, store)
        return carry

    lax.fori_loop(0, 8, row_blocks, 0)


def column_kernel(pos, *refs):
    sources, cols, targets = refs[:13], refs[13], refs[14:27]
    spectrum, a_hi, a_lo, sems = refs[27:]
    first, own, other, band1, band2, band3, wave_hi, wave_lo, along_hi, along_lo, key, col_key, col_kx = targets
    zl, x = pos[3], pos[4]
    copies = fetch(sources, targets, sems)
    for copy in copies[:6]:
        copy.wait()

    def ready():
        for copy in copies[6:]:
            copy.wait()

    spectrum[: 2 * NKX * 8, :] = first[...]
    bands = [band1, band2, band3]
    waves(pos, own, other, bands, wave_hi, wave_lo, along_hi, along_lo, ready, a_hi, a_lo, spectrum, 1)

    def columns(part, carry):
        j = (zl ^ part) * 4 + x

        def store(s, real, imag):
            cols[part, (x - s) & 3] = jnp.concatenate([real, imag], axis=0).astype(BF)

        picked(spectrum, 4, key, col_key[j], col_kx[j], store)
        return carry

    lax.fori_loop(0, 2, columns, 0)


def whole(shape):
    return pl.BlockSpec(shape, lambda *_: (0,) * len(shape), pipeline_mode=pl.Buffered(1))


def resident():
    return pl.BlockSpec(memory_space=pltpu.VMEM)


def transform_call(kernel, pos, operands, outs, scratch, flops, name):
    return pl.pallas_call(
        kernel,
        grid_spec=pltpu.PrefetchScalarGridSpec(
            num_scalar_prefetch=1,
            grid=(1,),
            in_specs=[pl.BlockSpec(memory_space=pl.ANY)] * len(operands),
            out_specs=[whole(v.shape) for v in outs],
            scratch_shapes=[pltpu.VMEM(v.shape, v.dtype) for v in operands]
            + scratch
            + [pltpu.SemaphoreType.DMA((len(operands),))],
        ),
        out_shape=outs,
        compiler_params=pltpu.CompilerParams(vmem_limit_bytes=60 << 20),
        cost_estimate=pl.CostEstimate(flops=flops, transcendentals=0, bytes_accessed=6 * 2**20),
        name=name,
    )(pos, *operands)


def row_pairs(pos, own, other, band, gmap):
    consts = [jnp.asarray(t) for t in tables()[:5]]
    outs = [jax.ShapeDtypeStruct((32, 16, 256), BF), jax.ShapeDtypeStruct((2 * NKX * 8, DISC), BF)]
    scratch = [pltpu.VMEM((256, 1024), BF)] * 2
    operands = [own, other, band, *consts, gmap.reshape(8, 1, 1024)]
    return transform_call(row_kernel, pos, operands, outs, scratch, 4 * 10**9, "row_pairs")


def column_pairs(pos, first, own, other, bands):
    consts = [jnp.asarray(t) for t in tables()[:7]]
    outs = [jax.ShapeDtypeStruct((2, 4, 16, CAN), BF)]
    scratch = [pltpu.VMEM((8 * NKX * 8, DISC), BF)] + [pltpu.VMEM((768, 1024), BF)] * 2
    operands = [first, own, other, *bands, *consts]
    return transform_call(column_kernel, pos, operands, outs, scratch, 8 * 10**9, "column_pairs")[0]


def prepare_kernel(pos, omega, r0, r1, r2, r3, gap, gmap, ident, scaled, hot, sign, row_k):
    zh, co, zl, x = pos[0], pos[2], pos[3], pos[4]

    @pl.when(pl.program_id(0) == 0)
    def _():
        kx, ky, kz = folded(gmap[0])
        flip = jnp.where((kz < 0) | ((kz == 0) & ((ky < 0) | ((ky == 0) & (kx < 0)))), -1, 1)
        wanted = (flip * ((kx * 64 + ky) * 64 + kz)).astype(F32)
        names = jnp.broadcast_to(ident[0].astype(F32), (128, CAN)).T
        for t in range(8):
            at = slice(t * 128, (t + 1) * 128)
            hot[:, at] = jnp.where(names == wanted[:, at], jnp.float32(1), jnp.float32(0)).astype(BF)
        sign[...] = jnp.concatenate([jnp.ones((8, 1024), F32), jnp.broadcast_to(flip.astype(F32), (8, 1024))], axis=0)

    for side in range(2):
        co_at = co if side == 0 else 1 - co
        energies = []
        for s in range(4):
            zh_at = (zh - s) & 3
            energies.append(gap[zh_at, 0, co_at])
            for sx, ref in enumerate((r0, r1, r2, r3)):
                for szl in range(2):
                    n = (zl ^ szl) * 4 + ((x - sx) & 3)
                    to = pl.multiple_of(side * 512 + s * 128 + n * 16, 16)
                    row_k[pl.ds(to, 16), :] = ref[szl, zh_at, 0, co_at]
        energy = jnp.concatenate(energies, axis=1)
        total = row_k[side * 512 : side * 512 + 512, :].astype(F32).T
        for w in range(6):
            weight = -2.0 * energy / (energy * energy + omega[w] * omega[w])
            weight = weight / jnp.sqrt(jnp.float32(2048))
            at = slice(side * 512, side * 512 + 512)
            scaled[pl.program_id(0), w * 256 : (w + 1) * 256, at] = (total * weight).astype(BF)


def prepare(pos, omega, rows, gap, gmap, ident):
    rows = [pltpu.with_memory_space_constraint(r, pltpu.HBM) for r in rows]
    gmap, ident = (pltpu.with_memory_space_constraint(v, pltpu.HBM) for v in (gmap.reshape(8, 1, 1024), ident))
    row_spec = pl.BlockSpec((2, 4, 1, 2, 16, 256), lambda s, pos, om: (0, 0, (pos[1] - s) & 3, 0, 0, 0))
    return pl.pallas_call(
        prepare_kernel,
        grid_spec=pltpu.PrefetchScalarGridSpec(
            num_scalar_prefetch=2,
            grid=(4,),
            in_specs=[row_spec] * 4
            + [
                pl.BlockSpec((4, 1, 2, 1, 128), lambda s, pos, om: (0, (pos[1] - s) & 3, 0, 0, 0)),
                pl.BlockSpec((1, 1, 1024), lambda s, pos, om: (pos[3] * 4 + pos[4], 0, 0)),
                pl.BlockSpec((1, 1, CAN), lambda s, pos, om: (pos[3] * 4 + pos[4], 0, 0)),
            ],
            out_specs=[resident(), resident(), resident()],
            scratch_shapes=[pltpu.VMEM((1024, 256), BF)],
        ),
        out_shape=[pltpu.VMEM((4, 1536, 1024), BF), pltpu.VMEM((CAN, 1024), BF), pltpu.VMEM((16, 1024), F32)],
        compiler_params=pltpu.CompilerParams(vmem_limit_bytes=20 << 20),
        cost_estimate=pl.CostEstimate(flops=10**9, transcendentals=0, bytes_accessed=20 * 2**20),
        name="scaled_rows",
    )(pos, omega, *rows, gap, gmap, ident)


def expand(mine, theirs, hot, sign, cols):
    for side, ref in enumerate((mine, theirs)):
        full = dot(ref[...].reshape(512, CAN), hot[...]).reshape(32, 16, 1024) * sign[...][None]
        full = full.reshape(512, 1024).astype(BF)
        for t in range(4):
            cols[t, side * 512 : side * 512 + 512, :] = full[:, t * 256 : (t + 1) * 256]


def product_step(sy, mine, theirs, scaled, hot, sign, total, last):
    def kernel(mine, theirs, scaled, hot, sign, *refs):
        out, cols = refs[-2:]
        add = None if total is None else refs[0]
        if last:
            n = pl.program_id(0)
            pl.when(n == 0)(lambda: expand(mine, theirs, hot, sign, cols))
            at = pl.ds(pl.multiple_of(n * 256, 256), 256)
            out[...] = add[:, :, at] + dot(scaled[sy], cols[n]).reshape(6, 256, 256)
        else:
            expand(mine, theirs, hot, sign, cols)
            for n in range(4):
                at = slice(n * 256, n * 256 + 256)
                part = dot(scaled[sy], cols[n]).reshape(6, 256, 256)
                out[:, :, at] = part if add is None else add[:, :, at] + part

    operands = [mine, theirs, scaled, hot, sign] + ([] if total is None else [total])
    aliases = {} if total is None or last else {5: 0}
    return pl.pallas_call(
        kernel,
        grid=(4 if last else 1,),
        in_specs=[resident()] * len(operands),
        out_specs=pl.BlockSpec((6, 256, 256), lambda n: (0, 0, n)) if last else resident(),
        scratch_shapes=[pltpu.VMEM((4, 1024, 256), BF)],
        out_shape=(jax.ShapeDtypeStruct if last else pltpu.VMEM)((6, 256, 1024), F32),
        input_output_aliases=aliases,
        compiler_params=pltpu.CompilerParams(vmem_limit_bytes=20 << 20),
        cost_estimate=pl.CostEstimate(flops=46 * 10**8, transcendentals=0, bytes_accessed=10 * 2**20),
        name="response_product",
    )(*operands)


def shifted(value, axis, shift):
    size = lax.axis_size(axis)
    return lax.ppermute(value, axis, [(i, (i + shift) % size) for i in range(size)])


def around(value, axis):
    return [value] + [shifted(value, axis, s) for s in range(1, lax.axis_size(axis))]


def neighbours(value, axis):
    return shifted(value, axis, 1), shifted(value, axis, 3)


def opposite(behind, ahead, axis):
    half = behind.shape[0] // 2
    return shifted(ahead[:half], axis, 3), shifted(behind[half:], axis, 1)


def body(valence, conduction, eps_val, eps_cond, omega, gmap):
    pos = jnp.stack([lax.axis_index(a) for a in AXES]).astype(jnp.int32)
    bands = around(conduction.reshape(256, 128), "x")
    own = lax.all_to_all(jnp.broadcast_to(valence, (8, *valence.shape)), NARROW, 0, 0, tiled=True)
    own, bands = lax.optimization_barrier((own, bands))
    own = jnp.stack(around(own, "zh"))
    gap = jnp.broadcast_to((eps_cond[:, None] - eps_val)[:, None, :], (256, 2, 8)).reshape(4, 4, 2, 1, 128)
    own, gap = lax.optimization_barrier((own, gap))
    own = jnp.stack(around(own, "y"))
    other = shifted(own, "co", 1)

    rows, spectrum = row_pairs(pos, own, other, bands[0], gmap)
    rows = lax.all_to_all(rows, WIDE, 0, 0, tiled=True)
    cols = column_pairs(pos, spectrum, own, other, bands[1:])
    kept, got = cols[0], shifted(cols[1], "zl", 1)
    lower = lax.axis_index("zl") == 0
    cols = jnp.concatenate([jnp.where(lower, kept, got), jnp.where(lower, got, kept)])
    behind, ahead = neighbours(cols, "zh")
    cols = jnp.stack([cols, behind, jnp.concatenate(opposite(behind, ahead, "zh")), ahead])

    rows = jnp.stack(around(rows, "zl")).reshape(2, 4, 4, 2, 16, 256)
    behind, ahead = neighbours(rows, "x")
    rows = [rows, behind, jnp.concatenate(opposite(behind, ahead, "x")), ahead]

    behind, ahead = neighbours(cols, "y")
    rows, behind, ahead = lax.optimization_barrier((rows, behind, ahead))
    far = opposite(behind, ahead, "y")
    scaled, hot, sign = prepare(pos, omega, rows, gap, gmap, jnp.asarray(tables()[-1]))
    total = product_step(0, cols, shifted(cols, "co", 1), scaled, hot, sign, None, False)
    total, far = lax.optimization_barrier((total, far))
    for sy, mine in ((1, behind), (3, ahead), (2, jnp.concatenate(far))):
        theirs = shifted(mine, "co", 1)
        total = product_step(sy, mine, theirs, scaled, hot, sign, total, sy == 2)
    return total


def solution(mesh):
    torus = Mesh(mesh.devices.reshape(4, 4, 2, 2, 4), AXES)
    return jax.shard_map(
        body,
        mesh=torus,
        in_specs=(P(None, AXES), P(AXES, None), P(), P(), P(), P()),
        out_specs=P(None, WIDE, NARROW),
        check_vma=False,
    )
```

```python
import functools

import jax
import jax.numpy as jnp
import ml_dtypes
import numpy as np
from jax import lax
from jax.experimental import pallas as pl
from jax.experimental.pallas import tpu as pltpu
from jax.sharding import Mesh
from jax.sharding import PartitionSpec as P

GRID = 32
AXES = ("zh", "y", "co", "zl", "x")
WIDE = ("zh", "y", "co")
NARROW = ("zl", "x")
NPW = 8192
DISC = 256
NKX = 26
CAN = 640
BF = jnp.bfloat16
F32 = jnp.float32


def split_bf16(value):
    high = value.astype(BF)
    return high, (value - high.astype(value.dtype)).astype(BF)


def tables():
    k = np.arange(GRID)
    fold = np.where(k < GRID // 2, k, k - GRID)
    length = fold[:, None, None] ** 2 + fold[None, :, None] ** 2 + fold[None, None, :] ** 2
    ordered = np.sort(length.ravel())[:NPW]
    limit = ordered[-1]
    disc = []
    for ky in range(-15, 16):
        for kz in range(0, 16):
            if ky * ky + kz * kz <= limit and (kz > 0 or ky >= 0):
                disc.append((ky, kz))
    assert len(disc) <= DISC
    points = np.arange(GRID)
    wave = np.zeros((GRID, GRID, 2 * DISC))
    key = np.full((DISC, 1), -9000, np.int32)
    for m, (ky, kz) in enumerate(disc):
        angle = 2 * np.pi * ((ky * points[:, None] + kz * points[None, :]) % GRID) / GRID
        wave[:, :, m] = np.cos(angle)
        wave[:, :, DISC + m] = -np.sin(angle)
        key[m, 0] = ky * 64 + kz
    kx = np.arange(NKX) - 12
    assert limit < 13 * 13
    angle = 2 * np.pi * (kx[:, None] * points[None, :] % GRID) / GRID
    eye = np.eye(8)
    along = np.concatenate([np.kron(np.cos(angle), eye), np.kron(np.sin(angle), eye)])
    blocks = 8
    col_key = np.full((blocks, 1, CAN), -8000, np.int32)
    col_kx = np.zeros((blocks, 1, CAN), np.int32)
    col_id = np.full((blocks, 1, CAN), -(1 << 20), np.int32)
    size = NPW // blocks
    for j in range(blocks):
        low, high = ordered[j * size], ordered[(j + 1) * size - 1]
        n = 0
        for ky, kz in disc:
            for x in range(-12, 13):
                if (ky, kz) == (0, 0) and x < 0:
                    continue
                if low <= x * x + ky * ky + kz * kz <= high:
                    col_key[j, 0, n] = ky * 64 + kz
                    col_kx[j, 0, n] = x + 12
                    col_id[j, 0, n] = (x * 64 + ky) * 64 + kz
                    n += 1
        assert n <= CAN
    wave = wave.reshape(GRID * GRID, 2 * DISC).astype(np.float32)
    along = along.astype(np.float32)
    return split_np(wave) + split_np(along) + (key, col_key, col_kx, col_id)


def split_np(value):


    high = value.astype(ml_dtypes.bfloat16)
    low = (value - high.astype(np.float32)).astype(ml_dtypes.bfloat16)
    return high, low


def folded(index):
    def fold(k):
        return jnp.where(k < GRID // 2, k, k - GRID)

    return (
        fold(lax.shift_right_logical(index, 10)),
        fold(lax.shift_right_logical(index, 5) & 31),
        fold(index & 31),
    )


def dot(a, b):
    return jnp.dot(a, b, preferred_element_type=F32)


def fetch(sources, targets, sems):
    copies = [pltpu.make_async_copy(s, t, sems.at[i]) for i, (s, t) in enumerate(zip(sources, targets))]
    for copy in copies:
        copy.start()
    return copies


def picked(spectrum, count, key, wanted, kx, store):
    half = NKX * 8
    hot = jnp.where(key[...] == wanted, jnp.float32(1), jnp.float32(0)).astype(BF)
    found = dot(spectrum[: 2 * count * half, :], hot)
    masks = [jnp.broadcast_to(kx == i, (8, wanted.shape[1])) for i in range(NKX - 1)]
    for s in range(count):
        parts = []
        for part in range(2):
            base = (2 * s + part) * half
            value = found[base : base + 8]
            for i in range(1, NKX - 1):
                value = jnp.where(masks[i], found[base + i * 8 : base + i * 8 + 8], value)
            parts.append(value)
        store(s, *parts)


def waves(pos, own, other, bands, wave_hi, wave_lo, along_hi, along_lo, ready, a_hi, a_lo, spectrum, first):
    zh, y, co = pos[0], pos[1], pos[2]
    count = len(bands)

    def product(q, carry):
        szh = (zh - q // 4) & 3
        sy = (y - q % 4) & 3
        start = pl.multiple_of(q * 16, 16)
        rows_of = [band[pl.ds(start, 16), :] for band in bands]
        for n in range(8):
            mine = own[sy, szh, n]
            theirs = other[sy, szh, n]
            lower = jnp.where(co == 0, mine, theirs)
            upper = jnp.where(co == 0, theirs, mine)
            for s in range(count):
                pair = [lower * rows_of[s][n : n + 1, :], upper * rows_of[s][8 + n : 9 + n, :]]
                high, low = split_bf16(jnp.concatenate(pair, axis=0))
                at = pl.ds(pl.multiple_of(s * 256 + start, 16), 16)
                a_hi[at, n * 128 : (n + 1) * 128] = high
                a_lo[at, n * 128 : (n + 1) * 128] = low
        return carry

    lax.fori_loop(0, 16, product, 0)
    ready()
    field = dot(a_hi[...], wave_hi[...]) + (dot(a_lo[...], wave_hi[...]) + dot(a_hi[...], wave_lo[...]))
    half = NKX * 8
    norm = jnp.float32(1.0) / jnp.sqrt(jnp.float32(GRID**3))
    for s in range(count):
        f_hi, f_lo = split_bf16(field[s * 256 : s * 256 + 256])
        full = dot(along_hi[...], f_hi) + (dot(along_lo[...], f_hi) + dot(along_hi[...], f_lo))
        real = full[:half, :DISC] + full[half:, DISC:]
        imag = full[:half, DISC:] - full[half:, :DISC]
        at = 2 * (first + s) * half
        spectrum[at : at + half, :] = (real * norm).astype(BF)
        spectrum[at + half : at + 2 * half, :] = (imag * norm).astype(BF)


def row_kernel(pos, *refs):
    sources, rows, spectrum, targets = refs[:9], refs[9], refs[10], refs[11:20]
    a_hi, a_lo, sems = refs[20:]
    own, other, band, wave_hi, wave_lo, along_hi, along_lo, key, gmap = targets
    copies = fetch(sources, targets, sems)
    for copy in copies[:3]:
        copy.wait()

    def ready():
        for copy in copies[3:]:
            copy.wait()

    waves(pos, own, other, [band], wave_hi, wave_lo, along_hi, along_lo, ready, a_hi, a_lo, spectrum, 0)

    def row_blocks(r, carry):
        kx, ky, kz = folded(gmap[r])
        flip = jnp.where((kz < 0) | ((kz == 0) & (ky < 0)), -1, 1)
        sign = flip.astype(F32)

        def store(s, real, imag):
            both = jnp.concatenate([real, imag * sign], axis=0).astype(BF)
            for t in range(4):
                rows[4 * r + t] = both[:, t * 256 : (t + 1) * 256]

        picked(spectrum, 1, key, flip * (ky * 64 + kz), flip * kx + 12, store)
        return carry

    lax.fori_loop(0, 8, row_blocks, 0)


def column_kernel(pos, *refs):
    sources, cols, targets = refs[:13], refs[13], refs[14:27]
    spectrum, a_hi, a_lo, sems = refs[27:]
    first, own, other, band1, band2, band3, wave_hi, wave_lo, along_hi, along_lo, key, col_key, col_kx = targets
    zl, x = pos[3], pos[4]
    copies = fetch(sources, targets, sems)
    for copy in copies[:6]:
        copy.wait()

    def ready():
        for copy in copies[6:]:
            copy.wait()

    spectrum[: 2 * NKX * 8, :] = first[...]
    bands = [band1, band2, band3]
    waves(pos, own, other, bands, wave_hi, wave_lo, along_hi, along_lo, ready, a_hi, a_lo, spectrum, 1)

    def columns(part, carry):
        j = (zl ^ part) * 4 + x

        def store(s, real, imag):
            cols[part, (x - s) & 3] = jnp.concatenate([real, imag], axis=0).astype(BF)

        picked(spectrum, 4, key, col_key[j], col_kx[j], store)
        return carry

    lax.fori_loop(0, 2, columns, 0)


def whole(shape):
    return pl.BlockSpec(shape, lambda *_: (0,) * len(shape), pipeline_mode=pl.Buffered(1))


def resident():
    return pl.BlockSpec(memory_space=pltpu.VMEM)


def transform_call(kernel, pos, operands, outs, scratch, flops, name):
    return pl.pallas_call(
        kernel,
        grid_spec=pltpu.PrefetchScalarGridSpec(
            num_scalar_prefetch=1,
            grid=(1,),
            in_specs=[pl.BlockSpec(memory_space=pl.ANY)] * len(operands),
            out_specs=[whole(v.shape) for v in outs],
            scratch_shapes=[pltpu.VMEM(v.shape, v.dtype) for v in operands]
            + scratch
            + [pltpu.SemaphoreType.DMA((len(operands),))],
        ),
        out_shape=outs,
        compiler_params=pltpu.CompilerParams(vmem_limit_bytes=60 << 20),
        cost_estimate=pl.CostEstimate(flops=flops, transcendentals=0, bytes_accessed=6 * 2**20),
        name=name,
    )(pos, *operands)


def row_pairs(pos, own, other, band, gmap):
    consts = [jnp.asarray(t) for t in tables()[:5]]
    outs = [jax.ShapeDtypeStruct((32, 16, 256), BF), jax.ShapeDtypeStruct((2 * NKX * 8, DISC), BF)]
    scratch = [pltpu.VMEM((256, 1024), BF)] * 2
    operands = [own, other, band, *consts, gmap.reshape(8, 1, 1024)]
    return transform_call(row_kernel, pos, operands, outs, scratch, 4 * 10**9, "row_pairs")


def column_pairs(pos, first, own, other, bands):
    consts = [jnp.asarray(t) for t in tables()[:7]]
    outs = [jax.ShapeDtypeStruct((2, 4, 16, CAN), BF)]
    scratch = [pltpu.VMEM((8 * NKX * 8, DISC), BF)] + [pltpu.VMEM((768, 1024), BF)] * 2
    operands = [first, own, other, *bands, *consts]
    return transform_call(column_kernel, pos, operands, outs, scratch, 8 * 10**9, "column_pairs")[0]


def prepare_kernel(pos, omega, r0, r1, r2, r3, gap, gmap, ident, scaled, hot, sign, row_k):
    zh, co, zl, x = pos[0], pos[2], pos[3], pos[4]

    @pl.when(pl.program_id(0) == 0)
    def _():
        kx, ky, kz = folded(gmap[0])
        flip = jnp.where((kz < 0) | ((kz == 0) & ((ky < 0) | ((ky == 0) & (kx < 0)))), -1, 1)
        wanted = (flip * ((kx * 64 + ky) * 64 + kz)).astype(F32)
        names = jnp.broadcast_to(ident[0].astype(F32), (128, CAN)).T
        for t in range(8):
            at = slice(t * 128, (t + 1) * 128)
            hot[:, at] = jnp.where(names == wanted[:, at], jnp.float32(1), jnp.float32(0)).astype(BF)
        sign[...] = jnp.concatenate([jnp.ones((8, 1024), F32), jnp.broadcast_to(flip.astype(F32), (8, 1024))], axis=0)

    for side in range(2):
        co_at = co if side == 0 else 1 - co
        energies = []
        for s in range(4):
            zh_at = (zh - s) & 3
            energies.append(gap[zh_at, 0, co_at])
            for sx, ref in enumerate((r0, r1, r2, r3)):
                for szl in range(2):
                    n = (zl ^ szl) * 4 + ((x - sx) & 3)
                    to = pl.multiple_of(side * 512 + s * 128 + n * 16, 16)
                    row_k[pl.ds(to, 16), :] = ref[szl, zh_at, 0, co_at]
        energy = jnp.concatenate(energies, axis=1)
        total = row_k[side * 512 : side * 512 + 512, :].astype(F32).T
        for w in range(6):
            weight = -2.0 * energy / (energy * energy + omega[w] * omega[w])
            weight = weight / jnp.sqrt(jnp.float32(2048))
            at = slice(side * 512, side * 512 + 512)
            scaled[pl.program_id(0), w * 256 : (w + 1) * 256, at] = (total * weight).astype(BF)


def prepare(pos, omega, rows, gap, gmap, ident):
    rows = [pltpu.with_memory_space_constraint(r, pltpu.HBM) for r in rows]
    gmap, ident = (pltpu.with_memory_space_constraint(v, pltpu.HBM) for v in (gmap.reshape(8, 1, 1024), ident))
    row_spec = pl.BlockSpec((2, 4, 1, 2, 16, 256), lambda s, pos, om: (0, 0, (pos[1] - s) & 3, 0, 0, 0))
    return pl.pallas_call(
        prepare_kernel,
        grid_spec=pltpu.PrefetchScalarGridSpec(
            num_scalar_prefetch=2,
            grid=(4,),
            in_specs=[row_spec] * 4
            + [
                pl.BlockSpec((4, 1, 2, 1, 128), lambda s, pos, om: (0, (pos[1] - s) & 3, 0, 0, 0)),
                pl.BlockSpec((1, 1, 1024), lambda s, pos, om: (pos[3] * 4 + pos[4], 0, 0)),
                pl.BlockSpec((1, 1, CAN), lambda s, pos, om: (pos[3] * 4 + pos[4], 0, 0)),
            ],
            out_specs=[resident(), resident(), resident()],
            scratch_shapes=[pltpu.VMEM((1024, 256), BF)],
        ),
        out_shape=[pltpu.VMEM((4, 1536, 1024), BF), pltpu.VMEM((CAN, 1024), BF), pltpu.VMEM((16, 1024), F32)],
        compiler_params=pltpu.CompilerParams(vmem_limit_bytes=20 << 20),
        cost_estimate=pl.CostEstimate(flops=10**9, transcendentals=0, bytes_accessed=20 * 2**20),
        name="scaled_rows",
    )(pos, omega, *rows, gap, gmap, ident)


def expand(mine, theirs, hot, sign, cols):
    for side, ref in enumerate((mine, theirs)):
        full = dot(ref[...].reshape(512, CAN), hot[...]).reshape(32, 16, 1024) * sign[...][None]
        full = full.reshape(512, 1024).astype(BF)
        for t in range(4):
            cols[t, side * 512 : side * 512 + 512, :] = full[:, t * 256 : (t + 1) * 256]


def product_step(sy, mine, theirs, scaled, hot, sign, total, last):
    def kernel(mine, theirs, scaled, hot, sign, *refs):
        out, cols = refs[-2:]
        add = None if total is None else refs[0]
        if last:
            n = pl.program_id(0)
            pl.when(n == 0)(lambda: expand(mine, theirs, hot, sign, cols))
            at = pl.ds(pl.multiple_of(n * 256, 256), 256)
            out[...] = add[:, :, at] + dot(scaled[sy], cols[n]).reshape(6, 256, 256)
        else:
            expand(mine, theirs, hot, sign, cols)
            for n in range(4):
                at = slice(n * 256, n * 256 + 256)
                part = dot(scaled[sy], cols[n]).reshape(6, 256, 256)
                out[:, :, at] = part if add is None else add[:, :, at] + part

    operands = [mine, theirs, scaled, hot, sign] + ([] if total is None else [total])
    aliases = {} if total is None or last else {5: 0}
    return pl.pallas_call(
        kernel,
        grid=(4 if last else 1,),
        in_specs=[resident()] * len(operands),
        out_specs=pl.BlockSpec((6, 256, 256), lambda n: (0, 0, n)) if last else resident(),
        scratch_shapes=[pltpu.VMEM((4, 1024, 256), BF)],
        out_shape=(jax.ShapeDtypeStruct if last else pltpu.VMEM)((6, 256, 1024), F32),
        input_output_aliases=aliases,
        compiler_params=pltpu.CompilerParams(vmem_limit_bytes=20 << 20),
        cost_estimate=pl.CostEstimate(flops=46 * 10**8, transcendentals=0, bytes_accessed=10 * 2**20),
        name="response_product",
    )(*operands)


def shifted(value, axis, shift):
    size = lax.axis_size(axis)
    return lax.ppermute(value, axis, [(i, (i + shift) % size) for i in range(size)])


def around(value, axis):
    return [value] + [shifted(value, axis, s) for s in range(1, lax.axis_size(axis))]


def neighbours(value, axis):
    return shifted(value, axis, 1), shifted(value, axis, 3)


def opposite(behind, ahead, axis):
    half = behind.shape[0] // 2
    return shifted(ahead[:half], axis, 3), shifted(behind[half:], axis, 1)


def body(valence, conduction, eps_val, eps_cond, omega, gmap):
    pos = jnp.stack([lax.axis_index(a) for a in AXES]).astype(jnp.int32)
    bands = around(conduction.reshape(256, 128), "x")
    own = lax.all_to_all(jnp.broadcast_to(valence, (8, *valence.shape)), NARROW, 0, 0, tiled=True)
    own, bands = lax.optimization_barrier((own, bands))
    own = jnp.stack(around(own, "zh"))
    gap = jnp.broadcast_to((eps_cond[:, None] - eps_val)[:, None, :], (256, 2, 8)).reshape(4, 4, 2, 1, 128)
    own, gap = lax.optimization_barrier((own, gap))
    own = jnp.stack(around(own, "y"))
    other = shifted(own, "co", 1)

    rows, spectrum = row_pairs(pos, own, other, bands[0], gmap)
    rows = lax.all_to_all(rows, WIDE, 0, 0, tiled=True)
    cols = column_pairs(pos, spectrum, own, other, bands[1:])
    kept, got = cols[0], shifted(cols[1], "zl", 1)
    lower = lax.axis_index("zl") == 0
    cols = jnp.concatenate([jnp.where(lower, kept, got), jnp.where(lower, got, kept)])
    rows = jnp.stack(around(rows, "zl")).reshape(2, 4, 4, 2, 16, 256)
    rows, cols = lax.optimization_barrier((rows, cols))
    behind, ahead = neighbours(rows, "x")
    rows = [rows, behind, jnp.concatenate(opposite(behind, ahead, "x")), ahead]

    behind, ahead = neighbours(cols, "zh")
    cols = jnp.stack([cols, behind, jnp.concatenate(opposite(behind, ahead, "zh")), ahead])
    behind, ahead = neighbours(cols, "y")
    scaled, hot, sign = prepare(pos, omega, rows, gap, gmap, jnp.asarray(tables()[-1]))
    scaled, hot, sign, behind, ahead = lax.optimization_barrier((scaled, hot, sign, behind, ahead))
    far = opposite(behind, ahead, "y")
    total = product_step(0, cols, shifted(cols, "co", 1), scaled, hot, sign, None, False)
    total, far = lax.optimization_barrier((total, far))
    for sy, mine in ((1, behind), (3, ahead), (2, jnp.concatenate(far))):
        theirs = shifted(mine, "co", 1)
        total = product_step(sy, mine, theirs, scaled, hot, sign, total, sy == 2)
    return total


def solution(mesh):
    torus = Mesh(mesh.devices.reshape(4, 4, 2, 2, 4), AXES)
    return jax.shard_map(
        body,
        mesh=torus,
        in_specs=(P(None, AXES), P(AXES, None), P(), P(), P(), P()),
        out_specs=P(None, WIDE, NARROW),
        check_vma=False,
    )
```

```python
import functools

import jax
import jax.numpy as jnp
import ml_dtypes
import numpy as np
from jax import lax
from jax.experimental import pallas as pl
from jax.experimental.pallas import tpu as pltpu
from jax.sharding import Mesh
from jax.sharding import PartitionSpec as P

GRID = 32
AXES = ("zh", "y", "co", "zl", "x")
WIDE = ("zh", "y", "co")
NARROW = ("zl", "x")
NPW = 8192
DISC = 256
NKX = 26
CAN = 640
BF = jnp.bfloat16
F32 = jnp.float32


def split_bf16(value):
    high = value.astype(BF)
    return high, (value - high.astype(value.dtype)).astype(BF)


def tables():
    k = np.arange(GRID)
    fold = np.where(k < GRID // 2, k, k - GRID)
    length = fold[:, None, None] ** 2 + fold[None, :, None] ** 2 + fold[None, None, :] ** 2
    ordered = np.sort(length.ravel())[:NPW]
    limit = ordered[-1]
    disc = []
    for ky in range(-15, 16):
        for kz in range(0, 16):
            if ky * ky + kz * kz <= limit and (kz > 0 or ky >= 0):
                disc.append((ky, kz))
    assert len(disc) <= DISC
    points = np.arange(GRID)
    wave = np.zeros((GRID, GRID, 2 * DISC))
    key = np.full((DISC, 1), -9000, np.int32)
    for m, (ky, kz) in enumerate(disc):
        angle = 2 * np.pi * ((ky * points[:, None] + kz * points[None, :]) % GRID) / GRID
        wave[:, :, m] = np.cos(angle)
        wave[:, :, DISC + m] = -np.sin(angle)
        key[m, 0] = ky * 64 + kz
    kx = np.arange(NKX) - 12
    assert limit < 13 * 13
    angle = 2 * np.pi * (kx[:, None] * points[None, :] % GRID) / GRID
    eye = np.eye(8)
    along = np.concatenate([np.kron(np.cos(angle), eye), np.kron(np.sin(angle), eye)])
    blocks = 8
    col_key = np.full((blocks, 1, CAN), -8000, np.int32)
    col_kx = np.zeros((blocks, 1, CAN), np.int32)
    col_id = np.full((blocks, 1, CAN), -(1 << 20), np.int32)
    size = NPW // blocks
    for j in range(blocks):
        low, high = ordered[j * size], ordered[(j + 1) * size - 1]
        n = 0
        for ky, kz in disc:
            for x in range(-12, 13):
                if (ky, kz) == (0, 0) and x < 0:
                    continue
                if low <= x * x + ky * ky + kz * kz <= high:
                    col_key[j, 0, n] = ky * 64 + kz
                    col_kx[j, 0, n] = x + 12
                    col_id[j, 0, n] = (x * 64 + ky) * 64 + kz
                    n += 1
        assert n <= CAN
    wave = wave.reshape(GRID * GRID, 2 * DISC).astype(np.float32)
    along = along.astype(np.float32)
    return split_np(wave) + split_np(along) + (key, col_key, col_kx, col_id)


def split_np(value):


    high = value.astype(ml_dtypes.bfloat16)
    low = (value - high.astype(np.float32)).astype(ml_dtypes.bfloat16)
    return high, low


def folded(index):
    def fold(k):
        return jnp.where(k < GRID // 2, k, k - GRID)

    return (
        fold(lax.shift_right_logical(index, 10)),
        fold(lax.shift_right_logical(index, 5) & 31),
        fold(index & 31),
    )


def dot(a, b):
    return jnp.dot(a, b, preferred_element_type=F32)


def fetch(sources, targets, sems):
    copies = [pltpu.make_async_copy(s, t, sems.at[i]) for i, (s, t) in enumerate(zip(sources, targets))]
    for copy in copies:
        copy.start()
    return copies


def picked(spectrum, count, key, wanted, kx, store):
    half = NKX * 8
    hot = jnp.where(key[...] == wanted, jnp.float32(1), jnp.float32(0)).astype(BF)
    found = dot(spectrum[: 2 * count * half, :], hot)
    masks = [jnp.broadcast_to(kx == i, (8, wanted.shape[1])) for i in range(NKX - 1)]
    for s in range(count):
        parts = []
        for part in range(2):
            base = (2 * s + part) * half
            value = found[base : base + 8]
            for i in range(1, NKX - 1):
                value = jnp.where(masks[i], found[base + i * 8 : base + i * 8 + 8], value)
            parts.append(value)
        store(s, *parts)


def waves(pos, own, other, bands, wave_hi, wave_lo, along_hi, along_lo, ready, a_hi, a_lo, spectrum, first):
    zh, y, co = pos[0], pos[1], pos[2]
    count = len(bands)

    def product(q, carry):
        szh = (zh - q // 4) & 3
        sy = (y - q % 4) & 3
        start = pl.multiple_of(q * 16, 16)
        rows_of = [band[pl.ds(start, 16), :] for band in bands]
        for n in range(8):
            mine = own[sy, szh, n]
            theirs = other[sy, szh, n]
            lower = jnp.where(co == 0, mine, theirs)
            upper = jnp.where(co == 0, theirs, mine)
            for s in range(count):
                pair = [lower * rows_of[s][n : n + 1, :], upper * rows_of[s][8 + n : 9 + n, :]]
                high, low = split_bf16(jnp.concatenate(pair, axis=0))
                at = pl.ds(pl.multiple_of(s * 256 + start, 16), 16)
                a_hi[at, n * 128 : (n + 1) * 128] = high
                a_lo[at, n * 128 : (n + 1) * 128] = low
        return carry

    lax.fori_loop(0, 16, product, 0)
    ready()
    field = dot(a_hi[...], wave_hi[...]) + (dot(a_lo[...], wave_hi[...]) + dot(a_hi[...], wave_lo[...]))
    half = NKX * 8
    norm = jnp.float32(1.0) / jnp.sqrt(jnp.float32(GRID**3))
    for s in range(count):
        f_hi, f_lo = split_bf16(field[s * 256 : s * 256 + 256])
        full = dot(along_hi[...], f_hi) + (dot(along_lo[...], f_hi) + dot(along_hi[...], f_lo))
        real = full[:half, :DISC] + full[half:, DISC:]
        imag = full[:half, DISC:] - full[half:, :DISC]
        at = 2 * (first + s) * half
        spectrum[at : at + half, :] = (real * norm).astype(BF)
        spectrum[at + half : at + 2 * half, :] = (imag * norm).astype(BF)


def row_kernel(pos, *refs):
    sources, rows, spectrum, targets = refs[:9], refs[9], refs[10], refs[11:20]
    a_hi, a_lo, sems = refs[20:]
    own, other, band, wave_hi, wave_lo, along_hi, along_lo, key, gmap = targets
    copies = fetch(sources, targets, sems)
    for copy in copies[:3]:
        copy.wait()

    def ready():
        for copy in copies[3:]:
            copy.wait()

    waves(pos, own, other, [band], wave_hi, wave_lo, along_hi, along_lo, ready, a_hi, a_lo, spectrum, 0)

    def row_blocks(r, carry):
        kx, ky, kz = folded(gmap[r])
        flip = jnp.where((kz < 0) | ((kz == 0) & (ky < 0)), -1, 1)
        sign = flip.astype(F32)

        def store(s, real, imag):
            both = jnp.concatenate([real, imag * sign], axis=0).astype(BF)
            for t in range(4):
                rows[4 * r + t] = both[:, t * 256 : (t + 1) * 256]

        picked(spectrum, 1, key, flip * (ky * 64 + kz), flip * kx + 12, store)
        return carry

    lax.fori_loop(0, 8, row_blocks, 0)


def column_kernel(pos, *refs):
    sources, cols, targets = refs[:13], refs[13], refs[14:27]
    spectrum, a_hi, a_lo, sems = refs[27:]
    first, own, other, band1, band2, band3, wave_hi, wave_lo, along_hi, along_lo, key, col_key, col_kx = targets
    zl, x = pos[3], pos[4]
    copies = fetch(sources, targets, sems)
    for copy in copies[:6]:
        copy.wait()

    def ready():
        for copy in copies[6:]:
            copy.wait()

    spectrum[: 2 * NKX * 8, :] = first[...]
    bands = [band1, band2, band3]
    waves(pos, own, other, bands, wave_hi, wave_lo, along_hi, along_lo, ready, a_hi, a_lo, spectrum, 1)

    def columns(part, carry):
        j = (zl ^ part) * 4 + x

        def store(s, real, imag):
            cols[part, (x - s) & 3] = jnp.concatenate([real, imag], axis=0).astype(BF)

        picked(spectrum, 4, key, col_key[j], col_kx[j], store)
        return carry

    lax.fori_loop(0, 2, columns, 0)


def whole(shape):
    return pl.BlockSpec(shape, lambda *_: (0,) * len(shape), pipeline_mode=pl.Buffered(1))


def resident():
    return pl.BlockSpec(memory_space=pltpu.VMEM)


def transform_call(kernel, pos, operands, outs, scratch, flops, name):
    return pl.pallas_call(
        kernel,
        grid_spec=pltpu.PrefetchScalarGridSpec(
            num_scalar_prefetch=1,
            grid=(1,),
            in_specs=[pl.BlockSpec(memory_space=pl.ANY)] * len(operands),
            out_specs=[whole(v.shape) for v in outs],
            scratch_shapes=[pltpu.VMEM(v.shape, v.dtype) for v in operands]
            + scratch
            + [pltpu.SemaphoreType.DMA((len(operands),))],
        ),
        out_shape=outs,
        compiler_params=pltpu.CompilerParams(vmem_limit_bytes=60 << 20),
        cost_estimate=pl.CostEstimate(flops=flops, transcendentals=0, bytes_accessed=6 * 2**20),
        name=name,
    )(pos, *operands)


def row_pairs(pos, own, other, band, gmap):
    consts = [jnp.asarray(t) for t in tables()[:5]]
    outs = [jax.ShapeDtypeStruct((32, 16, 256), BF), jax.ShapeDtypeStruct((2 * NKX * 8, DISC), BF)]
    scratch = [pltpu.VMEM((256, 1024), BF)] * 2
    operands = [own, other, band, *consts, gmap.reshape(8, 1, 1024)]
    return transform_call(row_kernel, pos, operands, outs, scratch, 4 * 10**9, "row_pairs")


def column_pairs(pos, first, own, other, bands):
    consts = [jnp.asarray(t) for t in tables()[:7]]
    outs = [jax.ShapeDtypeStruct((2, 4, 16, CAN), BF)]
    scratch = [pltpu.VMEM((8 * NKX * 8, DISC), BF)] + [pltpu.VMEM((768, 1024), BF)] * 2
    operands = [first, own, other, *bands, *consts]
    return transform_call(column_kernel, pos, operands, outs, scratch, 8 * 10**9, "column_pairs")[0]


def prepare_kernel(pos, omega, r0, r1, r2, r3, gap, gmap, ident, scaled, hot, sign, row_k):
    zh, co, zl, x = pos[0], pos[2], pos[3], pos[4]

    @pl.when(pl.program_id(0) == 0)
    def _():
        kx, ky, kz = folded(gmap[0])
        flip = jnp.where((kz < 0) | ((kz == 0) & ((ky < 0) | ((ky == 0) & (kx < 0)))), -1, 1)
        wanted = (flip * ((kx * 64 + ky) * 64 + kz)).astype(F32)
        names = jnp.broadcast_to(ident[0].astype(F32), (128, CAN)).T
        signs = jnp.concatenate([jnp.ones((8, 1024), F32), jnp.broadcast_to(flip.astype(F32), (8, 1024))], axis=0)
        for t in range(8):
            at = slice(t * 128, (t + 1) * 128)
            here = slice(t % 2 * 128, t % 2 * 128 + 128)
            hot[t // 2, :, here] = jnp.where(names == wanted[:, at], jnp.float32(1), jnp.float32(0)).astype(BF)
            sign[t // 2, :, here] = signs[:, at]

    for side in range(2):
        co_at = co if side == 0 else 1 - co
        energies = []
        for s in range(4):
            zh_at = (zh - s) & 3
            energies.append(gap[zh_at, 0, co_at])
            for sx, ref in enumerate((r0, r1, r2, r3)):
                for szl in range(2):
                    n = (zl ^ szl) * 4 + ((x - sx) & 3)
                    to = pl.multiple_of(side * 512 + s * 128 + n * 16, 16)
                    row_k[pl.ds(to, 16), :] = ref[szl, zh_at, 0, co_at]
        energy = jnp.concatenate(energies, axis=1)
        total = row_k[side * 512 : side * 512 + 512, :].astype(F32).T
        for w in range(6):
            weight = -2.0 * energy / (energy * energy + omega[w] * omega[w])
            weight = weight / jnp.sqrt(jnp.float32(2048))
            at = slice(side * 512, side * 512 + 512)
            scaled[pl.program_id(0), w * 256 : (w + 1) * 256, at] = (total * weight).astype(BF)


def prepare(pos, omega, rows, gap, gmap, ident):
    rows = [pltpu.with_memory_space_constraint(r, pltpu.HBM) for r in rows]
    gmap, ident = (pltpu.with_memory_space_constraint(v, pltpu.HBM) for v in (gmap.reshape(8, 1, 1024), ident))
    row_spec = pl.BlockSpec((2, 4, 1, 2, 16, 256), lambda s, pos, om: (0, 0, (pos[1] - s) & 3, 0, 0, 0))
    return pl.pallas_call(
        prepare_kernel,
        grid_spec=pltpu.PrefetchScalarGridSpec(
            num_scalar_prefetch=2,
            grid=(4,),
            in_specs=[row_spec] * 4
            + [
                pl.BlockSpec((4, 1, 2, 1, 128), lambda s, pos, om: (0, (pos[1] - s) & 3, 0, 0, 0)),
                pl.BlockSpec((1, 1, 1024), lambda s, pos, om: (pos[3] * 4 + pos[4], 0, 0)),
                pl.BlockSpec((1, 1, CAN), lambda s, pos, om: (pos[3] * 4 + pos[4], 0, 0)),
            ],
            out_specs=[resident(), resident(), resident()],
            scratch_shapes=[pltpu.VMEM((1024, 256), BF)],
        ),
        out_shape=[pltpu.VMEM((4, 1536, 1024), BF), pltpu.VMEM((4, CAN, 256), BF), pltpu.VMEM((4, 16, 256), F32)],
        compiler_params=pltpu.CompilerParams(vmem_limit_bytes=20 << 20),
        cost_estimate=pl.CostEstimate(flops=10**9, transcendentals=0, bytes_accessed=20 * 2**20),
        name="scaled_rows",
    )(pos, omega, *rows, gap, gmap, ident)


def product_step(sy, mine, theirs, scaled, hot, sign, total, last):
    def kernel(mine, theirs, scaled, hot, sign, *refs):
        out, cols = refs[-2:]
        add = None if total is None else refs[0]

        def quarter(n):
            for side, ref in enumerate((mine, theirs)):
                full = dot(ref[...].reshape(512, CAN), hot[n]).reshape(32, 16, 256) * sign[n][None]
                cols[n, side * 512 : side * 512 + 512, :] = full.reshape(512, 256).astype(BF)
            part = dot(scaled[sy], cols[n]).reshape(6, 256, 256)
            at = pl.ds(pl.multiple_of(n * 256, 256), 256)
            part = part if add is None else add[:, :, at] + part
            if last:
                out[...] = part
            else:
                out[:, :, at] = part

        if last:
            quarter(pl.program_id(0))
        else:
            pl.loop(0, 4)(quarter)

    operands = [mine, theirs, scaled, hot, sign] + ([] if total is None else [total])
    aliases = {} if total is None or last else {5: 0}
    return pl.pallas_call(
        kernel,
        grid=(4 if last else 1,),
        in_specs=[resident()] * len(operands),
        out_specs=pl.BlockSpec((6, 256, 256), lambda n: (0, 0, n)) if last else resident(),
        scratch_shapes=[pltpu.VMEM((4, 1024, 256), BF)],
        out_shape=(jax.ShapeDtypeStruct if last else pltpu.VMEM)((6, 256, 1024), F32),
        input_output_aliases=aliases,
        compiler_params=pltpu.CompilerParams(vmem_limit_bytes=20 << 20),
        cost_estimate=pl.CostEstimate(flops=46 * 10**8, transcendentals=0, bytes_accessed=10 * 2**20),
        name="response_product",
    )(*operands)


def shifted(value, axis, shift):
    size = lax.axis_size(axis)
    return lax.ppermute(value, axis, [(i, (i + shift) % size) for i in range(size)])


def around(value, axis):
    return [value] + [shifted(value, axis, s) for s in range(1, lax.axis_size(axis))]


def neighbours(value, axis):
    return shifted(value, axis, 1), shifted(value, axis, 3)


def opposite(behind, ahead, axis):
    half = behind.shape[0] // 2
    return shifted(ahead[:half], axis, 3), shifted(behind[half:], axis, 1)


def body(valence, conduction, eps_val, eps_cond, omega, gmap):
    pos = jnp.stack([lax.axis_index(a) for a in AXES]).astype(jnp.int32)
    bands = around(conduction.reshape(256, 128), "x")
    own = lax.all_to_all(jnp.broadcast_to(valence, (8, *valence.shape)), NARROW, 0, 0, tiled=True)
    own, bands = lax.optimization_barrier((own, bands))
    own = jnp.stack(around(own, "zh"))
    gap = jnp.broadcast_to((eps_cond[:, None] - eps_val)[:, None, :], (256, 2, 8)).reshape(4, 4, 2, 1, 128)
    own, gap = lax.optimization_barrier((own, gap))
    own = jnp.stack(around(own, "y"))
    other = shifted(own, "co", 1)

    rows, spectrum = row_pairs(pos, own, other, bands[0], gmap)
    rows = lax.all_to_all(rows, WIDE, 0, 0, tiled=True)
    cols = column_pairs(pos, spectrum, own, other, bands[1:])
    kept, got = cols[0], shifted(cols[1], "zl", 1)
    lower = lax.axis_index("zl") == 0
    cols = jnp.concatenate([jnp.where(lower, kept, got), jnp.where(lower, got, kept)])
    rows = jnp.stack(around(rows, "zl")).reshape(2, 4, 4, 2, 16, 256)
    rows, cols = lax.optimization_barrier((rows, cols))
    near_x = neighbours(rows, "x")
    near_zh = neighbours(cols, "zh")
    near_x, near_zh = lax.optimization_barrier((near_x, near_zh))
    rows = [rows, near_x[0], jnp.concatenate(opposite(*near_x, "x")), near_x[1]]
    cols = jnp.stack([cols, near_zh[0], jnp.concatenate(opposite(*near_zh, "zh")), near_zh[1]])
    near_y = neighbours(cols, "y")
    scaled, hot, sign = prepare(pos, omega, rows, gap, gmap, jnp.asarray(tables()[-1]))
    total = product_step(0, cols, shifted(cols, "co", 1), scaled, hot, sign, None, False)
    total, near_y = lax.optimization_barrier((total, near_y))
    far = opposite(*near_y, "y")
    total = product_step(1, near_y[0], shifted(near_y[0], "co", 1), scaled, hot, sign, total, False)
    total, far = lax.optimization_barrier((total, far))
    for sy, mine in ((3, near_y[1]), (2, jnp.concatenate(far))):
        theirs = shifted(mine, "co", 1)
        total = product_step(sy, mine, theirs, scaled, hot, sign, total, sy == 2)
    return total


def solution(mesh):
    torus = Mesh(mesh.devices.reshape(4, 4, 2, 2, 4), AXES)
    return jax.shard_map(
        body,
        mesh=torus,
        in_specs=(P(None, AXES), P(AXES, None), P(), P(), P(), P()),
        out_specs=P(None, WIDE, NARROW),
        check_vma=False,
    )
```

```python
import functools

import jax
import jax.numpy as jnp
import ml_dtypes
import numpy as np
from jax import lax
from jax.experimental import pallas as pl
from jax.experimental.pallas import tpu as pltpu
from jax.sharding import Mesh
from jax.sharding import PartitionSpec as P

GRID = 32
AXES = ("zh", "y", "co", "zl", "x")
WIDE = ("zh", "y", "co")
NARROW = ("zl", "x")
NPW = 8192
DISC = 256
NKX = 26
CAN = 640
BF = jnp.bfloat16
F32 = jnp.float32


def split_bf16(value):
    high = value.astype(BF)
    return high, (value - high.astype(value.dtype)).astype(BF)


def tables():
    k = np.arange(GRID)
    fold = np.where(k < GRID // 2, k, k - GRID)
    length = fold[:, None, None] ** 2 + fold[None, :, None] ** 2 + fold[None, None, :] ** 2
    ordered = np.sort(length.ravel())[:NPW]
    limit = ordered[-1]
    disc = []
    for ky in range(-15, 16):
        for kz in range(0, 16):
            if ky * ky + kz * kz <= limit and (kz > 0 or ky >= 0):
                disc.append((ky, kz))
    assert len(disc) <= DISC
    points = np.arange(GRID)
    wave = np.zeros((GRID, GRID, 2 * DISC))
    key = np.full((DISC, 1), -9000, np.int32)
    for m, (ky, kz) in enumerate(disc):
        angle = 2 * np.pi * ((ky * points[:, None] + kz * points[None, :]) % GRID) / GRID
        wave[:, :, m] = np.cos(angle)
        wave[:, :, DISC + m] = -np.sin(angle)
        key[m, 0] = ky * 64 + kz
    kx = np.arange(NKX) - 12
    assert limit < 13 * 13
    angle = 2 * np.pi * (kx[:, None] * points[None, :] % GRID) / GRID
    eye = np.eye(8)
    along = np.concatenate([np.kron(np.cos(angle), eye), np.kron(np.sin(angle), eye)])
    blocks = 8
    col_key = np.full((blocks, 1, CAN), -8000, np.int32)
    col_kx = np.zeros((blocks, 1, CAN), np.int32)
    col_id = np.full((blocks, 1, CAN), -(1 << 20), np.int32)
    size = NPW // blocks
    for j in range(blocks):
        low, high = ordered[j * size], ordered[(j + 1) * size - 1]
        n = 0
        for ky, kz in disc:
            for x in range(-12, 13):
                if (ky, kz) == (0, 0) and x < 0:
                    continue
                if low <= x * x + ky * ky + kz * kz <= high:
                    col_key[j, 0, n] = ky * 64 + kz
                    col_kx[j, 0, n] = x + 12
                    col_id[j, 0, n] = (x * 64 + ky) * 64 + kz
                    n += 1
        assert n <= CAN
    wave = wave.reshape(GRID * GRID, 2 * DISC).astype(np.float32)
    along = along.astype(np.float32)
    return split_np(wave) + split_np(along) + (key, col_key, col_kx, col_id)


def split_np(value):


    high = value.astype(ml_dtypes.bfloat16)
    low = (value - high.astype(np.float32)).astype(ml_dtypes.bfloat16)
    return high, low


def folded(index):
    def fold(k):
        return jnp.where(k < GRID // 2, k, k - GRID)

    return (
        fold(lax.shift_right_logical(index, 10)),
        fold(lax.shift_right_logical(index, 5) & 31),
        fold(index & 31),
    )


def dot(a, b):
    return jnp.dot(a, b, preferred_element_type=F32)


def fetch(sources, targets, sems):
    copies = [pltpu.make_async_copy(s, t, sems.at[i]) for i, (s, t) in enumerate(zip(sources, targets))]
    for copy in copies:
        copy.start()
    return copies


def picked(spectrum, count, key, wanted, kx, store):
    half = NKX * 8
    hot = jnp.where(key[...] == wanted, jnp.float32(1), jnp.float32(0)).astype(BF)
    found = dot(spectrum[: 2 * count * half, :], hot)
    masks = [jnp.broadcast_to(kx == i, (8, wanted.shape[1])) for i in range(NKX - 1)]
    for s in range(count):
        parts = []
        for part in range(2):
            base = (2 * s + part) * half
            value = found[base : base + 8]
            for i in range(1, NKX - 1):
                value = jnp.where(masks[i], found[base + i * 8 : base + i * 8 + 8], value)
            parts.append(value)
        store(s, *parts)


def waves(pos, own, other, bands, wave_hi, wave_lo, along_hi, along_lo, ready, a_hi, a_lo, spectrum, first):
    zh, y, co = pos[0], pos[1], pos[2]
    count = len(bands)

    def product(q, carry):
        szh = (zh - q // 4) & 3
        sy = (y - q % 4) & 3
        start = pl.multiple_of(q * 16, 16)
        rows_of = [band[pl.ds(start, 16), :] for band in bands]
        for n in range(8):
            mine = own[sy, szh, n]
            theirs = other[sy, szh, n]
            lower = jnp.where(co == 0, mine, theirs)
            upper = jnp.where(co == 0, theirs, mine)
            for s in range(count):
                pair = [lower * rows_of[s][n : n + 1, :], upper * rows_of[s][8 + n : 9 + n, :]]
                high, low = split_bf16(jnp.concatenate(pair, axis=0))
                at = pl.ds(pl.multiple_of(s * 256 + start, 16), 16)
                a_hi[at, n * 128 : (n + 1) * 128] = high
                a_lo[at, n * 128 : (n + 1) * 128] = low
        return carry

    lax.fori_loop(0, 16, product, 0)
    ready()
    field = dot(a_hi[...], wave_hi[...]) + (dot(a_lo[...], wave_hi[...]) + dot(a_hi[...], wave_lo[...]))
    half = NKX * 8
    norm = jnp.float32(1.0) / jnp.sqrt(jnp.float32(GRID**3))
    for s in range(count):
        f_hi, f_lo = split_bf16(field[s * 256 : s * 256 + 256])
        full = dot(along_hi[...], f_hi) + (dot(along_lo[...], f_hi) + dot(along_hi[...], f_lo))
        real = full[:half, :DISC] + full[half:, DISC:]
        imag = full[:half, DISC:] - full[half:, :DISC]
        at = 2 * (first + s) * half
        spectrum[at : at + half, :] = (real * norm).astype(BF)
        spectrum[at + half : at + 2 * half, :] = (imag * norm).astype(BF)


def row_kernel(pos, *refs):
    sources, rows, spectrum, targets = refs[:9], refs[9], refs[10], refs[11:20]
    a_hi, a_lo, sems = refs[20:]
    own, other, band, wave_hi, wave_lo, along_hi, along_lo, key, gmap = targets
    copies = fetch(sources, targets, sems)
    for copy in copies[:3]:
        copy.wait()

    def ready():
        for copy in copies[3:]:
            copy.wait()

    waves(pos, own, other, [band], wave_hi, wave_lo, along_hi, along_lo, ready, a_hi, a_lo, spectrum, 0)

    def row_blocks(r, carry):
        kx, ky, kz = folded(gmap[r])
        flip = jnp.where((kz < 0) | ((kz == 0) & (ky < 0)), -1, 1)
        sign = flip.astype(F32)

        def store(s, real, imag):
            both = jnp.concatenate([real, imag * sign], axis=0).astype(BF)
            for t in range(4):
                rows[4 * r + t] = both[:, t * 256 : (t + 1) * 256]

        picked(spectrum, 1, key, flip * (ky * 64 + kz), flip * kx + 12, store)
        return carry

    lax.fori_loop(0, 8, row_blocks, 0)


def column_kernel(pos, *refs):
    sources, cols, targets = refs[:13], refs[13], refs[14:27]
    spectrum, a_hi, a_lo, sems = refs[27:]
    first, own, other, band1, band2, band3, wave_hi, wave_lo, along_hi, along_lo, key, col_key, col_kx = targets
    zl, x = pos[3], pos[4]
    copies = fetch(sources, targets, sems)
    for copy in copies[:6]:
        copy.wait()

    def ready():
        for copy in copies[6:]:
            copy.wait()

    spectrum[: 2 * NKX * 8, :] = first[...]
    bands = [band1, band2, band3]
    waves(pos, own, other, bands, wave_hi, wave_lo, along_hi, along_lo, ready, a_hi, a_lo, spectrum, 1)

    def columns(part, carry):
        j = (zl ^ part) * 4 + x

        def store(s, real, imag):
            cols[part, (x - s) & 3] = jnp.concatenate([real, imag], axis=0).astype(BF)

        picked(spectrum, 4, key, col_key[j], col_kx[j], store)
        return carry

    lax.fori_loop(0, 2, columns, 0)


def whole(shape):
    return pl.BlockSpec(shape, lambda *_: (0,) * len(shape), pipeline_mode=pl.Buffered(1))


def resident():
    return pl.BlockSpec(memory_space=pltpu.VMEM)


def transform_call(kernel, pos, operands, outs, scratch, flops, name):
    return pl.pallas_call(
        kernel,
        grid_spec=pltpu.PrefetchScalarGridSpec(
            num_scalar_prefetch=1,
            grid=(1,),
            in_specs=[pl.BlockSpec(memory_space=pl.ANY)] * len(operands),
            out_specs=[whole(v.shape) for v in outs],
            scratch_shapes=[pltpu.VMEM(v.shape, v.dtype) for v in operands]
            + scratch
            + [pltpu.SemaphoreType.DMA((len(operands),))],
        ),
        out_shape=outs,
        compiler_params=pltpu.CompilerParams(vmem_limit_bytes=60 << 20),
        cost_estimate=pl.CostEstimate(flops=flops, transcendentals=0, bytes_accessed=6 * 2**20),
        name=name,
    )(pos, *operands)


def row_pairs(pos, own, other, band, gmap):
    consts = [jnp.asarray(t) for t in tables()[:5]]
    outs = [jax.ShapeDtypeStruct((32, 16, 256), BF), jax.ShapeDtypeStruct((2 * NKX * 8, DISC), BF)]
    scratch = [pltpu.VMEM((256, 1024), BF)] * 2
    operands = [own, other, band, *consts, gmap.reshape(8, 1, 1024)]
    return transform_call(row_kernel, pos, operands, outs, scratch, 4 * 10**9, "row_pairs")


def column_pairs(pos, first, own, other, bands):
    consts = [jnp.asarray(t) for t in tables()[:7]]
    outs = [jax.ShapeDtypeStruct((2, 4, 16, CAN), BF)]
    scratch = [pltpu.VMEM((8 * NKX * 8, DISC), BF)] + [pltpu.VMEM((768, 1024), BF)] * 2
    operands = [first, own, other, *bands, *consts]
    return transform_call(column_kernel, pos, operands, outs, scratch, 8 * 10**9, "column_pairs")[0]


def prepare_kernel(pos, omega, r0, r1, r2, r3, gap, gmap, ident, scaled, hot, sign, row_k):
    zh, co, zl, x = pos[0], pos[2], pos[3], pos[4]

    @pl.when(pl.program_id(0) == 0)
    def _():
        kx, ky, kz = folded(gmap[0])
        flip = jnp.where((kz < 0) | ((kz == 0) & ((ky < 0) | ((ky == 0) & (kx < 0)))), -1, 1)
        wanted = (flip * ((kx * 64 + ky) * 64 + kz)).astype(F32)
        names = jnp.broadcast_to(ident[0].astype(F32), (128, CAN)).T
        signs = jnp.concatenate([jnp.ones((8, 1024), F32), jnp.broadcast_to(flip.astype(F32), (8, 1024))], axis=0)
        for t in range(8):
            at = slice(t * 128, (t + 1) * 128)
            here = slice(t % 2 * 128, t % 2 * 128 + 128)
            hot[t // 2, :, here] = jnp.where(names == wanted[:, at], jnp.float32(1), jnp.float32(0)).astype(BF)
            sign[t // 2, :, here] = signs[:, at]

    for side in range(2):
        co_at = co if side == 0 else 1 - co
        energies = []
        for s in range(4):
            zh_at = (zh - s) & 3
            energies.append(gap[zh_at, 0, co_at])
            for sx, ref in enumerate((r0, r1, r2, r3)):
                for szl in range(2):
                    n = (zl ^ szl) * 4 + ((x - sx) & 3)
                    to = pl.multiple_of(side * 512 + s * 128 + n * 16, 16)
                    row_k[pl.ds(to, 16), :] = ref[szl, zh_at, 0, co_at]
        energy = jnp.concatenate(energies, axis=1)
        total = row_k[side * 512 : side * 512 + 512, :].astype(F32).T
        for w in range(6):
            weight = -2.0 * energy / (energy * energy + omega[w] * omega[w])
            weight = weight / jnp.sqrt(jnp.float32(2048))
            at = slice(side * 512, side * 512 + 512)
            scaled[pl.program_id(0), w * 256 : (w + 1) * 256, at] = (total * weight).astype(BF)


def prepare(pos, omega, rows, gap, gmap, ident):
    rows = [pltpu.with_memory_space_constraint(r, pltpu.HBM) for r in rows]
    gmap, ident = (pltpu.with_memory_space_constraint(v, pltpu.HBM) for v in (gmap.reshape(8, 1, 1024), ident))
    row_spec = pl.BlockSpec((2, 4, 1, 2, 16, 256), lambda s, pos, om: (0, 0, (pos[1] - s) & 3, 0, 0, 0))
    return pl.pallas_call(
        prepare_kernel,
        grid_spec=pltpu.PrefetchScalarGridSpec(
            num_scalar_prefetch=2,
            grid=(4,),
            in_specs=[row_spec] * 4
            + [
                pl.BlockSpec((4, 1, 2, 1, 128), lambda s, pos, om: (0, (pos[1] - s) & 3, 0, 0, 0)),
                pl.BlockSpec((1, 1, 1024), lambda s, pos, om: (pos[3] * 4 + pos[4], 0, 0)),
                pl.BlockSpec((1, 1, CAN), lambda s, pos, om: (pos[3] * 4 + pos[4], 0, 0)),
            ],
            out_specs=[resident(), resident(), resident()],
            scratch_shapes=[pltpu.VMEM((1024, 256), BF)],
        ),
        out_shape=[pltpu.VMEM((4, 1536, 1024), BF), pltpu.VMEM((4, CAN, 256), BF), pltpu.VMEM((4, 16, 256), F32)],
        compiler_params=pltpu.CompilerParams(vmem_limit_bytes=20 << 20),
        cost_estimate=pl.CostEstimate(flops=10**9, transcendentals=0, bytes_accessed=20 * 2**20),
        name="scaled_rows",
    )(pos, omega, *rows, gap, gmap, ident)


def product_step(sy, mine, theirs, scaled, hot, sign, total, last):
    def kernel(mine, theirs, scaled, hot, sign, *refs):
        out, cols = refs[-2:]
        add = None if total is None else refs[0]

        def quarter(n):
            for side, ref in enumerate((mine, theirs)):
                full = dot(ref[...].reshape(512, CAN), hot[n]).reshape(32, 16, 256) * sign[n][None]
                cols[n, side * 512 : side * 512 + 512, :] = full.reshape(512, 256).astype(BF)
            part = dot(scaled[sy], cols[n]).reshape(6, 256, 256)
            at = pl.ds(pl.multiple_of(n * 256, 256), 256)
            part = part if add is None else add[:, :, at] + part
            if last:
                out[...] = part
            else:
                out[:, :, at] = part

        if last:
            quarter(pl.program_id(0))
        else:
            pl.loop(0, 4, unroll=2)(quarter)

    operands = [mine, theirs, scaled, hot, sign] + ([] if total is None else [total])
    aliases = {} if total is None or last else {5: 0}
    return pl.pallas_call(
        kernel,
        grid=(4 if last else 1,),
        in_specs=[resident()] * len(operands),
        out_specs=pl.BlockSpec((6, 256, 256), lambda n: (0, 0, n)) if last else resident(),
        scratch_shapes=[pltpu.VMEM((4, 1024, 256), BF)],
        out_shape=(jax.ShapeDtypeStruct if last else pltpu.VMEM)((6, 256, 1024), F32),
        input_output_aliases=aliases,
        compiler_params=pltpu.CompilerParams(vmem_limit_bytes=20 << 20),
        cost_estimate=pl.CostEstimate(flops=46 * 10**8, transcendentals=0, bytes_accessed=10 * 2**20),
        name="response_product",
    )(*operands)


def shifted(value, axis, shift):
    size = lax.axis_size(axis)
    return lax.ppermute(value, axis, [(i, (i + shift) % size) for i in range(size)])


def around(value, axis):
    return [value] + [shifted(value, axis, s) for s in range(1, lax.axis_size(axis))]


def neighbours(value, axis):
    return shifted(value, axis, 1), shifted(value, axis, 3)


def opposite(behind, ahead, axis):
    half = behind.shape[0] // 2
    return shifted(ahead[:half], axis, 3), shifted(behind[half:], axis, 1)


def body(valence, conduction, eps_val, eps_cond, omega, gmap):
    pos = jnp.stack([lax.axis_index(a) for a in AXES]).astype(jnp.int32)
    bands = around(conduction.reshape(256, 128), "x")
    own = lax.all_to_all(jnp.broadcast_to(valence, (8, *valence.shape)), NARROW, 0, 0, tiled=True)
    own, bands = lax.optimization_barrier((own, bands))
    own = jnp.stack(around(own, "zh"))
    gap = jnp.broadcast_to((eps_cond[:, None] - eps_val)[:, None, :], (256, 2, 8)).reshape(4, 4, 2, 1, 128)
    own, gap = lax.optimization_barrier((own, gap))
    own = jnp.stack(around(own, "y"))
    other = shifted(own, "co", 1)

    rows, spectrum = row_pairs(pos, own, other, bands[0], gmap)
    rows = lax.all_to_all(rows, WIDE, 0, 0, tiled=True)
    cols = column_pairs(pos, spectrum, own, other, bands[1:])
    kept, got = cols[0], shifted(cols[1], "zl", 1)
    lower = lax.axis_index("zl") == 0
    cols = jnp.concatenate([jnp.where(lower, kept, got), jnp.where(lower, got, kept)])
    rows = jnp.stack(around(rows, "zl")).reshape(2, 4, 4, 2, 16, 256)
    rows, cols = lax.optimization_barrier((rows, cols))
    near_x = neighbours(rows, "x")
    near_zh = neighbours(cols, "zh")
    near_x, near_zh = lax.optimization_barrier((near_x, near_zh))
    far_x, far_zh = lax.optimization_barrier((opposite(*near_x, "x"), opposite(*near_zh, "zh")))
    rows = [rows, near_x[0], jnp.concatenate(far_x), near_x[1]]
    cols = jnp.stack([cols, near_zh[0], jnp.concatenate(far_zh), near_zh[1]])
    near_y = neighbours(cols, "y")
    scaled, hot, sign = prepare(pos, omega, rows, gap, gmap, jnp.asarray(tables()[-1]))
    total = product_step(0, cols, shifted(cols, "co", 1), scaled, hot, sign, None, False)
    total, near_y = lax.optimization_barrier((total, near_y))
    far = opposite(*near_y, "y")
    total = product_step(1, near_y[0], shifted(near_y[0], "co", 1), scaled, hot, sign, total, False)
    total, far = lax.optimization_barrier((total, far))
    for sy, mine in ((3, near_y[1]), (2, jnp.concatenate(far))):
        theirs = shifted(mine, "co", 1)
        total = product_step(sy, mine, theirs, scaled, hot, sign, total, sy == 2)
    return total


def solution(mesh):
    torus = Mesh(mesh.devices.reshape(4, 4, 2, 2, 4), AXES)
    return jax.shard_map(
        body,
        mesh=torus,
        in_specs=(P(None, AXES), P(AXES, None), P(), P(), P(), P()),
        out_specs=P(None, WIDE, NARROW),
        check_vma=False,
    )
```

```python
import functools

import jax
import jax.numpy as jnp
import ml_dtypes
import numpy as np
from jax import lax
from jax.experimental import pallas as pl
from jax.experimental.pallas import tpu as pltpu
from jax.sharding import Mesh
from jax.sharding import PartitionSpec as P

GRID = 32
AXES = ("zh", "y", "co", "zl", "x")
WIDE = ("zh", "y", "co")
NARROW = ("zl", "x")
NPW = 8192
DISC = 256
NKX = 26
CAN = 640
BF = jnp.bfloat16
F32 = jnp.float32


def split_bf16(value):
    high = value.astype(BF)
    return high, (value - high.astype(value.dtype)).astype(BF)


def tables():
    k = np.arange(GRID)
    fold = np.where(k < GRID // 2, k, k - GRID)
    length = fold[:, None, None] ** 2 + fold[None, :, None] ** 2 + fold[None, None, :] ** 2
    ordered = np.sort(length.ravel())[:NPW]
    limit = ordered[-1]
    disc = []
    for ky in range(-15, 16):
        for kz in range(0, 16):
            if ky * ky + kz * kz <= limit and (kz > 0 or ky >= 0):
                disc.append((ky, kz))
    assert len(disc) <= DISC
    points = np.arange(GRID)
    wave = np.zeros((GRID, GRID, 2 * DISC))
    key = np.full((DISC, 1), -9000, np.int32)
    for m, (ky, kz) in enumerate(disc):
        angle = 2 * np.pi * ((ky * points[:, None] + kz * points[None, :]) % GRID) / GRID
        wave[:, :, m] = np.cos(angle)
        wave[:, :, DISC + m] = -np.sin(angle)
        key[m, 0] = ky * 64 + kz
    kx = np.arange(NKX) - 12
    assert limit < 13 * 13
    angle = 2 * np.pi * (kx[:, None] * points[None, :] % GRID) / GRID
    eye = np.eye(8)
    along = np.concatenate([np.kron(np.cos(angle), eye), np.kron(np.sin(angle), eye)])
    blocks = 8
    col_key = np.full((blocks, 1, CAN), -8000, np.int32)
    col_kx = np.zeros((blocks, 1, CAN), np.int32)
    col_id = np.full((blocks, 1, CAN), -(1 << 20), np.int32)
    size = NPW // blocks
    for j in range(blocks):
        low, high = ordered[j * size], ordered[(j + 1) * size - 1]
        n = 0
        for ky, kz in disc:
            for x in range(-12, 13):
                if (ky, kz) == (0, 0) and x < 0:
                    continue
                if low <= x * x + ky * ky + kz * kz <= high:
                    col_key[j, 0, n] = ky * 64 + kz
                    col_kx[j, 0, n] = x + 12
                    col_id[j, 0, n] = (x * 64 + ky) * 64 + kz
                    n += 1
        assert n <= CAN
    wave = wave.reshape(GRID * GRID, 2 * DISC).astype(np.float32)
    along = along.astype(np.float32)
    return split_np(wave) + split_np(along) + (key, col_key, col_kx, col_id)


def split_np(value):


    high = value.astype(ml_dtypes.bfloat16)
    low = (value - high.astype(np.float32)).astype(ml_dtypes.bfloat16)
    return high, low


def folded(index):
    def fold(k):
        return jnp.where(k < GRID // 2, k, k - GRID)

    return (
        fold(lax.shift_right_logical(index, 10)),
        fold(lax.shift_right_logical(index, 5) & 31),
        fold(index & 31),
    )


def dot(a, b):
    return jnp.dot(a, b, preferred_element_type=F32)


def fetch(sources, targets, sems):
    copies = [pltpu.make_async_copy(s, t, sems.at[i]) for i, (s, t) in enumerate(zip(sources, targets))]
    for copy in copies:
        copy.start()
    return copies


def picked(spectrum, count, key, wanted, kx, store):
    half = NKX * 8
    hot = jnp.where(key[...] == wanted, jnp.float32(1), jnp.float32(0)).astype(BF)
    found = dot(spectrum[: 2 * count * half, :], hot)
    masks = [jnp.broadcast_to(kx == i, (8, wanted.shape[1])) for i in range(NKX - 1)]
    for s in range(count):
        parts = []
        for part in range(2):
            base = (2 * s + part) * half
            value = found[base : base + 8]
            for i in range(1, NKX - 1):
                value = jnp.where(masks[i], found[base + i * 8 : base + i * 8 + 8], value)
            parts.append(value)
        store(s, *parts)


def waves(pos, own, other, bands, wave_hi, wave_lo, along_hi, along_lo, ready, a_hi, a_lo, spectrum, first):
    zh, y, co = pos[0], pos[1], pos[2]
    count = len(bands)

    def product(q, carry):
        szh = (zh - q // 4) & 3
        sy = (y - q % 4) & 3
        start = pl.multiple_of(q * 16, 16)
        rows_of = [band[pl.ds(start, 16), :] for band in bands]
        for n in range(8):
            mine = own[sy, szh, n]
            theirs = other[sy, szh, n]
            lower = jnp.where(co == 0, mine, theirs)
            upper = jnp.where(co == 0, theirs, mine)
            for s in range(count):
                pair = [lower * rows_of[s][n : n + 1, :], upper * rows_of[s][8 + n : 9 + n, :]]
                high, low = split_bf16(jnp.concatenate(pair, axis=0))
                at = pl.ds(pl.multiple_of(s * 256 + start, 16), 16)
                a_hi[at, n * 128 : (n + 1) * 128] = high
                a_lo[at, n * 128 : (n + 1) * 128] = low
        return carry

    lax.fori_loop(0, 16, product, 0)
    ready()
    field = dot(a_hi[...], wave_hi[...]) + (dot(a_lo[...], wave_hi[...]) + dot(a_hi[...], wave_lo[...]))
    half = NKX * 8
    norm = jnp.float32(1.0) / jnp.sqrt(jnp.float32(GRID**3))
    for s in range(count):
        f_hi, f_lo = split_bf16(field[s * 256 : s * 256 + 256])
        full = dot(along_hi[...], f_hi) + (dot(along_lo[...], f_hi) + dot(along_hi[...], f_lo))
        real = full[:half, :DISC] + full[half:, DISC:]
        imag = full[:half, DISC:] - full[half:, :DISC]
        at = 2 * (first + s) * half
        spectrum[at : at + half, :] = (real * norm).astype(BF)
        spectrum[at + half : at + 2 * half, :] = (imag * norm).astype(BF)


def row_kernel(pos, *refs):
    sources, rows, spectrum, targets = refs[:9], refs[9], refs[10], refs[11:20]
    a_hi, a_lo, sems = refs[20:]
    own, other, band, wave_hi, wave_lo, along_hi, along_lo, key, gmap = targets
    copies = fetch(sources, targets, sems)
    for copy in copies[:3]:
        copy.wait()

    def ready():
        for copy in copies[3:]:
            copy.wait()

    waves(pos, own, other, [band], wave_hi, wave_lo, along_hi, along_lo, ready, a_hi, a_lo, spectrum, 0)

    def row_blocks(r, carry):
        kx, ky, kz = folded(gmap[r])
        flip = jnp.where((kz < 0) | ((kz == 0) & (ky < 0)), -1, 1)
        sign = flip.astype(F32)

        def store(s, real, imag):
            both = jnp.concatenate([real, imag * sign], axis=0).astype(BF)
            for t in range(4):
                rows[4 * r + t] = both[:, t * 256 : (t + 1) * 256]

        picked(spectrum, 1, key, flip * (ky * 64 + kz), flip * kx + 12, store)
        return carry

    lax.fori_loop(0, 8, row_blocks, 0)


def column_kernel(pos, *refs):
    sources, cols, targets = refs[:13], refs[13], refs[14:27]
    spectrum, a_hi, a_lo, sems = refs[27:]
    first, own, other, band1, band2, band3, wave_hi, wave_lo, along_hi, along_lo, key, col_key, col_kx = targets
    zl, x = pos[3], pos[4]
    copies = fetch(sources, targets, sems)
    for copy in copies[:6]:
        copy.wait()

    def ready():
        for copy in copies[6:]:
            copy.wait()

    spectrum[: 2 * NKX * 8, :] = first[...]
    bands = [band1, band2, band3]
    waves(pos, own, other, bands, wave_hi, wave_lo, along_hi, along_lo, ready, a_hi, a_lo, spectrum, 1)

    def columns(part, carry):
        j = (zl ^ part) * 4 + x

        def store(s, real, imag):
            cols[part, (x - s) & 3] = jnp.concatenate([real, imag], axis=0).astype(BF)

        picked(spectrum, 4, key, col_key[j], col_kx[j], store)
        return carry

    lax.fori_loop(0, 2, columns, 0)


def whole(shape):
    return pl.BlockSpec(shape, lambda *_: (0,) * len(shape), pipeline_mode=pl.Buffered(1))


def resident():
    return pl.BlockSpec(memory_space=pltpu.VMEM)


def transform_call(kernel, pos, operands, outs, scratch, flops, name):
    return pl.pallas_call(
        kernel,
        grid_spec=pltpu.PrefetchScalarGridSpec(
            num_scalar_prefetch=1,
            grid=(1,),
            in_specs=[pl.BlockSpec(memory_space=pl.ANY)] * len(operands),
            out_specs=[whole(v.shape) for v in outs],
            scratch_shapes=[pltpu.VMEM(v.shape, v.dtype) for v in operands]
            + scratch
            + [pltpu.SemaphoreType.DMA((len(operands),))],
        ),
        out_shape=outs,
        compiler_params=pltpu.CompilerParams(vmem_limit_bytes=60 << 20),
        cost_estimate=pl.CostEstimate(flops=flops, transcendentals=0, bytes_accessed=6 * 2**20),
        name=name,
    )(pos, *operands)


def row_pairs(pos, own, other, band, gmap):
    consts = [jnp.asarray(t) for t in tables()[:5]]
    outs = [jax.ShapeDtypeStruct((32, 16, 256), BF), jax.ShapeDtypeStruct((2 * NKX * 8, DISC), BF)]
    scratch = [pltpu.VMEM((256, 1024), BF)] * 2
    operands = [own, other, band, *consts, gmap.reshape(8, 1, 1024)]
    return transform_call(row_kernel, pos, operands, outs, scratch, 4 * 10**9, "row_pairs")


def column_pairs(pos, first, own, other, bands):
    consts = [jnp.asarray(t) for t in tables()[:7]]
    outs = [jax.ShapeDtypeStruct((2, 4, 16, CAN), BF)]
    scratch = [pltpu.VMEM((8 * NKX * 8, DISC), BF)] + [pltpu.VMEM((768, 1024), BF)] * 2
    operands = [first, own, other, *bands, *consts]
    return transform_call(column_kernel, pos, operands, outs, scratch, 8 * 10**9, "column_pairs")[0]


def prepare_kernel(pos, omega, r0, r1, r2, r3, gap, gmap, ident, scaled, hot, sign, row_k):
    zh, co, zl, x = pos[0], pos[2], pos[3], pos[4]

    @pl.when(pl.program_id(0) == 0)
    def _():
        kx, ky, kz = folded(gmap[0])
        flip = jnp.where((kz < 0) | ((kz == 0) & ((ky < 0) | ((ky == 0) & (kx < 0)))), -1, 1)
        wanted = (flip * ((kx * 64 + ky) * 64 + kz)).astype(F32)
        names = jnp.broadcast_to(ident[0].astype(F32), (128, CAN)).T
        signs = jnp.concatenate([jnp.ones((8, 1024), F32), jnp.broadcast_to(flip.astype(F32), (8, 1024))], axis=0)
        for t in range(8):
            at = slice(t * 128, (t + 1) * 128)
            here = slice(t % 2 * 128, t % 2 * 128 + 128)
            hot[t // 2, :, here] = jnp.where(names == wanted[:, at], jnp.float32(1), jnp.float32(0)).astype(BF)
            sign[t // 2, :, here] = signs[:, at]

    for side in range(2):
        co_at = co if side == 0 else 1 - co
        energies = []
        for s in range(4):
            zh_at = (zh - s) & 3
            energies.append(gap[zh_at, 0, co_at])
            for sx, ref in enumerate((r0, r1, r2, r3)):
                for szl in range(2):
                    n = (zl ^ szl) * 4 + ((x - sx) & 3)
                    to = pl.multiple_of(side * 512 + s * 128 + n * 16, 16)
                    row_k[pl.ds(to, 16), :] = ref[szl, zh_at, 0, co_at]
        energy = jnp.concatenate(energies, axis=1)
        total = row_k[side * 512 : side * 512 + 512, :].astype(F32).T
        for w in range(6):
            weight = -2.0 * energy / (energy * energy + omega[w] * omega[w])
            weight = weight / jnp.sqrt(jnp.float32(2048))
            at = slice(side * 512, side * 512 + 512)
            scaled[pl.program_id(0), w * 256 : (w + 1) * 256, at] = (total * weight).astype(BF)


def prepare(pos, omega, rows, gap, gmap, ident):
    rows = [pltpu.with_memory_space_constraint(r, pltpu.HBM) for r in rows]
    gmap, ident = (pltpu.with_memory_space_constraint(v, pltpu.HBM) for v in (gmap.reshape(8, 1, 1024), ident))
    row_spec = pl.BlockSpec((2, 4, 1, 2, 16, 256), lambda s, pos, om: (0, 0, (pos[1] - s) & 3, 0, 0, 0))
    return pl.pallas_call(
        prepare_kernel,
        grid_spec=pltpu.PrefetchScalarGridSpec(
            num_scalar_prefetch=2,
            grid=(4,),
            in_specs=[row_spec] * 4
            + [
                pl.BlockSpec((4, 1, 2, 1, 128), lambda s, pos, om: (0, (pos[1] - s) & 3, 0, 0, 0)),
                pl.BlockSpec((1, 1, 1024), lambda s, pos, om: (pos[3] * 4 + pos[4], 0, 0)),
                pl.BlockSpec((1, 1, CAN), lambda s, pos, om: (pos[3] * 4 + pos[4], 0, 0)),
            ],
            out_specs=[resident(), resident(), resident()],
            scratch_shapes=[pltpu.VMEM((1024, 256), BF)],
        ),
        out_shape=[pltpu.VMEM((4, 1536, 1024), BF), pltpu.VMEM((4, CAN, 256), BF), pltpu.VMEM((4, 16, 256), F32)],
        compiler_params=pltpu.CompilerParams(vmem_limit_bytes=20 << 20),
        cost_estimate=pl.CostEstimate(flops=10**9, transcendentals=0, bytes_accessed=20 * 2**20),
        name="scaled_rows",
    )(pos, omega, *rows, gap, gmap, ident)


def product_step(sy, mine, theirs, scaled, hot, sign, total, last):
    def kernel(mine, theirs, scaled, hot, sign, *refs):
        out, cols = refs[-2:]
        add = None if total is None else refs[0]

        def quarter(n):
            for side, ref in enumerate((mine, theirs)):
                full = dot(ref[...].reshape(512, CAN), hot[n]).reshape(32, 16, 256) * sign[n][None]
                cols[n, side * 512 : side * 512 + 512, :] = full.reshape(512, 256).astype(BF)
            part = dot(scaled[sy], cols[n]).reshape(6, 256, 256)
            at = pl.ds(pl.multiple_of(n * 256, 256), 256)
            part = part if add is None else add[:, :, at] + part
            if last:
                out[...] = part
            else:
                out[:, :, at] = part

        if last:
            quarter(pl.program_id(0))
        else:
            pl.loop(0, 4, unroll=2)(quarter)

    operands = [mine, theirs, scaled, hot, sign] + ([] if total is None else [total])
    aliases = {} if total is None or last else {5: 0}
    return pl.pallas_call(
        kernel,
        grid=(4 if last else 1,),
        in_specs=[resident()] * len(operands),
        out_specs=pl.BlockSpec((6, 256, 256), lambda n: (0, 0, n)) if last else resident(),
        scratch_shapes=[pltpu.VMEM((4, 1024, 256), BF)],
        out_shape=(jax.ShapeDtypeStruct if last else pltpu.VMEM)((6, 256, 1024), F32),
        input_output_aliases=aliases,
        compiler_params=pltpu.CompilerParams(vmem_limit_bytes=20 << 20),
        cost_estimate=pl.CostEstimate(flops=46 * 10**8, transcendentals=0, bytes_accessed=10 * 2**20),
        name="response_product",
    )(*operands)


def shifted(value, axis, shift):
    size = lax.axis_size(axis)
    return lax.ppermute(value, axis, [(i, (i + shift) % size) for i in range(size)])


def around(value, axis):
    return [value] + [shifted(value, axis, s) for s in range(1, lax.axis_size(axis))]


def neighbours(value, axis):
    return shifted(value, axis, 1), shifted(value, axis, 3)


def opposite(behind, ahead, axis):
    half = behind.shape[0] // 2
    return shifted(ahead[:half], axis, 3), shifted(behind[half:], axis, 1)


def body(valence, conduction, eps_val, eps_cond, omega, gmap):
    pos = jnp.stack([lax.axis_index(a) for a in AXES]).astype(jnp.int32)
    bands = around(conduction.reshape(256, 128), "x")
    own = lax.all_to_all(jnp.broadcast_to(valence, (8, *valence.shape)), NARROW, 0, 0, tiled=True)
    own, bands = lax.optimization_barrier((own, bands))
    own = jnp.stack(around(own, "zh"))
    gap = jnp.broadcast_to((eps_cond[:, None] - eps_val)[:, None, :], (256, 2, 8)).reshape(4, 4, 2, 1, 128)
    own, gap = lax.optimization_barrier((own, gap))
    own = jnp.stack(around(own, "y"))
    other = shifted(own, "co", 1)

    rows, spectrum = row_pairs(pos, own, other, bands[0], gmap)
    rows = lax.all_to_all(rows, WIDE, 0, 0, tiled=True)
    cols = column_pairs(pos, spectrum, own, other, bands[1:])
    kept, got = cols[0], shifted(cols[1], "zl", 1)
    lower = lax.axis_index("zl") == 0
    cols = jnp.concatenate([jnp.where(lower, kept, got), jnp.where(lower, got, kept)])
    rows = jnp.stack(around(rows, "zl")).reshape(2, 4, 4, 2, 16, 256)
    rows, cols = lax.optimization_barrier((rows, cols))
    near_x = neighbours(rows, "x")
    near_zh = neighbours(cols, "zh")
    near_x, near_zh = lax.optimization_barrier((near_x, near_zh))
    far_x, far_zh = lax.optimization_barrier((opposite(*near_x, "x"), opposite(*near_zh, "zh")))
    rows = [rows, near_x[0], jnp.concatenate(far_x), near_x[1]]
    cols = jnp.stack([cols, near_zh[0], jnp.concatenate(far_zh), near_zh[1]])
    near_y = neighbours(cols, "y")
    scaled, hot, sign = prepare(pos, omega, rows, gap, gmap, jnp.asarray(tables()[-1]))
    scaled, hot, sign, near_y = lax.optimization_barrier((scaled, hot, sign, near_y))
    far = opposite(*near_y, "y")
    total = product_step(0, cols, shifted(cols, "co", 1), scaled, hot, sign, None, False)
    total = product_step(1, near_y[0], shifted(near_y[0], "co", 1), scaled, hot, sign, total, False)
    total, far = lax.optimization_barrier((total, far))
    for sy, mine in ((3, near_y[1]), (2, jnp.concatenate(far))):
        theirs = shifted(mine, "co", 1)
        total = product_step(sy, mine, theirs, scaled, hot, sign, total, sy == 2)
    return total


def solution(mesh):
    torus = Mesh(mesh.devices.reshape(4, 4, 2, 2, 4), AXES)
    return jax.shard_map(
        body,
        mesh=torus,
        in_specs=(P(None, AXES), P(AXES, None), P(), P(), P(), P()),
        out_specs=P(None, WIDE, NARROW),
        check_vma=False,
    )
```

```python
import functools

import jax
import jax.numpy as jnp
import ml_dtypes
import numpy as np
from jax import lax
from jax.experimental import pallas as pl
from jax.experimental.pallas import tpu as pltpu
from jax.sharding import Mesh
from jax.sharding import PartitionSpec as P

GRID = 32
AXES = ("zh", "y", "co", "zl", "x")
WIDE = ("zh", "y", "co")
NARROW = ("zl", "x")
NPW = 8192
DISC = 256
NKX = 26
CAN = 640
BF = jnp.bfloat16
F32 = jnp.float32


def split_bf16(value):
    high = value.astype(BF)
    return high, (value - high.astype(value.dtype)).astype(BF)


def tables():
    k = np.arange(GRID)
    fold = np.where(k < GRID // 2, k, k - GRID)
    length = fold[:, None, None] ** 2 + fold[None, :, None] ** 2 + fold[None, None, :] ** 2
    ordered = np.sort(length.ravel())[:NPW]
    limit = ordered[-1]
    disc = []
    for ky in range(-15, 16):
        for kz in range(0, 16):
            if ky * ky + kz * kz <= limit and (kz > 0 or ky >= 0):
                disc.append((ky, kz))
    assert len(disc) <= DISC
    points = np.arange(GRID)
    wave = np.zeros((GRID, GRID, 2 * DISC))
    key = np.full((DISC, 1), -9000, np.int32)
    for m, (ky, kz) in enumerate(disc):
        angle = 2 * np.pi * ((ky * points[:, None] + kz * points[None, :]) % GRID) / GRID
        wave[:, :, m] = np.cos(angle)
        wave[:, :, DISC + m] = -np.sin(angle)
        key[m, 0] = ky * 64 + kz
    kx = np.arange(NKX) - 12
    assert limit < 13 * 13
    angle = 2 * np.pi * (kx[:, None] * points[None, :] % GRID) / GRID
    eye = np.eye(8)
    along = np.concatenate([np.kron(np.cos(angle), eye), np.kron(np.sin(angle), eye)])
    blocks = 8
    col_key = np.full((blocks, 1, CAN), -8000, np.int32)
    col_kx = np.zeros((blocks, 1, CAN), np.int32)
    col_id = np.full((blocks, 1, CAN), -(1 << 20), np.int32)
    size = NPW // blocks
    for j in range(blocks):
        low, high = ordered[j * size], ordered[(j + 1) * size - 1]
        n = 0
        for ky, kz in disc:
            for x in range(-12, 13):
                if (ky, kz) == (0, 0) and x < 0:
                    continue
                if low <= x * x + ky * ky + kz * kz <= high:
                    col_key[j, 0, n] = ky * 64 + kz
                    col_kx[j, 0, n] = x + 12
                    col_id[j, 0, n] = (x * 64 + ky) * 64 + kz
                    n += 1
        assert n <= CAN
    wave = wave.reshape(GRID * GRID, 2 * DISC).astype(np.float32)
    along = along.astype(np.float32)
    return split_np(wave) + split_np(along) + (key, col_key, col_kx, col_id)


def split_np(value):


    high = value.astype(ml_dtypes.bfloat16)
    low = (value - high.astype(np.float32)).astype(ml_dtypes.bfloat16)
    return high, low


def folded(index):
    def fold(k):
        return jnp.where(k < GRID // 2, k, k - GRID)

    return (
        fold(lax.shift_right_logical(index, 10)),
        fold(lax.shift_right_logical(index, 5) & 31),
        fold(index & 31),
    )


def dot(a, b):
    return jnp.dot(a, b, preferred_element_type=F32)


def fetch(sources, targets, sems):
    copies = [pltpu.make_async_copy(s, t, sems.at[i]) for i, (s, t) in enumerate(zip(sources, targets))]
    for copy in copies:
        copy.start()
    return copies


def picked(spectrum, count, key, wanted, kx, store):
    half = NKX * 8
    hot = jnp.where(key[...] == wanted, jnp.float32(1), jnp.float32(0)).astype(BF)
    found = dot(spectrum[: 2 * count * half, :], hot)
    masks = [jnp.broadcast_to(kx == i, (8, wanted.shape[1])) for i in range(NKX - 1)]
    for s in range(count):
        parts = []
        for part in range(2):
            base = (2 * s + part) * half
            value = found[base : base + 8]
            for i in range(1, NKX - 1):
                value = jnp.where(masks[i], found[base + i * 8 : base + i * 8 + 8], value)
            parts.append(value)
        store(s, *parts)


def waves(pos, own, other, bands, wave_hi, wave_lo, along_hi, along_lo, ready, a_hi, a_lo, spectrum, first):
    zh, y, co = pos[0], pos[1], pos[2]
    count = len(bands)

    def product(q, carry):
        szh = zh ^ (q // 4)
        sy = y ^ (q % 4)
        start = pl.multiple_of(q * 16, 16)
        rows_of = [band[pl.ds(start, 16), :] for band in bands]
        for n in range(8):
            mine = own[sy, szh, n]
            theirs = other[sy, szh, n]
            lower = jnp.where(co == 0, mine, theirs)
            upper = jnp.where(co == 0, theirs, mine)
            for s in range(count):
                pair = [lower * rows_of[s][n : n + 1, :], upper * rows_of[s][8 + n : 9 + n, :]]
                high, low = split_bf16(jnp.concatenate(pair, axis=0))
                at = pl.ds(pl.multiple_of(s * 256 + start, 16), 16)
                a_hi[at, n * 128 : (n + 1) * 128] = high
                a_lo[at, n * 128 : (n + 1) * 128] = low
        return carry

    lax.fori_loop(0, 16, product, 0)
    ready()
    field = dot(a_hi[...], wave_hi[...]) + (dot(a_lo[...], wave_hi[...]) + dot(a_hi[...], wave_lo[...]))
    half = NKX * 8
    norm = jnp.float32(1.0) / jnp.sqrt(jnp.float32(GRID**3))
    for s in range(count):
        f_hi, f_lo = split_bf16(field[s * 256 : s * 256 + 256])
        full = dot(along_hi[...], f_hi) + (dot(along_lo[...], f_hi) + dot(along_hi[...], f_lo))
        real = full[:half, :DISC] + full[half:, DISC:]
        imag = full[:half, DISC:] - full[half:, :DISC]
        at = 2 * (first + s) * half
        spectrum[at : at + half, :] = (real * norm).astype(BF)
        spectrum[at + half : at + 2 * half, :] = (imag * norm).astype(BF)


def row_kernel(pos, *refs):
    sources, rows, spectrum, targets = refs[:9], refs[9], refs[10], refs[11:20]
    a_hi, a_lo, sems = refs[20:]
    own, other, band, wave_hi, wave_lo, along_hi, along_lo, key, gmap = targets
    copies = fetch(sources, targets, sems)
    for copy in copies[:3]:
        copy.wait()

    def ready():
        for copy in copies[3:]:
            copy.wait()

    waves(pos, own, other, [band], wave_hi, wave_lo, along_hi, along_lo, ready, a_hi, a_lo, spectrum, 0)

    def row_blocks(r, carry):
        kx, ky, kz = folded(gmap[r])
        flip = jnp.where((kz < 0) | ((kz == 0) & (ky < 0)), -1, 1)
        sign = flip.astype(F32)

        def store(s, real, imag):
            both = jnp.concatenate([real, imag * sign], axis=0).astype(BF)
            for t in range(4):
                rows[4 * r + t] = both[:, t * 256 : (t + 1) * 256]

        picked(spectrum, 1, key, flip * (ky * 64 + kz), flip * kx + 12, store)
        return carry

    lax.fori_loop(0, 8, row_blocks, 0)


def column_kernel(pos, *refs):
    sources, cols, targets = refs[:13], refs[13], refs[14:27]
    spectrum, a_hi, a_lo, sems = refs[27:]
    first, own, other, band1, band2, band3, wave_hi, wave_lo, along_hi, along_lo, key, col_key, col_kx = targets
    zl, x = pos[3], pos[4]
    copies = fetch(sources, targets, sems)
    for copy in copies[:6]:
        copy.wait()

    def ready():
        for copy in copies[6:]:
            copy.wait()

    spectrum[: 2 * NKX * 8, :] = first[...]
    bands = [band1, band2, band3]
    waves(pos, own, other, bands, wave_hi, wave_lo, along_hi, along_lo, ready, a_hi, a_lo, spectrum, 1)

    def columns(part, carry):
        j = (zl ^ part) * 4 + x

        def store(s, real, imag):
            cols[part, (x - s) & 3] = jnp.concatenate([real, imag], axis=0).astype(BF)

        picked(spectrum, 4, key, col_key[j], col_kx[j], store)
        return carry

    lax.fori_loop(0, 2, columns, 0)


def whole(shape):
    return pl.BlockSpec(shape, lambda *_: (0,) * len(shape), pipeline_mode=pl.Buffered(1))


def resident():
    return pl.BlockSpec(memory_space=pltpu.VMEM)


def transform_call(kernel, pos, operands, outs, scratch, flops, name):
    return pl.pallas_call(
        kernel,
        grid_spec=pltpu.PrefetchScalarGridSpec(
            num_scalar_prefetch=1,
            grid=(1,),
            in_specs=[pl.BlockSpec(memory_space=pl.ANY)] * len(operands),
            out_specs=[whole(v.shape) for v in outs],
            scratch_shapes=[pltpu.VMEM(v.shape, v.dtype) for v in operands]
            + scratch
            + [pltpu.SemaphoreType.DMA((len(operands),))],
        ),
        out_shape=outs,
        compiler_params=pltpu.CompilerParams(vmem_limit_bytes=60 << 20),
        cost_estimate=pl.CostEstimate(flops=flops, transcendentals=0, bytes_accessed=6 * 2**20),
        name=name,
    )(pos, *operands)


def row_pairs(pos, own, other, band, gmap):
    consts = [jnp.asarray(t) for t in tables()[:5]]
    outs = [jax.ShapeDtypeStruct((32, 16, 256), BF), jax.ShapeDtypeStruct((2 * NKX * 8, DISC), BF)]
    scratch = [pltpu.VMEM((256, 1024), BF)] * 2
    operands = [own, other, band, *consts, gmap.reshape(8, 1, 1024)]
    return transform_call(row_kernel, pos, operands, outs, scratch, 4 * 10**9, "row_pairs")


def column_pairs(pos, first, own, other, bands):
    consts = [jnp.asarray(t) for t in tables()[:7]]
    outs = [jax.ShapeDtypeStruct((2, 4, 16, CAN), BF)]
    scratch = [pltpu.VMEM((8 * NKX * 8, DISC), BF)] + [pltpu.VMEM((768, 1024), BF)] * 2
    operands = [first, own, other, *bands, *consts]
    return transform_call(column_kernel, pos, operands, outs, scratch, 8 * 10**9, "column_pairs")[0]


def prepare_kernel(pos, omega, r0, r1, r2, r3, gap, gmap, ident, scaled, hot, sign, row_k):
    zh, co, zl, x = pos[0], pos[2], pos[3], pos[4]

    @pl.when(pl.program_id(0) == 0)
    def _():
        kx, ky, kz = folded(gmap[0])
        flip = jnp.where((kz < 0) | ((kz == 0) & ((ky < 0) | ((ky == 0) & (kx < 0)))), -1, 1)
        wanted = (flip * ((kx * 64 + ky) * 64 + kz)).astype(F32)
        names = jnp.broadcast_to(ident[0].astype(F32), (128, CAN)).T
        signs = jnp.concatenate([jnp.ones((8, 1024), F32), jnp.broadcast_to(flip.astype(F32), (8, 1024))], axis=0)
        for t in range(8):
            at = slice(t * 128, (t + 1) * 128)
            here = slice(t % 2 * 128, t % 2 * 128 + 128)
            hot[t // 2, :, here] = jnp.where(names == wanted[:, at], jnp.float32(1), jnp.float32(0)).astype(BF)
            sign[t // 2, :, here] = signs[:, at]

    for side in range(2):
        co_at = co if side == 0 else 1 - co
        energies = []
        for s in range(4):
            zh_at = (zh - s) & 3
            energies.append(gap[zh_at, 0, co_at])
            for sx, ref in enumerate((r0, r1, r2, r3)):
                for szl in range(2):
                    n = (zl ^ szl) * 4 + ((x - sx) & 3)
                    to = pl.multiple_of(side * 512 + s * 128 + n * 16, 16)
                    row_k[pl.ds(to, 16), :] = ref[szl, zh_at, 0, co_at]
        energy = jnp.concatenate(energies, axis=1)
        total = row_k[side * 512 : side * 512 + 512, :].astype(F32).T
        for w in range(6):
            weight = -2.0 * energy / (energy * energy + omega[w] * omega[w])
            weight = weight / jnp.sqrt(jnp.float32(2048))
            at = slice(side * 512, side * 512 + 512)
            scaled[pl.program_id(0), w * 256 : (w + 1) * 256, at] = (total * weight).astype(BF)


def prepare(pos, omega, rows, gap, gmap, ident):
    rows = [pltpu.with_memory_space_constraint(r, pltpu.HBM) for r in rows]
    gmap, ident = (pltpu.with_memory_space_constraint(v, pltpu.HBM) for v in (gmap.reshape(8, 1, 1024), ident))
    row_spec = pl.BlockSpec((2, 4, 1, 2, 16, 256), lambda s, pos, om: (0, 0, (pos[1] - s) & 3, 0, 0, 0))
    return pl.pallas_call(
        prepare_kernel,
        grid_spec=pltpu.PrefetchScalarGridSpec(
            num_scalar_prefetch=2,
            grid=(4,),
            in_specs=[row_spec] * 4
            + [
                pl.BlockSpec((4, 1, 2, 1, 128), lambda s, pos, om: (0, (pos[1] - s) & 3, 0, 0, 0)),
                pl.BlockSpec((1, 1, 1024), lambda s, pos, om: (pos[3] * 4 + pos[4], 0, 0)),
                pl.BlockSpec((1, 1, CAN), lambda s, pos, om: (pos[3] * 4 + pos[4], 0, 0)),
            ],
            out_specs=[resident(), resident(), resident()],
            scratch_shapes=[pltpu.VMEM((1024, 256), BF)],
        ),
        out_shape=[pltpu.VMEM((4, 1536, 1024), BF), pltpu.VMEM((4, CAN, 256), BF), pltpu.VMEM((4, 16, 256), F32)],
        compiler_params=pltpu.CompilerParams(vmem_limit_bytes=20 << 20),
        cost_estimate=pl.CostEstimate(flops=10**9, transcendentals=0, bytes_accessed=20 * 2**20),
        name="scaled_rows",
    )(pos, omega, *rows, gap, gmap, ident)


def product_step(sy, mine, theirs, scaled, hot, sign, total, last):
    def kernel(mine, theirs, scaled, hot, sign, *refs):
        out, cols = refs[-2:]
        add = None if total is None else refs[0]

        def quarter(n):
            for side, ref in enumerate((mine, theirs)):
                full = dot(ref[...].reshape(512, CAN), hot[n]).reshape(32, 16, 256) * sign[n][None]
                cols[n, side * 512 : side * 512 + 512, :] = full.reshape(512, 256).astype(BF)
            part = dot(scaled[sy], cols[n]).reshape(6, 256, 256)
            at = pl.ds(pl.multiple_of(n * 256, 256), 256)
            part = part if add is None else add[:, :, at] + part
            if last:
                out[...] = part
            else:
                out[:, :, at] = part

        if last:
            quarter(pl.program_id(0))
        else:
            pl.loop(0, 4, unroll=2)(quarter)

    operands = [mine, theirs, scaled, hot, sign] + ([] if total is None else [total])
    aliases = {} if total is None or last else {5: 0}
    return pl.pallas_call(
        kernel,
        grid=(4 if last else 1,),
        in_specs=[resident()] * len(operands),
        out_specs=pl.BlockSpec((6, 256, 256), lambda n: (0, 0, n)) if last else resident(),
        scratch_shapes=[pltpu.VMEM((4, 1024, 256), BF)],
        out_shape=(jax.ShapeDtypeStruct if last else pltpu.VMEM)((6, 256, 1024), F32),
        input_output_aliases=aliases,
        compiler_params=pltpu.CompilerParams(vmem_limit_bytes=20 << 20),
        cost_estimate=pl.CostEstimate(flops=46 * 10**8, transcendentals=0, bytes_accessed=10 * 2**20),
        name="response_product",
    )(*operands)


def shifted(value, axis, shift):
    size = lax.axis_size(axis)
    return lax.ppermute(value, axis, [(i, (i + shift) % size) for i in range(size)])


def around(value, axis):
    return [value] + [shifted(value, axis, s) for s in range(1, lax.axis_size(axis))]


def doubled(value, axis):
    pair = jnp.stack([value, lax.ppermute(value, axis, [(i, i ^ 1) for i in range(4)])])
    far = lax.ppermute(pair, axis, [(i, i ^ 3) for i in range(4)])
    return jnp.stack([pair[0], pair[1], far[1], far[0]])


def neighbours(value, axis):
    return shifted(value, axis, 1), shifted(value, axis, 3)


def opposite(behind, ahead, axis):
    half = behind.shape[0] // 2
    return shifted(ahead[:half], axis, 3), shifted(behind[half:], axis, 1)


def body(valence, conduction, eps_val, eps_cond, omega, gmap):
    pos = jnp.stack([lax.axis_index(a) for a in AXES]).astype(jnp.int32)
    bands = around(conduction.reshape(256, 128), "x")
    own = lax.all_to_all(jnp.broadcast_to(valence, (8, *valence.shape)), NARROW, 0, 0, tiled=True)
    own, bands = lax.optimization_barrier((own, bands))
    own = doubled(own, "zh")
    gap = jnp.broadcast_to((eps_cond[:, None] - eps_val)[:, None, :], (256, 2, 8)).reshape(4, 4, 2, 1, 128)
    own, gap = lax.optimization_barrier((own, gap))
    own = doubled(own, "y")
    other = shifted(own, "co", 1)

    rows, spectrum = row_pairs(pos, own, other, bands[0], gmap)
    rows = lax.all_to_all(rows, WIDE, 0, 0, tiled=True)
    cols = column_pairs(pos, spectrum, own, other, bands[1:])
    kept, got = cols[0], shifted(cols[1], "zl", 1)
    lower = lax.axis_index("zl") == 0
    cols = jnp.concatenate([jnp.where(lower, kept, got), jnp.where(lower, got, kept)])
    rows = jnp.stack(around(rows, "zl")).reshape(2, 4, 4, 2, 16, 256)
    rows, cols = lax.optimization_barrier((rows, cols))
    near_x = neighbours(rows, "x")
    near_zh = neighbours(cols, "zh")
    near_x, near_zh = lax.optimization_barrier((near_x, near_zh))
    far_x, far_zh = lax.optimization_barrier((opposite(*near_x, "x"), opposite(*near_zh, "zh")))
    rows = [rows, near_x[0], jnp.concatenate(far_x), near_x[1]]
    cols = jnp.stack([cols, near_zh[0], jnp.concatenate(far_zh), near_zh[1]])
    near_y = neighbours(cols, "y")
    scaled, hot, sign = prepare(pos, omega, rows, gap, gmap, jnp.asarray(tables()[-1]))
    scaled, hot, sign, near_y = lax.optimization_barrier((scaled, hot, sign, near_y))
    far = opposite(*near_y, "y")
    total = product_step(0, cols, shifted(cols, "co", 1), scaled, hot, sign, None, False)
    total = product_step(1, near_y[0], shifted(near_y[0], "co", 1), scaled, hot, sign, total, False)
    total, far = lax.optimization_barrier((total, far))
    for sy, mine in ((3, near_y[1]), (2, jnp.concatenate(far))):
        theirs = shifted(mine, "co", 1)
        total = product_step(sy, mine, theirs, scaled, hot, sign, total, sy == 2)
    return total


def solution(mesh):
    torus = Mesh(mesh.devices.reshape(4, 4, 2, 2, 4), AXES)
    return jax.shard_map(
        body,
        mesh=torus,
        in_specs=(P(None, AXES), P(AXES, None), P(), P(), P(), P()),
        out_specs=P(None, WIDE, NARROW),
        check_vma=False,
    )
```

```python
import functools

import jax
import jax.numpy as jnp
import ml_dtypes
import numpy as np
from jax import lax
from jax.experimental import pallas as pl
from jax.experimental.pallas import tpu as pltpu
from jax.sharding import Mesh
from jax.sharding import PartitionSpec as P

GRID = 32
AXES = ("zh", "y", "co", "zl", "x")
WIDE = ("zh", "y", "co")
NARROW = ("zl", "x")
NPW = 8192
DISC = 256
NKX = 26
CAN = 640
BF = jnp.bfloat16
F32 = jnp.float32


def split_bf16(value):
    high = value.astype(BF)
    return high, (value - high.astype(value.dtype)).astype(BF)


def tables():
    k = np.arange(GRID)
    fold = np.where(k < GRID // 2, k, k - GRID)
    length = fold[:, None, None] ** 2 + fold[None, :, None] ** 2 + fold[None, None, :] ** 2
    ordered = np.sort(length.ravel())[:NPW]
    limit = ordered[-1]
    disc = []
    for ky in range(-15, 16):
        for kz in range(0, 16):
            if ky * ky + kz * kz <= limit and (kz > 0 or ky >= 0):
                disc.append((ky, kz))
    assert len(disc) <= DISC
    points = np.arange(GRID)
    wave = np.zeros((GRID, GRID, 2 * DISC))
    key = np.full((DISC, 1), -9000, np.int32)
    for m, (ky, kz) in enumerate(disc):
        angle = 2 * np.pi * ((ky * points[:, None] + kz * points[None, :]) % GRID) / GRID
        wave[:, :, m] = np.cos(angle)
        wave[:, :, DISC + m] = -np.sin(angle)
        key[m, 0] = ky * 64 + kz
    kx = np.arange(NKX) - 12
    assert limit < 13 * 13
    angle = 2 * np.pi * (kx[:, None] * points[None, :] % GRID) / GRID
    eye = np.eye(8)
    along = np.concatenate([np.kron(np.cos(angle), eye), np.kron(np.sin(angle), eye)])
    blocks = 8
    col_key = np.full((blocks, 1, CAN), -8000, np.int32)
    col_kx = np.zeros((blocks, 1, CAN), np.int32)
    col_id = np.full((blocks, 1, CAN), -(1 << 20), np.int32)
    size = NPW // blocks
    for j in range(blocks):
        low, high = ordered[j * size], ordered[(j + 1) * size - 1]
        n = 0
        for ky, kz in disc:
            for x in range(-12, 13):
                if (ky, kz) == (0, 0) and x < 0:
                    continue
                if low <= x * x + ky * ky + kz * kz <= high:
                    col_key[j, 0, n] = ky * 64 + kz
                    col_kx[j, 0, n] = x + 12
                    col_id[j, 0, n] = (x * 64 + ky) * 64 + kz
                    n += 1
        assert n <= CAN
    wave = wave.reshape(GRID * GRID, 2 * DISC).astype(np.float32)
    along = along.astype(np.float32)
    return split_np(wave) + split_np(along) + (key, col_key, col_kx, col_id)


def split_np(value):


    high = value.astype(ml_dtypes.bfloat16)
    low = (value - high.astype(np.float32)).astype(ml_dtypes.bfloat16)
    return high, low


def folded(index):
    def fold(k):
        return jnp.where(k < GRID // 2, k, k - GRID)

    return (
        fold(lax.shift_right_logical(index, 10)),
        fold(lax.shift_right_logical(index, 5) & 31),
        fold(index & 31),
    )


def dot(a, b):
    return jnp.dot(a, b, preferred_element_type=F32)


def fetch(sources, targets, sems):
    copies = [pltpu.make_async_copy(s, t, sems.at[i]) for i, (s, t) in enumerate(zip(sources, targets))]
    for copy in copies:
        copy.start()
    return copies


def picked(spectrum, count, key, wanted, kx, store):
    half = NKX * 8
    hot = jnp.where(key[...] == wanted, jnp.float32(1), jnp.float32(0)).astype(BF)
    found = dot(spectrum[: 2 * count * half, :], hot)
    masks = [jnp.broadcast_to(kx == i, (8, wanted.shape[1])) for i in range(NKX - 1)]
    for s in range(count):
        parts = []
        for part in range(2):
            base = (2 * s + part) * half
            value = found[base : base + 8]
            for i in range(1, NKX - 1):
                value = jnp.where(masks[i], found[base + i * 8 : base + i * 8 + 8], value)
            parts.append(value)
        store(s, *parts)


def waves(pos, own, other, bands, wave_hi, wave_lo, along_hi, along_lo, ready, a_hi, a_lo, spectrum, first):
    zh, y, co = pos[0], pos[1], pos[2]
    count = len(bands)

    def product(q, carry):
        szh = (zh - q // 4) & 3
        sy = (y - q % 4) & 3
        start = pl.multiple_of(q * 16, 16)
        rows_of = [band[pl.ds(start, 16), :] for band in bands]
        for n in range(8):
            mine = own[sy, szh, n]
            theirs = other[sy, szh, n]
            lower = jnp.where(co == 0, mine, theirs)
            upper = jnp.where(co == 0, theirs, mine)
            for s in range(count):
                pair = [lower * rows_of[s][n : n + 1, :], upper * rows_of[s][8 + n : 9 + n, :]]
                high, low = split_bf16(jnp.concatenate(pair, axis=0))
                at = pl.ds(pl.multiple_of(s * 256 + start, 16), 16)
                a_hi[at, n * 128 : (n + 1) * 128] = high
                a_lo[at, n * 128 : (n + 1) * 128] = low
        return carry

    lax.fori_loop(0, 16, product, 0)
    ready()
    field = dot(a_hi[...], wave_hi[...]) + (dot(a_lo[...], wave_hi[...]) + dot(a_hi[...], wave_lo[...]))
    half = NKX * 8
    norm = jnp.float32(1.0) / jnp.sqrt(jnp.float32(GRID**3))
    for s in range(count):
        f_hi, f_lo = split_bf16(field[s * 256 : s * 256 + 256])
        full = dot(along_hi[...], f_hi) + (dot(along_lo[...], f_hi) + dot(along_hi[...], f_lo))
        real = full[:half, :DISC] + full[half:, DISC:]
        imag = full[:half, DISC:] - full[half:, :DISC]
        at = 2 * (first + s) * half
        spectrum[at : at + half, :] = (real * norm).astype(BF)
        spectrum[at + half : at + 2 * half, :] = (imag * norm).astype(BF)


def row_kernel(pos, *refs):
    sources, rows, spectrum, targets = refs[:9], refs[9], refs[10], refs[11:20]
    a_hi, a_lo, sems = refs[20:]
    own, other, band, wave_hi, wave_lo, along_hi, along_lo, key, gmap = targets
    copies = fetch(sources, targets, sems)
    for copy in copies[:3]:
        copy.wait()

    def ready():
        for copy in copies[3:]:
            copy.wait()

    waves(pos, own, other, [band], wave_hi, wave_lo, along_hi, along_lo, ready, a_hi, a_lo, spectrum, 0)

    def row_blocks(r, carry):
        kx, ky, kz = folded(gmap[r])
        flip = jnp.where((kz < 0) | ((kz == 0) & (ky < 0)), -1, 1)
        sign = flip.astype(F32)

        def store(s, real, imag):
            both = jnp.concatenate([real, imag * sign], axis=0).astype(BF)
            for t in range(4):
                rows[4 * r + t] = both[:, t * 256 : (t + 1) * 256]

        picked(spectrum, 1, key, flip * (ky * 64 + kz), flip * kx + 12, store)
        return carry

    lax.fori_loop(0, 8, row_blocks, 0)


def column_kernel(pos, *refs):
    sources, cols, targets = refs[:13], refs[13], refs[14:27]
    spectrum, a_hi, a_lo, sems = refs[27:]
    first, own, other, band1, band2, band3, wave_hi, wave_lo, along_hi, along_lo, key, col_key, col_kx = targets
    zl, x = pos[3], pos[4]
    copies = fetch(sources, targets, sems)
    for copy in copies[:6]:
        copy.wait()

    def ready():
        for copy in copies[6:]:
            copy.wait()

    spectrum[: 2 * NKX * 8, :] = first[...]
    bands = [band1, band2, band3]
    waves(pos, own, other, bands, wave_hi, wave_lo, along_hi, along_lo, ready, a_hi, a_lo, spectrum, 1)

    def columns(part, carry):
        j = (zl ^ part) * 4 + x

        def store(s, real, imag):
            cols[part, (x - s) & 3] = jnp.concatenate([real, imag], axis=0).astype(BF)

        picked(spectrum, 4, key, col_key[j], col_kx[j], store)
        return carry

    lax.fori_loop(0, 2, columns, 0)


def whole(shape):
    return pl.BlockSpec(shape, lambda *_: (0,) * len(shape), pipeline_mode=pl.Buffered(1))


def resident():
    return pl.BlockSpec(memory_space=pltpu.VMEM)


def transform_call(kernel, pos, operands, outs, scratch, flops, name):
    return pl.pallas_call(
        kernel,
        grid_spec=pltpu.PrefetchScalarGridSpec(
            num_scalar_prefetch=1,
            grid=(1,),
            in_specs=[pl.BlockSpec(memory_space=pl.ANY)] * len(operands),
            out_specs=[whole(v.shape) for v in outs],
            scratch_shapes=[pltpu.VMEM(v.shape, v.dtype) for v in operands]
            + scratch
            + [pltpu.SemaphoreType.DMA((len(operands),))],
        ),
        out_shape=outs,
        compiler_params=pltpu.CompilerParams(vmem_limit_bytes=60 << 20),
        cost_estimate=pl.CostEstimate(flops=flops, transcendentals=0, bytes_accessed=6 * 2**20),
        name=name,
    )(pos, *operands)


def row_pairs(pos, own, other, band, gmap):
    consts = [jnp.asarray(t) for t in tables()[:5]]
    outs = [jax.ShapeDtypeStruct((32, 16, 256), BF), jax.ShapeDtypeStruct((2 * NKX * 8, DISC), BF)]
    scratch = [pltpu.VMEM((256, 1024), BF)] * 2
    operands = [own, other, band, *consts, gmap.reshape(8, 1, 1024)]
    return transform_call(row_kernel, pos, operands, outs, scratch, 4 * 10**9, "row_pairs")


def column_pairs(pos, first, own, other, bands):
    consts = [jnp.asarray(t) for t in tables()[:7]]
    outs = [jax.ShapeDtypeStruct((2, 4, 16, CAN), BF)]
    scratch = [pltpu.VMEM((8 * NKX * 8, DISC), BF)] + [pltpu.VMEM((768, 1024), BF)] * 2
    operands = [first, own, other, *bands, *consts]
    return transform_call(column_kernel, pos, operands, outs, scratch, 8 * 10**9, "column_pairs")[0]


def prepare_kernel(pos, omega, r0, r1, r2, r3, gap, gmap, ident, scaled, hot, sign, row_k):
    zh, co, zl, x = pos[0], pos[2], pos[3], pos[4]

    @pl.when(pl.program_id(0) == 0)
    def _():
        kx, ky, kz = folded(gmap[0])
        flip = jnp.where((kz < 0) | ((kz == 0) & ((ky < 0) | ((ky == 0) & (kx < 0)))), -1, 1)
        wanted = (flip * ((kx * 64 + ky) * 64 + kz)).astype(F32)
        names = jnp.broadcast_to(ident[0].astype(F32), (128, CAN)).T
        signs = jnp.concatenate([jnp.ones((8, 1024), F32), jnp.broadcast_to(flip.astype(F32), (8, 1024))], axis=0)
        for t in range(8):
            at = slice(t * 128, (t + 1) * 128)
            here = slice(t % 2 * 128, t % 2 * 128 + 128)
            hot[t // 2, :, here] = jnp.where(names == wanted[:, at], jnp.float32(1), jnp.float32(0)).astype(BF)
            sign[t // 2, :, here] = signs[:, at]

    for side in range(2):
        co_at = co if side == 0 else 1 - co
        energies = []
        for s in range(4):
            zh_at = (zh - s) & 3
            energies.append(gap[zh_at, 0, co_at])
            for sx, ref in enumerate((r0, r1, r2, r3)):
                for szl in range(2):
                    n = (zl ^ szl) * 4 + ((x - sx) & 3)
                    to = pl.multiple_of(side * 512 + s * 128 + n * 16, 16)
                    row_k[pl.ds(to, 16), :] = ref[szl, zh_at, 0, co_at]
        energy = jnp.concatenate(energies, axis=1)
        total = row_k[side * 512 : side * 512 + 512, :].astype(F32).T
        for w in range(6):
            weight = -2.0 * energy / (energy * energy + omega[w] * omega[w])
            weight = weight / jnp.sqrt(jnp.float32(2048))
            at = slice(side * 512, side * 512 + 512)
            scaled[pl.program_id(0), w * 256 : (w + 1) * 256, at] = (total * weight).astype(BF)


def prepare(pos, omega, rows, gap, gmap, ident):
    rows = [pltpu.with_memory_space_constraint(r, pltpu.HBM) for r in rows]
    gmap, ident = (pltpu.with_memory_space_constraint(v, pltpu.HBM) for v in (gmap.reshape(8, 1, 1024), ident))
    row_spec = pl.BlockSpec((2, 4, 1, 2, 16, 256), lambda s, pos, om: (0, 0, (pos[1] - s) & 3, 0, 0, 0))
    return pl.pallas_call(
        prepare_kernel,
        grid_spec=pltpu.PrefetchScalarGridSpec(
            num_scalar_prefetch=2,
            grid=(4,),
            in_specs=[row_spec] * 4
            + [
                pl.BlockSpec((4, 1, 2, 1, 128), lambda s, pos, om: (0, (pos[1] - s) & 3, 0, 0, 0)),
                pl.BlockSpec((1, 1, 1024), lambda s, pos, om: (pos[3] * 4 + pos[4], 0, 0)),
                pl.BlockSpec((1, 1, CAN), lambda s, pos, om: (pos[3] * 4 + pos[4], 0, 0)),
            ],
            out_specs=[resident(), resident(), resident()],
            scratch_shapes=[pltpu.VMEM((1024, 256), BF)],
        ),
        out_shape=[pltpu.VMEM((4, 1536, 1024), BF), pltpu.VMEM((4, CAN, 256), BF), pltpu.VMEM((4, 16, 256), F32)],
        compiler_params=pltpu.CompilerParams(vmem_limit_bytes=20 << 20),
        cost_estimate=pl.CostEstimate(flops=10**9, transcendentals=0, bytes_accessed=20 * 2**20),
        name="scaled_rows",
    )(pos, omega, *rows, gap, gmap, ident)


def product_step(sy, mine, theirs, scaled, hot, sign, total, last):
    def kernel(mine, theirs, scaled, hot, sign, *refs):
        out, cols = refs[-2:]
        add = None if total is None else refs[0]

        def quarter(n):
            for side, ref in enumerate((mine, theirs)):
                full = dot(ref[...].reshape(512, CAN), hot[n]).reshape(32, 16, 256) * sign[n][None]
                cols[n, side * 512 : side * 512 + 512, :] = full.reshape(512, 256).astype(BF)
            part = dot(scaled[sy], cols[n]).reshape(6, 256, 256)
            at = pl.ds(pl.multiple_of(n * 256, 256), 256)
            part = part if add is None else add[:, :, at] + part
            if last:
                out[...] = part
            else:
                out[:, :, at] = part

        if last:
            quarter(pl.program_id(0))
        else:
            pl.loop(0, 4, unroll=2)(quarter)

    operands = [mine, theirs, scaled, hot, sign] + ([] if total is None else [total])
    aliases = {} if total is None or last else {5: 0}
    return pl.pallas_call(
        kernel,
        grid=(4 if last else 1,),
        in_specs=[resident()] * len(operands),
        out_specs=pl.BlockSpec((6, 256, 256), lambda n: (0, 0, n)) if last else resident(),
        scratch_shapes=[pltpu.VMEM((4, 1024, 256), BF)],
        out_shape=(jax.ShapeDtypeStruct if last else pltpu.VMEM)((6, 256, 1024), F32),
        input_output_aliases=aliases,
        compiler_params=pltpu.CompilerParams(vmem_limit_bytes=20 << 20),
        cost_estimate=pl.CostEstimate(flops=46 * 10**8, transcendentals=0, bytes_accessed=10 * 2**20),
        name="response_product",
    )(*operands)


def shifted(value, axis, shift):
    size = lax.axis_size(axis)
    return lax.ppermute(value, axis, [(i, (i + shift) % size) for i in range(size)])


def around(value, axis):
    return [value] + [shifted(value, axis, s) for s in range(1, lax.axis_size(axis))]


def neighbours(value, axis):
    return shifted(value, axis, 1), shifted(value, axis, 3)


def opposite(behind, ahead, axis):
    half = behind.shape[0] // 2
    return shifted(ahead[:half], axis, 3), shifted(behind[half:], axis, 1)


def body(valence, conduction, eps_val, eps_cond, omega, gmap):
    pos = jnp.stack([lax.axis_index(a) for a in AXES]).astype(jnp.int32)
    bands = around(conduction.reshape(256, 128), "x")
    own = lax.all_to_all(jnp.broadcast_to(valence, (8, *valence.shape)), NARROW, 0, 0, tiled=True)
    own, bands = lax.optimization_barrier((own, bands))
    own = jnp.stack(around(own, "zh"))
    gap = jnp.broadcast_to((eps_cond[:, None] - eps_val)[:, None, :], (256, 2, 8)).reshape(4, 4, 2, 1, 128)
    own, gap = lax.optimization_barrier((own, gap))
    own = jnp.stack(around(own, "y"))
    other = shifted(own, "co", 1)

    rows, spectrum = row_pairs(pos, own, other, bands[0], gmap)
    rows = lax.all_to_all(rows, WIDE, 0, 0, tiled=True)
    cols = column_pairs(pos, spectrum, own, other, bands[1:])
    kept, got = cols[0], shifted(cols[1], "zl", 1)
    lower = lax.axis_index("zl") == 0
    cols = jnp.concatenate([jnp.where(lower, kept, got), jnp.where(lower, got, kept)])
    rows = jnp.stack(around(rows, "zl")).reshape(2, 4, 4, 2, 16, 256)
    rows, cols = lax.optimization_barrier((rows, cols))
    near_x = neighbours(rows, "x")
    near_zh = neighbours(cols, "zh")
    near_x, near_zh = lax.optimization_barrier((near_x, near_zh))
    far_x, far_zh = lax.optimization_barrier((opposite(*near_x, "x"), opposite(*near_zh, "zh")))
    rows = [rows, near_x[0], jnp.concatenate(far_x), near_x[1]]
    cols = jnp.stack([cols, near_zh[0], jnp.concatenate(far_zh), near_zh[1]])
    near_y = neighbours(cols, "y")
    scaled, hot, sign = prepare(pos, omega, rows, gap, gmap, jnp.asarray(tables()[-1]))
    hot, own_cols = lax.optimization_barrier((hot, cols))
    theirs = shifted(own_cols, "co", 1)
    scaled, hot, sign, near_y = lax.optimization_barrier((scaled, hot, sign, near_y))
    far = opposite(*near_y, "y")
    total = product_step(0, cols, theirs, scaled, hot, sign, None, False)
    total = product_step(1, near_y[0], shifted(near_y[0], "co", 1), scaled, hot, sign, total, False)
    total, far = lax.optimization_barrier((total, far))
    for sy, mine in ((3, near_y[1]), (2, jnp.concatenate(far))):
        theirs = shifted(mine, "co", 1)
        total = product_step(sy, mine, theirs, scaled, hot, sign, total, sy == 2)
    return total


def solution(mesh):
    torus = Mesh(mesh.devices.reshape(4, 4, 2, 2, 4), AXES)
    return jax.shard_map(
        body,
        mesh=torus,
        in_specs=(P(None, AXES), P(AXES, None), P(), P(), P(), P()),
        out_specs=P(None, WIDE, NARROW),
        check_vma=False,
    )
```

```python
import functools

import jax
import jax.numpy as jnp
import ml_dtypes
import numpy as np
from jax import lax
from jax.experimental import pallas as pl
from jax.experimental.pallas import tpu as pltpu
from jax.sharding import Mesh
from jax.sharding import PartitionSpec as P

GRID = 32
AXES = ("zh", "y", "co", "zl", "x")
WIDE = ("zh", "y", "co")
NARROW = ("zl", "x")
NPW = 8192
DISC = 256
NKX = 26
CAN = 640
BF = jnp.bfloat16
F32 = jnp.float32


def split_bf16(value):
    high = value.astype(BF)
    return high, (value - high.astype(value.dtype)).astype(BF)


def tables():
    k = np.arange(GRID)
    fold = np.where(k < GRID // 2, k, k - GRID)
    length = fold[:, None, None] ** 2 + fold[None, :, None] ** 2 + fold[None, None, :] ** 2
    ordered = np.sort(length.ravel())[:NPW]
    limit = ordered[-1]
    disc = []
    for ky in range(-15, 16):
        for kz in range(0, 16):
            if ky * ky + kz * kz <= limit and (kz > 0 or ky >= 0):
                disc.append((ky, kz))
    assert len(disc) <= DISC
    points = np.arange(GRID)
    wave = np.zeros((GRID, GRID, 2 * DISC))
    key = np.full((DISC, 1), -9000, np.int32)
    for m, (ky, kz) in enumerate(disc):
        angle = 2 * np.pi * ((ky * points[:, None] + kz * points[None, :]) % GRID) / GRID
        wave[:, :, m] = np.cos(angle)
        wave[:, :, DISC + m] = -np.sin(angle)
        key[m, 0] = ky * 64 + kz
    kx = np.arange(NKX) - 12
    assert limit < 13 * 13
    angle = 2 * np.pi * (kx[:, None] * points[None, :] % GRID) / GRID
    eye = np.eye(8)
    along = np.concatenate([np.kron(np.cos(angle), eye), np.kron(np.sin(angle), eye)])
    blocks = 8
    col_key = np.full((blocks, 1, CAN), -8000, np.int32)
    col_kx = np.zeros((blocks, 1, CAN), np.int32)
    col_id = np.full((blocks, 1, CAN), -(1 << 20), np.int32)
    size = NPW // blocks
    for j in range(blocks):
        low, high = ordered[j * size], ordered[(j + 1) * size - 1]
        n = 0
        for ky, kz in disc:
            for x in range(-12, 13):
                if (ky, kz) == (0, 0) and x < 0:
                    continue
                if low <= x * x + ky * ky + kz * kz <= high:
                    col_key[j, 0, n] = ky * 64 + kz
                    col_kx[j, 0, n] = x + 12
                    col_id[j, 0, n] = (x * 64 + ky) * 64 + kz
                    n += 1
        assert n <= CAN
    wave = wave.reshape(GRID * GRID, 2 * DISC).astype(np.float32)
    along = along.astype(np.float32)
    return split_np(wave) + split_np(along) + (key, col_key, col_kx, col_id)


def split_np(value):


    high = value.astype(ml_dtypes.bfloat16)
    low = (value - high.astype(np.float32)).astype(ml_dtypes.bfloat16)
    return high, low


def folded(index):
    def fold(k):
        return jnp.where(k < GRID // 2, k, k - GRID)

    return (
        fold(lax.shift_right_logical(index, 10)),
        fold(lax.shift_right_logical(index, 5) & 31),
        fold(index & 31),
    )


def dot(a, b):
    return jnp.dot(a, b, preferred_element_type=F32)


def fetch(sources, targets, sems):
    copies = [pltpu.make_async_copy(s, t, sems.at[i]) for i, (s, t) in enumerate(zip(sources, targets))]
    for copy in copies:
        copy.start()
    return copies


def picked(spectrum, count, key, wanted, kx, store):
    half = NKX * 8
    hot = jnp.where(key[...] == wanted, jnp.float32(1), jnp.float32(0)).astype(BF)
    found = dot(spectrum[: 2 * count * half, :], hot)
    masks = [jnp.broadcast_to(kx == i, (8, wanted.shape[1])) for i in range(NKX - 1)]
    for s in range(count):
        parts = []
        for part in range(2):
            base = (2 * s + part) * half
            value = found[base : base + 8]
            for i in range(1, NKX - 1):
                value = jnp.where(masks[i], found[base + i * 8 : base + i * 8 + 8], value)
            parts.append(value)
        store(s, *parts)


def waves(pos, own, other, bands, wave_hi, wave_lo, along_hi, along_lo, ready, a_hi, a_lo, spectrum, first):
    zh, y, co = pos[0], pos[1], pos[2]
    count = len(bands)

    def product(q, carry):
        szh = (zh - q // 4) & 3
        sy = (y - q % 4) & 3
        start = pl.multiple_of(q * 16, 16)
        rows_of = [band[pl.ds(start, 16), :] for band in bands]
        for n in range(8):
            mine = own[sy, szh, n]
            theirs = other[sy, szh, n]
            lower = jnp.where(co == 0, mine, theirs)
            upper = jnp.where(co == 0, theirs, mine)
            for s in range(count):
                pair = [lower * rows_of[s][n : n + 1, :], upper * rows_of[s][8 + n : 9 + n, :]]
                high, low = split_bf16(jnp.concatenate(pair, axis=0))
                at = pl.ds(pl.multiple_of(s * 256 + start, 16), 16)
                a_hi[at, n * 128 : (n + 1) * 128] = high
                a_lo[at, n * 128 : (n + 1) * 128] = low
        return carry

    lax.fori_loop(0, 16, product, 0)
    ready()
    field = dot(a_hi[...], wave_hi[...]) + (dot(a_lo[...], wave_hi[...]) + dot(a_hi[...], wave_lo[...]))
    half = NKX * 8
    norm = jnp.float32(1.0) / jnp.sqrt(jnp.float32(GRID**3))
    for s in range(count):
        f_hi, f_lo = split_bf16(field[s * 256 : s * 256 + 256])
        full = dot(along_hi[...], f_hi) + (dot(along_lo[...], f_hi) + dot(along_hi[...], f_lo))
        real = full[:half, :DISC] + full[half:, DISC:]
        imag = full[:half, DISC:] - full[half:, :DISC]
        at = 2 * (first + s) * half
        spectrum[at : at + half, :] = (real * norm).astype(BF)
        spectrum[at + half : at + 2 * half, :] = (imag * norm).astype(BF)


def row_kernel(pos, *refs):
    sources, rows, spectrum, targets = refs[:9], refs[9], refs[10], refs[11:20]
    a_hi, a_lo, sems = refs[20:]
    own, other, band, wave_hi, wave_lo, along_hi, along_lo, key, gmap = targets
    copies = fetch(sources, targets, sems)
    for copy in copies[:3]:
        copy.wait()

    def ready():
        for copy in copies[3:]:
            copy.wait()

    waves(pos, own, other, [band], wave_hi, wave_lo, along_hi, along_lo, ready, a_hi, a_lo, spectrum, 0)

    def row_blocks(r, carry):
        kx, ky, kz = folded(gmap[r])
        flip = jnp.where((kz < 0) | ((kz == 0) & (ky < 0)), -1, 1)
        sign = flip.astype(F32)

        def store(s, real, imag):
            both = jnp.concatenate([real, imag * sign], axis=0).astype(BF)
            for t in range(4):
                rows[4 * r + t] = both[:, t * 256 : (t + 1) * 256]

        picked(spectrum, 1, key, flip * (ky * 64 + kz), flip * kx + 12, store)
        return carry

    lax.fori_loop(0, 8, row_blocks, 0)


def column_kernel(pos, *refs):
    sources, cols, targets = refs[:13], refs[13], refs[14:27]
    spectrum, a_hi, a_lo, sems = refs[27:]
    first, own, other, band1, band2, band3, wave_hi, wave_lo, along_hi, along_lo, key, col_key, col_kx = targets
    zl, x = pos[3], pos[4]
    copies = fetch(sources, targets, sems)
    for copy in copies[:6]:
        copy.wait()

    def ready():
        for copy in copies[6:]:
            copy.wait()

    spectrum[: 2 * NKX * 8, :] = first[...]
    bands = [band1, band2, band3]
    waves(pos, own, other, bands, wave_hi, wave_lo, along_hi, along_lo, ready, a_hi, a_lo, spectrum, 1)

    def columns(part, carry):
        j = (zl ^ part) * 4 + x

        def store(s, real, imag):
            cols[part, (x - s) & 3] = jnp.concatenate([real, imag], axis=0).astype(BF)

        picked(spectrum, 4, key, col_key[j], col_kx[j], store)
        return carry

    lax.fori_loop(0, 2, columns, 0)


def whole(shape):
    return pl.BlockSpec(shape, lambda *_: (0,) * len(shape), pipeline_mode=pl.Buffered(1))


def resident():
    return pl.BlockSpec(memory_space=pltpu.VMEM)


def transform_call(kernel, pos, operands, outs, scratch, flops, name):
    return pl.pallas_call(
        kernel,
        grid_spec=pltpu.PrefetchScalarGridSpec(
            num_scalar_prefetch=1,
            grid=(1,),
            in_specs=[pl.BlockSpec(memory_space=pl.ANY)] * len(operands),
            out_specs=[whole(v.shape) for v in outs],
            scratch_shapes=[pltpu.VMEM(v.shape, v.dtype) for v in operands]
            + scratch
            + [pltpu.SemaphoreType.DMA((len(operands),))],
        ),
        out_shape=outs,
        compiler_params=pltpu.CompilerParams(vmem_limit_bytes=60 << 20),
        cost_estimate=pl.CostEstimate(flops=flops, transcendentals=0, bytes_accessed=6 * 2**20),
        name=name,
    )(pos, *operands)


def row_pairs(pos, own, other, band, gmap):
    consts = [jnp.asarray(t) for t in tables()[:5]]
    outs = [jax.ShapeDtypeStruct((32, 16, 256), BF), jax.ShapeDtypeStruct((2 * NKX * 8, DISC), BF)]
    scratch = [pltpu.VMEM((256, 1024), BF)] * 2
    operands = [own, other, band, *consts, gmap.reshape(8, 1, 1024)]
    return transform_call(row_kernel, pos, operands, outs, scratch, 4 * 10**9, "row_pairs")


def column_pairs(pos, first, own, other, bands):
    consts = [jnp.asarray(t) for t in tables()[:7]]
    outs = [jax.ShapeDtypeStruct((2, 4, 16, CAN), BF)]
    scratch = [pltpu.VMEM((8 * NKX * 8, DISC), BF)] + [pltpu.VMEM((768, 1024), BF)] * 2
    operands = [first, own, other, *bands, *consts]
    return transform_call(column_kernel, pos, operands, outs, scratch, 8 * 10**9, "column_pairs")[0]


def prepare_kernel(pos, omega, r0, r1, r2, r3, gap, gmap, ident, scaled, hot, sign, row_k):
    zh, co, zl, x = pos[0], pos[2], pos[3], pos[4]

    @pl.when(pl.program_id(0) == 0)
    def _():
        kx, ky, kz = folded(gmap[0])
        flip = jnp.where((kz < 0) | ((kz == 0) & ((ky < 0) | ((ky == 0) & (kx < 0)))), -1, 1)
        wanted = (flip * ((kx * 64 + ky) * 64 + kz)).astype(F32)
        names = jnp.broadcast_to(ident[0].astype(F32), (128, CAN)).T
        signs = jnp.concatenate([jnp.ones((8, 1024), F32), jnp.broadcast_to(flip.astype(F32), (8, 1024))], axis=0)
        for t in range(8):
            at = slice(t * 128, (t + 1) * 128)
            here = slice(t % 2 * 128, t % 2 * 128 + 128)
            hot[t // 2, :, here] = jnp.where(names == wanted[:, at], jnp.float32(1), jnp.float32(0)).astype(BF)
            sign[t // 2, :, here] = signs[:, at]

    for side in range(2):
        co_at = co if side == 0 else 1 - co
        energies = []
        for s in range(4):
            zh_at = (zh - s) & 3
            energies.append(gap[zh_at, 0, co_at])
            for sx, ref in enumerate((r0, r1, r2, r3)):
                for szl in range(2):
                    n = (zl ^ szl) * 4 + ((x - sx) & 3)
                    to = pl.multiple_of(side * 512 + s * 128 + n * 16, 16)
                    row_k[pl.ds(to, 16), :] = ref[szl, zh_at, 0, co_at]
        energy = jnp.concatenate(energies, axis=1)
        total = row_k[side * 512 : side * 512 + 512, :].astype(F32).T
        for w in range(6):
            weight = -2.0 * energy / (energy * energy + omega[w] * omega[w])
            weight = weight / jnp.sqrt(jnp.float32(2048))
            at = slice(side * 512, side * 512 + 512)
            scaled[pl.program_id(0), w * 256 : (w + 1) * 256, at] = (total * weight).astype(BF)


def prepare(pos, omega, rows, gap, gmap, ident):
    rows = [pltpu.with_memory_space_constraint(r, pltpu.HBM) for r in rows]
    gmap, ident = (pltpu.with_memory_space_constraint(v, pltpu.HBM) for v in (gmap.reshape(8, 1, 1024), ident))
    row_spec = pl.BlockSpec((2, 4, 1, 2, 16, 256), lambda s, pos, om: (0, 0, (pos[1] - s) & 3, 0, 0, 0))
    return pl.pallas_call(
        prepare_kernel,
        grid_spec=pltpu.PrefetchScalarGridSpec(
            num_scalar_prefetch=2,
            grid=(4,),
            in_specs=[row_spec] * 4
            + [
                pl.BlockSpec((4, 1, 2, 1, 128), lambda s, pos, om: (0, (pos[1] - s) & 3, 0, 0, 0)),
                pl.BlockSpec((1, 1, 1024), lambda s, pos, om: (pos[3] * 4 + pos[4], 0, 0)),
                pl.BlockSpec((1, 1, CAN), lambda s, pos, om: (pos[3] * 4 + pos[4], 0, 0)),
            ],
            out_specs=[resident(), resident(), resident()],
            scratch_shapes=[pltpu.VMEM((1024, 256), BF)],
        ),
        out_shape=[pltpu.VMEM((4, 1536, 1024), BF), pltpu.VMEM((4, CAN, 256), BF), pltpu.VMEM((4, 16, 256), F32)],
        compiler_params=pltpu.CompilerParams(vmem_limit_bytes=20 << 20),
        cost_estimate=pl.CostEstimate(flops=10**9, transcendentals=0, bytes_accessed=20 * 2**20),
        name="scaled_rows",
    )(pos, omega, *rows, gap, gmap, ident)


def product_step(sy, mine, theirs, scaled, hot, sign, total, last, which=None):
    def kernel(mine, theirs, scaled, hot, sign, *refs):
        out, cols = refs[-2:]
        add = None if total is None else refs[0]

        def quarter(n):
            for side, ref in enumerate((mine, theirs)):
                block = ref[which] if side == 1 and which is not None else ref[...]
                full = dot(block.reshape(512, CAN), hot[n]).reshape(32, 16, 256) * sign[n][None]
                cols[n, side * 512 : side * 512 + 512, :] = full.reshape(512, 256).astype(BF)
            part = dot(scaled[sy], cols[n]).reshape(6, 256, 256)
            at = pl.ds(pl.multiple_of(n * 256, 256), 256)
            part = part if add is None else add[:, :, at] + part
            if last:
                out[...] = part
            else:
                out[:, :, at] = part

        if last:
            quarter(pl.program_id(0))
        else:
            pl.loop(0, 4, unroll=2)(quarter)

    operands = [mine, theirs, scaled, hot, sign] + ([] if total is None else [total])
    aliases = {} if total is None or last else {5: 0}
    return pl.pallas_call(
        kernel,
        grid=(4 if last else 1,),
        in_specs=[resident()] * len(operands),
        out_specs=pl.BlockSpec((6, 256, 256), lambda n: (0, 0, n)) if last else resident(),
        scratch_shapes=[pltpu.VMEM((4, 1024, 256), BF)],
        out_shape=(jax.ShapeDtypeStruct if last else pltpu.VMEM)((6, 256, 1024), F32),
        input_output_aliases=aliases,
        compiler_params=pltpu.CompilerParams(vmem_limit_bytes=20 << 20),
        cost_estimate=pl.CostEstimate(flops=46 * 10**8, transcendentals=0, bytes_accessed=10 * 2**20),
        name="response_product",
    )(*operands)


def shifted(value, axis, shift):
    size = lax.axis_size(axis)
    return lax.ppermute(value, axis, [(i, (i + shift) % size) for i in range(size)])


def around(value, axis):
    return [value] + [shifted(value, axis, s) for s in range(1, lax.axis_size(axis))]


def neighbours(value, axis):
    return shifted(value, axis, 1), shifted(value, axis, 3)


def opposite(behind, ahead, axis):
    half = behind.shape[0] // 2
    return shifted(ahead[:half], axis, 3), shifted(behind[half:], axis, 1)


def body(valence, conduction, eps_val, eps_cond, omega, gmap):
    pos = jnp.stack([lax.axis_index(a) for a in AXES]).astype(jnp.int32)
    bands = around(conduction.reshape(256, 128), "x")
    own = lax.all_to_all(jnp.broadcast_to(valence, (8, *valence.shape)), NARROW, 0, 0, tiled=True)
    own, bands = lax.optimization_barrier((own, bands))
    own = jnp.stack(around(own, "zh"))
    gap = jnp.broadcast_to((eps_cond[:, None] - eps_val)[:, None, :], (256, 2, 8)).reshape(4, 4, 2, 1, 128)
    own, gap = lax.optimization_barrier((own, gap))
    own = jnp.stack(around(own, "y"))
    other = shifted(own, "co", 1)

    rows, spectrum = row_pairs(pos, own, other, bands[0], gmap)
    rows = lax.all_to_all(rows, WIDE, 0, 0, tiled=True)
    cols = column_pairs(pos, spectrum, own, other, bands[1:])
    kept, got = cols[0], shifted(cols[1], "zl", 1)
    lower = lax.axis_index("zl") == 0
    cols = jnp.concatenate([jnp.where(lower, kept, got), jnp.where(lower, got, kept)])
    rows = jnp.stack(around(rows, "zl")).reshape(2, 4, 4, 2, 16, 256)
    rows, cols = lax.optimization_barrier((rows, cols))
    near_x = neighbours(rows, "x")
    near_zh = neighbours(cols, "zh")
    near_x, near_zh = lax.optimization_barrier((near_x, near_zh))
    far_x, far_zh = lax.optimization_barrier((opposite(*near_x, "x"), opposite(*near_zh, "zh")))
    rows = [rows, near_x[0], jnp.concatenate(far_x), near_x[1]]
    cols = jnp.stack([cols, near_zh[0], jnp.concatenate(far_zh), near_zh[1]])
    near_y = neighbours(cols, "y")
    scaled, hot, sign = prepare(pos, omega, rows, gap, gmap, jnp.asarray(tables()[-1]))
    scaled, hot, sign, near_y = lax.optimization_barrier((scaled, hot, sign, near_y))
    far = opposite(*near_y, "y")
    total = product_step(0, cols, shifted(cols, "co", 1), scaled, hot, sign, None, False)
    both = shifted(jnp.stack(near_y), "co", 1)
    total = product_step(1, near_y[0], both, scaled, hot, sign, total, False, 0)
    total, far = lax.optimization_barrier((total, far))
    total = product_step(3, near_y[1], both, scaled, hot, sign, total, False, 1)
    far = jnp.concatenate(far)
    return product_step(2, far, shifted(far, "co", 1), scaled, hot, sign, total, True)


def solution(mesh):
    torus = Mesh(mesh.devices.reshape(4, 4, 2, 2, 4), AXES)
    return jax.shard_map(
        body,
        mesh=torus,
        in_specs=(P(None, AXES), P(AXES, None), P(), P(), P(), P()),
        out_specs=P(None, WIDE, NARROW),
        check_vma=False,
    )
```
